32 devices in a mesh: dp: 8 (over y, x, core), tensor: 4 (over z).
Axes of the slice: x: 2, y: 2, z: 4, core: 2. Of those that a mesh axis runs over, the one named last changes fastest.
Arguments:
- patches: float32 [64, 256, 16], P('dp'), may hold values from -5 to 5
- noise_draw: float32 [64, 256, 16], P('dp'), may hold values from -5 to 5
- timesteps: int32 [64], P('dp'), may hold values from 0 to 999
- labels: int32 [64], P('dp'), may hold values from 0 to 999
- w_attn: float32 [2, 4, 768, 768], P(None, None, 'dp', 'tensor'), may hold values from -0.3125 to 0.3125
- w_mlp: float32 [2, 2, 768, 3072], P(None, None, 'dp', 'tensor'), may hold values from -0.21875 to 0.21875
- w_mod: float32 [2, 768, 4608], P(None, 'dp', 'tensor'), may hold values from -0.21875 to 0.21875
- w_embed: float32 [3592, 768], P(None, 'dp'), as said below
- biases: float32 [33, 768], replicated, may hold values from -0.4375 to 0.4375
- momentum_attn: float32 [2, 4, 768, 768], P(None, None, 'dp', 'tensor'), may hold values from -0.15625 to 0.15625
- momentum_mlp: float32 [2, 2, 768, 3072], P(None, None, 'dp', 'tensor'), may hold values from -0.15625 to 0.15625
- momentum_mod: float32 [2, 768, 4608], P(None, 'dp', 'tensor'), may hold values from -0.15625 to 0.15625
- momentum_embed: float32 [3592, 768], P(None, 'dp'), may hold values from -0.15625 to 0.15625
- momentum_bias: float32 [33, 768], replicated, may hold values from -0.15625 to 0.15625
- first_attn: float32 [2, 4, 3072, 768], P(None, None, 'dp', 'tensor'), as said below
- second_attn: float32 [2, 4, 3072, 768], P(None, None, 'dp', 'tensor'), as said below
- first_mlp: float32 [2, 2, 3072, 3072], P(None, None, 'dp', 'tensor'), as said below
- second_mlp: float32 [2, 2, 3072, 3072], P(None, None, 'dp', 'tensor'), as said below
- first_mod: float32 [2, 3072, 4608], P(None, 'dp', 'tensor'), as said below
- second_mod: float32 [2, 3072, 4608], P(None, 'dp', 'tensor'), as said below
- first_embed: float32 [3592, 3072], P(None, 'dp'), as said below
- second_embed: float32 [3592, 3072], P(None, 'dp'), as said below
- first_bias: float32 [4, 33, 768], replicated, as said below
- second_bias: float32 [4, 33, 768], replicated, as said below
Outputs:
- loss: float32 [], replicated
- group_norms: float32 [4], replicated
- bias_grads: float32 [4, 33, 768], replicated
- new_attn: float32 [2, 4, 768, 768], P(None, None, 'dp', 'tensor')
- new_mlp: float32 [2, 2, 768, 3072], P(None, None, 'dp', 'tensor')
- new_mod: float32 [2, 768, 4608], P(None, 'dp', 'tensor')
- new_embed: float32 [3592, 768], P(None, 'dp')
- new_bias: float32 [33, 768], replicated
- new_momentum_attn: float32 [2, 4, 768, 768], P(None, None, 'dp', 'tensor')
- new_momentum_mlp: float32 [2, 2, 768, 3072], P(None, None, 'dp', 'tensor')
- new_momentum_mod: float32 [2, 768, 4608], P(None, 'dp', 'tensor')
- new_momentum_embed: float32 [3592, 768], P(None, 'dp')
- new_momentum_bias: float32 [33, 768], replicated
- new_first_attn: float32 [2, 4, 3072, 768], P(None, None, 'dp', 'tensor')
- new_second_attn: float32 [2, 4, 3072, 768], P(None, None, 'dp', 'tensor')
- new_first_mlp: float32 [2, 2, 3072, 3072], P(None, None, 'dp', 'tensor')
- new_second_mlp: float32 [2, 2, 3072, 3072], P(None, None, 'dp', 'tensor')
- new_first_mod: float32 [2, 3072, 4608], P(None, 'dp', 'tensor')
- new_second_mod: float32 [2, 3072, 4608], P(None, 'dp', 'tensor')
- new_first_embed: float32 [3592, 3072], P(None, 'dp')
- new_second_embed: float32 [3592, 3072], P(None, 'dp')
- new_first_bias: float32 [4, 33, 768], replicated
- new_second_bias: float32 [4, 33, 768], replicated
The draws below stay inside these ranges and needn't reach their ends.
Inputs may be any that keep to these rules, and one draw needn't show every extreme that they name: `w_embed`: rows scaled by block: class table 0.05, first timestep map 256^-0.5, patch map 16^-0.5, the rest 768^-0.5, truncated at 4 scales. `first_attn`: spread 0.11 g with g = 0.02 / sqrt(24017664), both signs. `second_attn`: between 1 and 4 times 0.0526 g^2, even in the logarithm. `first_mlp`: as first_attn. `second_mlp`: as second_attn. `first_mod`: as first_attn with 3 g in place of g. `second_mod`: as second_attn with 3 g in place of g. `first_embed`: as first_attn with 2 g in place of g. `second_embed`: as second_attn with 2 g in place of g. `first_bias`: as first_attn with 4 g in place of g. `second_bias`: as second_attn with 4 g in place of g.
All inputs are finite; a program needn't handle non-finite values.
Results may differ from the reference program's by a relative error of at most 0.019.
Values may be sent and summed in bfloat16 or wider, within the bound.
A program may use at most 384 MiB of HBM per device.

```python
import math
import jax
import jax.numpy as jnp
from jax import lax

D = 768
HD = 64
FF = 3072
NCLS = 1000
FREQ = 256
PATCH_IN = 16
SIDE = 16
L = 2
LAT_DEV = 8
GROUPS = 4
STEP_COUNT = 10
NSTEPS = 1000
S = 256
LB = 14
NB = 33
RE = 3592
LATENTS = 64
NPARAM = 24017664
N_DP = 8
N_TENSOR = 4


def gradient_size(factor):
    return factor * 0.02 / math.sqrt(NPARAM)


def first_draw(key, shape_out, factor):
    return 0.1 / 0.9 * gradient_size(factor) * jax.random.truncated_normal(key, -4.0, 4.0, shape_out, jnp.float32)


def second_draw(key, shape_out, factor):
    spread = jax.random.uniform(key, shape_out, jnp.float32, 0.0, math.log(4.0))
    return 0.05 / 0.95 * gradient_size(factor) ** 2 * jnp.exp(spread)


def draw_w_embed(key, part):
    scales = jnp.concatenate([jnp.full((NCLS,), 0.05, jnp.float32), jnp.full((FREQ,), FREQ ** (-0.5), jnp.float32), jnp.full((D,), D ** (-0.5), jnp.float32), jnp.full((PATCH_IN,), PATCH_IN ** (-0.5), jnp.float32), jnp.full((2 * D,), D ** (-0.5), jnp.float32), jnp.full((PATCH_IN,), D ** (-0.5), jnp.float32)])
    return scales[:, None] * jax.random.truncated_normal(key, -4.0, 4.0, (RE, D), jnp.float32)


def draw_first_attn(key, part):
    return first_draw(key, (L, 4, GROUPS * D, D), 1.0)


def draw_second_attn(key, part):
    return second_draw(key, (L, 4, GROUPS * D, D), 1.0)


def draw_first_mlp(key, part):
    return first_draw(key, (L, 2, GROUPS * D, FF), 1.0)


def draw_second_mlp(key, part):
    return second_draw(key, (L, 2, GROUPS * D, FF), 1.0)


def draw_first_mod(key, part):
    return first_draw(key, (L, GROUPS * D, 6 * D), 3.0)


def draw_second_mod(key, part):
    return second_draw(key, (L, GROUPS * D, 6 * D), 3.0)


def draw_first_embed(key, part):
    return first_draw(key, (RE, GROUPS * D), 2.0)


def draw_second_embed(key, part):
    return second_draw(key, (RE, GROUPS * D), 2.0)


def draw_first_bias(key, part):
    return first_draw(key, (GROUPS, NB, D), 4.0)


def draw_second_bias(key, part):
    return second_draw(key, (GROUPS, NB, D), 4.0)


def place_ends(entries, key, smallest, largest):
    place = [jax.random.randint(jax.random.fold_in(key, axis), (), 0, length) for axis, length in enumerate(entries.shape)]
    longest = entries.shape.index(max(entries.shape))
    next_to = place[:longest] + [(place[longest] + 1) % entries.shape[longest]] + place[longest + 1:]
    return entries.at[tuple(place)].set(smallest).at[tuple(next_to)].set(largest)


def shard_levels(rng, extent, cuts, low, high):
    gain, own = 1.0, jax.random.fold_in(rng, 6)
    for dim, shards_of in cuts:
        steps = jnp.exp(jax.random.uniform(jax.random.fold_in(own, dim), (shards_of,), jnp.float32, low / len(cuts), high / len(cuts)))
        gain = gain * jnp.repeat(steps, extent[dim] // shards_of).reshape([-1 if axis == dim else 1 for axis in range(len(extent))])
    return gain


def bell_draw(rng, shape, scale, bound, pieces=(), kind=jnp.bfloat16):
    drawn = scale * jax.random.normal(rng, shape, jnp.float32)
    if pieces:
        drawn = drawn * shard_levels(rng, shape, pieces, -0.22, 0.18)
    return jnp.clip(drawn, -bound, bound).astype(kind)


def setup_inputs(seed: int = 0) -> dict:
    arg_keys = jax.random.split(jax.random.key(seed), 25)
    patches = bell_draw(arg_keys[0], (LATENTS, S, PATCH_IN), 1.0, 5.0, ((0, 8),), jnp.float32)
    noise_draw = bell_draw(arg_keys[1], (LATENTS, S, PATCH_IN), 1.0, 5.0, ((0, 8),), jnp.float32)
    timesteps = place_ends(jax.random.randint(arg_keys[2], (LATENTS,), 0, NSTEPS), jax.random.fold_in(arg_keys[2], 1), 0, NSTEPS - 1).astype(jnp.int32)
    labels = place_ends(jax.random.randint(arg_keys[3], (LATENTS,), 0, NCLS), jax.random.fold_in(arg_keys[3], 1), 0, NCLS - 1).astype(jnp.int32)
    w_attn = bell_draw(arg_keys[4], (L, 4, D, D), (D // 2) ** -0.5, 0.3125, ((2, 8), (3, 4)), jnp.float32)
    w_mlp = bell_draw(arg_keys[5], (L, 2, D, FF), D ** -0.5, 0.21875, ((2, 8), (3, 4)), jnp.float32)
    w_mod = bell_draw(arg_keys[6], (L, D, 6 * D), D ** -0.5, 0.21875, ((1, 8), (2, 4)), jnp.float32)
    w_embed = draw_w_embed(jax.random.fold_in(arg_keys[24], 71), 0)
    biases = bell_draw(arg_keys[8], (NB, D), 0.03, 0.4375, (), jnp.float32)
    momentum_attn = bell_draw(arg_keys[9], (L, 4, D, D), 0.01, 0.15625, ((2, 8), (3, 4)), jnp.float32)
    momentum_mlp = bell_draw(arg_keys[10], (L, 2, D, FF), 0.01, 0.15625, ((2, 8), (3, 4)), jnp.float32)
    momentum_mod = bell_draw(arg_keys[11], (L, D, 6 * D), 0.01, 0.15625, ((1, 8), (2, 4)), jnp.float32)
    momentum_embed = bell_draw(arg_keys[12], (RE, D), 0.01, 0.15625, ((1, 8),), jnp.float32)
    momentum_bias = bell_draw(arg_keys[13], (NB, D), 0.01, 0.15625, (), jnp.float32)
    first_attn = draw_first_attn(jax.random.fold_in(arg_keys[24], 71), 0)
    second_attn = draw_second_attn(jax.random.fold_in(arg_keys[24], 71), 0)
    first_mlp = draw_first_mlp(jax.random.fold_in(arg_keys[24], 71), 0)
    second_mlp = draw_second_mlp(jax.random.fold_in(arg_keys[24], 71), 0)
    first_mod = draw_first_mod(jax.random.fold_in(arg_keys[24], 71), 0)
    second_mod = draw_second_mod(jax.random.fold_in(arg_keys[24], 71), 0)
    first_embed = draw_first_embed(jax.random.fold_in(arg_keys[24], 71), 0)
    second_embed = draw_second_embed(jax.random.fold_in(arg_keys[24], 71), 0)
    first_bias = draw_first_bias(jax.random.fold_in(arg_keys[24], 71), 0)
    second_bias = draw_second_bias(jax.random.fold_in(arg_keys[24], 71), 0)
    return dict(patches=patches, noise_draw=noise_draw, timesteps=timesteps, labels=labels, w_attn=w_attn, w_mlp=w_mlp, w_mod=w_mod, w_embed=w_embed, biases=biases, momentum_attn=momentum_attn, momentum_mlp=momentum_mlp, momentum_mod=momentum_mod, momentum_embed=momentum_embed, momentum_bias=momentum_bias, first_attn=first_attn, second_attn=second_attn, first_mlp=first_mlp, second_mlp=second_mlp, first_mod=first_mod, second_mod=second_mod, first_embed=first_embed, second_embed=second_embed, first_bias=first_bias, second_bias=second_bias)


@jax.custom_vjp
def low(v):
    return lax.optimization_barrier(v.astype(jnp.bfloat16)).astype(jnp.float32)

@jax.custom_vjp
def low_back(v):
    return v

def low_keep(v):
    return (low(v), None)

def low_pass(kept, grad):
    return (grad,)

def back_keep(v):
    return (v, None)

def back_low(kept, grad):
    return (low(grad),)
low.defvjp(low_keep, low_pass)
low_back.defvjp(back_keep, back_low)
HIGHEST = lax.Precision.HIGHEST
LEARN_RATE = 0.03
WEIGHT_DECAY = 0.1
BETA_FIRST = 0.9
BETA_SECOND = 0.95
ADAM_EPSILON = 1e-08
CLIP_NORM = 0.02
OUTER_RATE = 0.7
OUTER_MOMENTUM = 0.9

def matmul(left, right):
    return jnp.dot(left, right, precision=HIGHEST)

def normalize(values):
    centred = values - lax.optimization_barrier(jnp.mean(values, -1, keepdims=True))
    return centred * lax.rsqrt(lax.optimization_barrier(jnp.mean(centred * centred, -1, keepdims=True)) + 1e-06)

def positions():
    quarter = D // 4
    omegas = 1.0 / 10000.0 ** (jnp.arange(quarter, dtype=jnp.float32) / quarter)
    places = jnp.arange(S, dtype=jnp.int32)
    across = (places % SIDE).astype(jnp.float32)[:, None] * omegas[None, :]
    downward = (places // SIDE).astype(jnp.float32)[:, None] * omegas[None, :]
    return jnp.concatenate([jnp.sin(across), jnp.cos(across), jnp.sin(downward), jnp.cos(downward)], axis=1)

def frequencies(stamps):
    half_width = FREQ // 2
    freq_rates = jnp.exp(-jnp.log(10000.0) * jnp.arange(half_width, dtype=jnp.float32) / half_width)
    angles = stamps.astype(jnp.float32)[:, None] * freq_rates[None, :]
    return jnp.concatenate([jnp.cos(angles), jnp.sin(angles)], axis=1)

def signal_levels(stamps):
    noise_rates = jnp.linspace(0.0001, 0.02, NSTEPS, dtype=jnp.float32)
    kept_share = jnp.cumprod(1.0 - noise_rates)
    matches = stamps[:, None] == jnp.arange(NSTEPS, dtype=jnp.int32)[None, :]
    return lax.optimization_barrier(jnp.sum(jnp.where(matches, kept_share[None, :], 0.0), axis=1))

def embed_parts(matrix):
    bounds = [NCLS, NCLS + FREQ, NCLS + FREQ + D, NCLS + FREQ + D + PATCH_IN, NCLS + FREQ + 3 * D + PATCH_IN]
    return (matrix[:bounds[0]], matrix[bounds[0]:bounds[1]], matrix[bounds[1]:bounds[2]], matrix[bounds[2]:bounds[3]], matrix[bounds[3]:bounds[4]], matrix[bounds[4]:])

def attend(queries, key_rows, values):
    batch_size, length, total_width = queries.shape
    heads_here = total_width // HD
    query_heads = queries.reshape(batch_size, length, heads_here, HD)
    key_heads = key_rows.reshape(batch_size, length, heads_here, HD)
    value_heads = values.reshape(batch_size, length, heads_here, HD)
    scores = low_back(jnp.einsum('nqhd,nkhd->nhqk', query_heads, key_heads, precision=HIGHEST) * HD ** (-0.5))
    weights = low(jax.nn.softmax(scores, axis=-1))
    output = jnp.einsum('nhqk,nkhd->nqhd', weights, value_heads, precision=HIGHEST)
    return output.reshape(batch_size, length, total_width)

def forward(params, patches, noise_draw, timesteps, labels):
    w_attn, w_mlp, w_mod, w_embed, biases = params
    attn_low, mlp_low, mod_low, embed_low = (low(w_attn), low(w_mlp), low(w_mod), low(w_embed))
    class_table, first_time, second_time, patch_map, final_map, head_map = embed_parts(embed_low)
    bias_flat = biases.reshape(-1)
    bias_tail = bias_flat[L * LB * D:]
    signal = signal_levels(timesteps)[:, None, None]
    noised = low(jnp.sqrt(signal) * patches + jnp.sqrt(1.0 - signal) * noise_draw)
    stream = low_back(matmul(noised, patch_map)) + bias_tail[:D] + positions()
    hidden_time = low_back(matmul(low(frequencies(timesteps)), first_time) + bias_tail[D:2 * D])
    condition = low_back(matmul(low(jax.nn.silu(hidden_time)), second_time) + bias_tail[2 * D:3 * D] + class_table[labels])
    cond_act = low(jax.nn.silu(condition))
    shards = N_TENSOR
    col_width = D // shards
    unit_width = FF // shards
    mod_width = 6 * D // shards
    copies = [low_back(cond_act) for shard_at in range(shards)]
    for layer_at in range(L):
        bias_layer = bias_flat[layer_at * LB * D:(layer_at + 1) * LB * D]
        ada_bias = bias_layer[4 * D + FF:]
        modulation = low_back(jnp.concatenate([matmul(copies[shard_at], mod_low[layer_at][:, shard_at * mod_width:(shard_at + 1) * mod_width]) + ada_bias[shard_at * mod_width:(shard_at + 1) * mod_width] for shard_at in range(shards)], axis=1))
        mod_parts = [modulation[:, None, part_at * D:(part_at + 1) * D] for part_at in range(6)]
        hidden = low(normalize(stream) * (1.0 + mod_parts[1]) + mod_parts[0])
        branch = 0.0
        for shard_at in range(shards):
            col_start = shard_at * col_width
            col_end = col_start + col_width
            shared = low_back(hidden)
            queries = low_back(low(matmul(shared, attn_low[layer_at, 0][:, col_start:col_end]) + bias_layer[col_start:col_end]))
            key_rows = low_back(low(matmul(shared, attn_low[layer_at, 1][:, col_start:col_end])))
            values = low_back(low(matmul(shared, attn_low[layer_at, 2][:, col_start:col_end]) + bias_layer[D + col_start:D + col_end]))
            attended = low_back(low(attend(queries, key_rows, values)))
            branch = branch + low(matmul(attended, attn_low[layer_at, 3][:, col_start:col_end].T))
        stream = stream + mod_parts[2] * (low_back(branch) + bias_layer[2 * D:3 * D])
        hidden = low(normalize(stream) * (1.0 + mod_parts[4]) + mod_parts[3])
        branch = 0.0
        for shard_at in range(shards):
            col_start = shard_at * unit_width
            col_end = col_start + unit_width
            shared = low_back(hidden)
            before = low_back(matmul(shared, mlp_low[layer_at, 0][:, col_start:col_end]) + bias_layer[3 * D + col_start:3 * D + col_end])
            activated = low(jax.nn.gelu(before, approximate=True))
            branch = branch + low(matmul(activated, mlp_low[layer_at, 1][:, col_start:col_end].T))
        stream = stream + mod_parts[5] * (low_back(branch) + bias_layer[3 * D + FF:4 * D + FF])
    final_mod = low_back(matmul(cond_act, final_map.T) + bias_tail[3 * D:5 * D])
    hidden = low(normalize(stream) * (1.0 + final_mod[:, None, D:]) + final_mod[:, None, :D])
    predicted = low_back(matmul(hidden, head_map.T))
    errors = predicted - noise_draw
    return jnp.sum(errors * errors) / (N_DP // GROUPS * LAT_DEV * S * PATCH_IN)

def group_grads(params, inputs):

    def visit_block(carried, block_in):

        def loss_of(weights_now):
            return forward(weights_now, block_in[0], block_in[1], block_in[2], block_in[3])
        loss_now, pull_back = jax.vjp(loss_of, params)
        gradients = pull_back(jnp.ones_like(loss_now))[0]
        return ((carried[0] + loss_now, jax.tree.map(jnp.add, carried[1], gradients)), None)
    initial = (jnp.zeros((), jnp.float32), jax.tree.map(jnp.zeros_like, params))
    result, ignored = lax.scan(visit_block, initial, inputs)
    return result

def adam_update(gradient, first_old, second_old):
    first_new = BETA_FIRST * first_old + (1.0 - BETA_FIRST) * gradient
    second_new = BETA_SECOND * second_old + (1.0 - BETA_SECOND) * gradient * gradient
    update = first_new / (1.0 - BETA_FIRST ** STEP_COUNT) / (jnp.sqrt(second_new / (1.0 - BETA_SECOND ** STEP_COUNT)) + ADAM_EPSILON)
    return (update, first_new, second_new)

def reference(patches, noise_draw, timesteps, labels, w_attn, w_mlp, w_mod, w_embed, biases, momentum_attn, momentum_mlp, momentum_mod, momentum_embed, momentum_bias, first_attn, second_attn, first_mlp, second_mlp, first_mod, second_mod, first_embed, second_embed, first_bias, second_bias):
    stretches = N_DP // GROUPS
    params = (w_attn, w_mlp, w_mod, w_embed, biases)
    axes_at = (2, 2, 1, 1)
    firsts = (first_attn, first_mlp, first_mod, first_embed, first_bias)
    seconds = (second_attn, second_mlp, second_mod, second_embed, second_bias)
    momenta = (momentum_attn, momentum_mlp, momentum_mod, momentum_embed, momentum_bias)

    def own_rows(moment, axis_at, group_at):
        shape_in = moment.shape
        rows_all = shape_in[axis_at] // GROUPS
        shaped = moment.reshape(shape_in[:axis_at] + (stretches, GROUPS, rows_all // stretches) + shape_in[axis_at + 1:])
        picked = jnp.take(shaped, group_at, axis=axis_at + 1)
        return picked.reshape(shape_in[:axis_at] + (rows_all,) + shape_in[axis_at + 1:])

    def put_rows(pieces_in, axis_at):
        shape_in = pieces_in[0].shape
        parted = [piece_in.reshape(shape_in[:axis_at] + (stretches, shape_in[axis_at] // stretches) + shape_in[axis_at + 1:]) for piece_in in pieces_in]
        joined = jnp.stack(parted, axis=axis_at + 1)
        return joined.reshape(shape_in[:axis_at] + (GROUPS * shape_in[axis_at],) + shape_in[axis_at + 1:])
    losses, norm_list, local_weights, first_lists, second_lists, clipped_biases = ([], [], [], [], [], [])
    for group_at in range(GROUPS):
        picked_inputs = tuple((array_in.reshape((stretches, GROUPS, LAT_DEV) + array_in.shape[1:])[:, group_at] for array_in in (patches, noise_draw, timesteps, labels)))
        loss_now, grads_now = group_grads(params, picked_inputs)
        norm_now = jnp.sqrt(sum((jnp.sum(gradient_in * gradient_in) for gradient_in in grads_now)))
        scale_now = CLIP_NORM / (norm_now + 1e-06)
        weights_now, firsts_now, seconds_now = ([], [], [])
        for index_at in range(5):
            if index_at < 4:
                first_old = own_rows(firsts[index_at], axes_at[index_at], group_at)
                second_old = own_rows(seconds[index_at], axes_at[index_at], group_at)
            else:
                first_old = firsts[index_at][group_at]
                second_old = seconds[index_at][group_at]
            update, first_new, second_new = adam_update(grads_now[index_at] * scale_now, first_old, second_old)
            weights_now.append(params[index_at] - LEARN_RATE * (update + WEIGHT_DECAY * params[index_at]))
            firsts_now.append(first_new)
            seconds_now.append(second_new)
        clipped_biases.append(grads_now[4] * scale_now)
        losses.append(loss_now)
        norm_list.append(norm_now)
        local_weights.append(weights_now)
        first_lists.append(firsts_now)
        second_lists.append(seconds_now)
    new_weights, new_momenta, new_firsts, new_seconds = ([], [], [], [])
    for index_at in range(5):
        mean_local = sum((local_weights[group_at][index_at] for group_at in range(GROUPS))) / GROUPS
        outer_grad = params[index_at] - mean_local
        momentum_new = OUTER_MOMENTUM * momenta[index_at] + outer_grad
        new_weights.append(params[index_at] - OUTER_RATE * (outer_grad + OUTER_MOMENTUM * momentum_new))
        new_momenta.append(momentum_new)
        group_firsts = [first_lists[group_at][index_at] for group_at in range(GROUPS)]
        group_seconds = [second_lists[group_at][index_at] for group_at in range(GROUPS)]
        if index_at < 4:
            new_firsts.append(put_rows(group_firsts, axes_at[index_at]))
            new_seconds.append(put_rows(group_seconds, axes_at[index_at]))
        else:
            new_firsts.append(jnp.stack(group_firsts))
            new_seconds.append(jnp.stack(group_seconds))
    return (jnp.mean(jnp.stack(losses)), jnp.stack(norm_list), jnp.stack(clipped_biases), new_weights[0], new_weights[1], new_weights[2], new_weights[3], new_weights[4], new_momenta[0], new_momenta[1], new_momenta[2], new_momenta[3], new_momenta[4], new_firsts[0], new_seconds[0], new_firsts[1], new_seconds[1], new_firsts[2], new_seconds[2], new_firsts[3], new_seconds[3], new_firsts[4], new_seconds[4])
```

```python
import jax
import jax.numpy as jnp
from jax import lax
from jax.sharding import PartitionSpec as P

D = 768
HD = 64
FF = 3072
NCLS = 1000
FREQ = 256
PATCH_IN = 16
SIDE = 16
L = 2
GROUPS = 4
STEP_COUNT = 10
NSTEPS = 1000
S = 256
LB = 14


LOW_TYPE = jnp.bfloat16
LEARN_RATE = 0.03
WEIGHT_DECAY = 0.1
BETA_FIRST = 0.9
BETA_SECOND = 0.95
ADAM_EPSILON = 1e-08
CLIP_NORM = 0.02
OUTER_RATE = 0.7
OUTER_MOMENTUM = 0.9


def shortened(shard):
    return jax.tree.map(lambda a: a.astype(jnp.bfloat16) if a.dtype == jnp.float32 else a, shard)


def swapped(value, axis, bit):
    mask = 2**bit
    pairs = [(source, source ^ mask) for source in range(lax.axis_size(axis))]
    return lax.ppermute(value, axis, pairs)


def product(left, right):
    return jnp.dot(left, right, preferred_element_type=jnp.float32)


def product_t(left, right):
    return lax.dot_general(
        left, right, (((left.ndim - 1,), (1,)), ((), ())), preferred_element_type=jnp.float32
    )


def weight_grad(inputs, grads_out):
    leading = tuple(range(inputs.ndim - 1))
    return lax.dot_general(
        inputs, grads_out, ((leading, leading), ((), ())), preferred_element_type=jnp.float32
    )


def normalize(values):
    centred = values - jnp.mean(values, -1, keepdims=True)
    inverse = lax.rsqrt(jnp.mean(centred * centred, -1, keepdims=True) + 1e-06)
    return (centred * inverse, inverse)


def normalize_back(grad_in, normed, inverse):
    return inverse * (
        grad_in
        - jnp.mean(grad_in, -1, keepdims=True)
        - normed * jnp.mean(grad_in * normed, -1, keepdims=True)
    )


def gelu_tanh(values):
    return jax.nn.gelu(values, approximate=True)


def positions():
    quarter = D // 4
    omegas = 1.0 / 10000.0 ** (jnp.arange(quarter, dtype=jnp.float32) / quarter)
    places = jnp.arange(S, dtype=jnp.int32)
    across = (places % SIDE).astype(jnp.float32)[:, None] * omegas[None, :]
    downward = (places // SIDE).astype(jnp.float32)[:, None] * omegas[None, :]
    return jnp.concatenate(
        [jnp.sin(across), jnp.cos(across), jnp.sin(downward), jnp.cos(downward)], axis=1
    )


def frequencies(stamps):
    half_width = FREQ // 2
    freq_rates = jnp.exp(-jnp.log(10000.0) * jnp.arange(half_width, dtype=jnp.float32) / half_width)
    angles = stamps.astype(jnp.float32)[:, None] * freq_rates[None, :]
    return jnp.concatenate([jnp.cos(angles), jnp.sin(angles)], axis=1)


def signal_levels(stamps):
    noise_rates = jnp.linspace(0.0001, 0.02, NSTEPS, dtype=jnp.float32)
    kept_share = jnp.cumprod(1.0 - noise_rates)
    matches = stamps[:, None] == jnp.arange(NSTEPS, dtype=jnp.int32)[None, :]
    return jnp.sum(jnp.where(matches, kept_share[None, :], 0.0), axis=1)


def embed_parts(matrix):
    bounds = [
        NCLS,
        NCLS + FREQ,
        NCLS + FREQ + D,
        NCLS + FREQ + D + PATCH_IN,
        NCLS + FREQ + 3 * D + PATCH_IN,
    ]
    return (
        matrix[: bounds[0]],
        matrix[bounds[0] : bounds[1]],
        matrix[bounds[1] : bounds[2]],
        matrix[bounds[2] : bounds[3]],
        matrix[bounds[3] : bounds[4]],
        matrix[bounds[4] :],
    )


def split_heads(array_in):
    return array_in.reshape(array_in.shape[:2] + (array_in.shape[2] // HD, HD))


def head_scores(queries, key_rows):
    return jnp.einsum(
        "nqhd,nkhd->nhqk",
        split_heads(queries),
        split_heads(key_rows),
        preferred_element_type=jnp.float32,
    ) * HD ** (-0.5)


def attend(queries, key_rows, values):
    scores = head_scores(queries, key_rows)
    highest = jnp.max(scores, -1, keepdims=True)
    log_total = highest + jnp.log(jnp.sum(jnp.exp(scores - highest), -1, keepdims=True))
    weights = jnp.exp(scores - log_total).astype(LOW_TYPE)
    output = jnp.einsum(
        "nhqk,nkhd->nqhd", weights, split_heads(values), preferred_element_type=jnp.float32
    )
    return (output.reshape(queries.shape), log_total)


def attend_back(queries, key_rows, values, log_total, grad_out):
    weights = jnp.exp(head_scores(queries, key_rows) - log_total)
    grad_heads = split_heads(grad_out)
    grad_values = jnp.einsum(
        "nhqk,nqhd->nkhd", weights.astype(LOW_TYPE), grad_heads, preferred_element_type=jnp.float32
    )
    grad_weights = jnp.einsum(
        "nqhd,nkhd->nhqk", grad_heads, split_heads(values), preferred_element_type=jnp.float32
    )
    grad_scores = (
        weights * (grad_weights - jnp.sum(weights * grad_weights, -1, keepdims=True))
    ).astype(LOW_TYPE)
    grad_queries = jnp.einsum(
        "nhqk,nkhd->nqhd", grad_scores, split_heads(key_rows), preferred_element_type=jnp.float32
    ) * HD ** (-0.5)
    grad_keys = jnp.einsum(
        "nhqk,nqhd->nkhd", grad_scores, split_heads(queries), preferred_element_type=jnp.float32
    ) * HD ** (-0.5)
    return (
        grad_queries.reshape(queries.shape).astype(LOW_TYPE),
        grad_keys.reshape(queries.shape).astype(LOW_TYPE),
        grad_values.reshape(queries.shape).astype(LOW_TYPE),
    )


def place(vector_all, piece_in, offset):
    return lax.dynamic_update_slice_in_dim(vector_all, piece_in, offset, 0)


def flipped(value, masks):
    shards = lax.axis_size("tensor")
    count = lax.axis_size("dp") * shards
    pairs = [(source, source ^ masks[source // shards & 1]) for source in range(count)]
    return lax.ppermute(value, ("dp", "tensor"), pairs)


def picked_at(value, index_at, axis):
    return lax.dynamic_index_in_dim(value, index_at, axis, keepdims=False)


def layer_forward(stream, mod_parts, attn_now, mlp_now, bias_layer):
    width_all = stream.shape[-1]
    normed_one, inverse_one = normalize(stream)
    hidden_one = (normed_one * (1.0 + mod_parts[1]) + mod_parts[0]).astype(LOW_TYPE)
    queries = (product(hidden_one, attn_now[0]) + bias_layer[:width_all]).astype(LOW_TYPE)
    key_rows = product(hidden_one, attn_now[1]).astype(LOW_TYPE)
    values = (product(hidden_one, attn_now[2]) + bias_layer[width_all : 2 * width_all]).astype(
        LOW_TYPE
    )
    attended, log_total = attend(queries, key_rows, values)
    attended = attended.astype(LOW_TYPE)
    branch_one = product_t(attended, attn_now[3]) + bias_layer[2 * width_all : 3 * width_all]
    middle = stream + mod_parts[2] * branch_one
    normed_two, inverse_two = normalize(middle)
    hidden_two = (normed_two * (1.0 + mod_parts[4]) + mod_parts[3]).astype(LOW_TYPE)
    unit_width = mlp_now.shape[-1]
    before = [
        product(hidden_two, mlp_now[0, unit_at])
        + bias_layer[3 * width_all + unit_at * unit_width : 3 * width_all + (unit_at + 1) * unit_width]
        for unit_at in range(mlp_now.shape[1])
    ]
    activated = [gelu_tanh(part).astype(LOW_TYPE) for part in before]
    branch_two = bias_layer[3 * width_all + FF : 4 * width_all + FF] + sum(
        product_t(part, mlp_now[1, unit_at]) for unit_at, part in enumerate(activated)
    )
    result = middle + mod_parts[5] * branch_two
    kept_state = (
        normed_one,
        inverse_one,
        hidden_one,
        queries,
        key_rows,
        values,
        log_total,
        attended,
        branch_one,
        normed_two,
        inverse_two,
        hidden_two,
        before,
        activated,
        branch_two,
    )
    return (result, kept_state)


def layer_backward(grad_out, mod_parts, attn_now, mlp_now, kept_state):
    (
        normed_one,
        inverse_one,
        hidden_one,
        queries,
        key_rows,
        values,
        log_total,
        attended,
        branch_one,
        normed_two,
        inverse_two,
        hidden_two,
        saved_pre,
        activated,
        branch_two,
    ) = kept_state
    grad_gate_two = jnp.sum(grad_out * branch_two, 1)
    downward = grad_out * mod_parts[5]
    down_low = downward.astype(LOW_TYPE)
    grad_pre = [
        jax.vjp(gelu_tanh, part)[1](product(down_low, mlp_now[1, unit_at]))[0].astype(LOW_TYPE)
        for unit_at, part in enumerate(saved_pre)
    ]
    grad_down = [weight_grad(down_low, part).astype(LOW_TYPE) for part in activated]
    grad_up = [weight_grad(hidden_two, part).astype(LOW_TYPE) for part in grad_pre]
    mlp_sums = reduced_blocks(mlp_blocks(jnp.stack([jnp.stack(grad_up), jnp.stack(grad_down)])))
    grad_hidden_two = sum(
        product_t(part, mlp_now[0, unit_at]) for unit_at, part in enumerate(grad_pre)
    )
    grad_middle = grad_out + normalize_back(
        grad_hidden_two * (1.0 + mod_parts[4]), normed_two, inverse_two
    )
    grad_gate_one = jnp.sum(grad_middle * branch_one, 1)
    upward = grad_middle * mod_parts[2]
    up_low = upward.astype(LOW_TYPE)
    grad_out_map = weight_grad(up_low, attended)
    grad_attended = product(up_low, attn_now[3]).astype(LOW_TYPE)
    grad_queries, grad_keys, grad_values = attend_back(
        queries, key_rows, values, log_total, grad_attended
    )
    attn_sums = reduced_blocks(
        attn_blocks(
            jnp.stack(
                [
                    weight_grad(hidden_one, grad_queries).astype(LOW_TYPE),
                    weight_grad(hidden_one, grad_keys).astype(LOW_TYPE),
                    weight_grad(hidden_one, grad_values).astype(LOW_TYPE),
                    grad_out_map.astype(LOW_TYPE),
                ]
            )
        )
    )
    grad_hidden_one = (
        product_t(grad_queries, attn_now[0])
        + product_t(grad_keys, attn_now[1])
        + product_t(grad_values, attn_now[2])
    )
    grad_stream = grad_middle + normalize_back(
        grad_hidden_one * (1.0 + mod_parts[1]), normed_one, inverse_one
    )
    grad_modulation = jnp.concatenate(
        [
            jnp.sum(grad_hidden_one, 1),
            jnp.sum(grad_hidden_one * normed_one, 1),
            grad_gate_one,
            jnp.sum(grad_hidden_two, 1),
            jnp.sum(grad_hidden_two * normed_two, 1),
            grad_gate_two,
        ],
        axis=1,
    ).astype(LOW_TYPE)
    bias_grad = jnp.concatenate(
        [
            jnp.sum(grad_queries.astype(jnp.float32), (0, 1)),
            jnp.sum(grad_values.astype(jnp.float32), (0, 1)),
            jnp.sum(upward, (0, 1)),
        ]
        + [jnp.sum(part.astype(jnp.float32), (0, 1)) for part in grad_pre]
        + [jnp.sum(downward, (0, 1))]
    )
    return (grad_stream, attn_sums, mlp_sums, grad_modulation, bias_grad)


def attn_blocks(grads):
    stretches = lax.axis_size("dp") // GROUPS
    shards = lax.axis_size("tensor")
    kinds, rows_all, width_all = grads.shape
    shaped = grads.reshape(
        kinds, stretches, rows_all // stretches, 2, shards // 2, width_all // shards
    )
    return jnp.transpose(shaped, (3, 4, 1, 2, 0, 5)).reshape(
        2, 1, shards // 2, stretches, rows_all // stretches, kinds * width_all // shards
    )


def mlp_blocks(grads):
    stretches = lax.axis_size("dp") // GROUPS
    kinds, shards, rows_all, width = grads.shape
    shaped = grads.reshape(kinds, 2, shards // 2, stretches, rows_all // stretches, width)
    return jnp.transpose(shaped, (1, 0, 2, 3, 4, 5))


def summed_low(left, right):
    return (left.astype(jnp.float32) + right.astype(jnp.float32)).astype(LOW_TYPE)


def reduced_blocks(blocks):
    shards = lax.axis_size("tensor")
    dp_at, shard_at = (lax.axis_index("dp"), lax.axis_index("tensor"))
    low_bit, stretch, shard_low = (dp_at & 1, dp_at // GROUPS, shard_at & 1)
    kinds, columns, stretches, rows, width = blocks.shape[1:]
    core_mask = shards
    received = flipped(picked_at(blocks, 1 - low_bit, 0), (core_mask, core_mask))
    total = summed_low(picked_at(blocks, low_bit, 0), received)
    total = jnp.where(
        low_bit == 1,
        total.reshape(kinds, columns * stretches, rows, width),
        jnp.swapaxes(total, 1, 2).reshape(kinds, columns * stretches, rows, width),
    )
    column_step = (shard_low, 1)
    row_steps = [
        (stretch >> bit_at & 1, shards * GROUPS << bit_at)
        for bit_at in reversed(range(stretches.bit_length() - 1))
    ]
    rows_first, columns_first = (row_steps + [column_step], [column_step] + row_steps)
    for (bit_zero, mask_zero), (bit_one, mask_one) in zip(rows_first, columns_first):
        own_bit = jnp.where(low_bit == 1, bit_one, bit_zero)
        halves = total.reshape(kinds, 2, total.shape[1] // 2, rows, width)
        received = flipped(picked_at(halves, 1 - own_bit, 1), (mask_zero, mask_one))
        total = summed_low(picked_at(halves, own_bit, 1), received)
    count = lax.axis_size("dp") * shards
    pairs = []
    for source in range(count):
        core, high = (source // shards & 1, source % shards >> 1)
        changed = (core ^ high) * (shards + shards // 2)
        pairs.append((source, source ^ changed))
    return lax.ppermute(total[:, 0], ("dp", "tensor"), pairs)


def own_latents(value):
    shards = lax.axis_size("tensor")
    low_bit, shard_at = (lax.axis_index("dp") & 1, lax.axis_index("tensor"))
    count = value.shape[0] // shards
    base = (shard_at & 1) * 2
    mine = lax.dynamic_slice_in_dim(value, (base + low_bit) * count, count, 0)
    theirs = lax.dynamic_slice_in_dim(value, (base + 1 - low_bit) * count, count, 0)
    received = flipped(theirs, (shards, shards))
    return jnp.where(shard_at >> 1 == low_bit, mine, received)


def natural_order(gathered, stretches):
    shaped = gathered.reshape((stretches, 2, 2, 2, 2) + gathered.shape[1:])
    moved = jnp.moveaxis(shaped, 2, 4)
    return moved.reshape((-1,) + gathered.shape[2:])


def split_bits(array_in, axis_at, count_bits):
    dims_in = array_in.shape
    return array_in.reshape(
        dims_in[:axis_at]
        + (2,) * count_bits
        + (dims_in[axis_at] >> count_bits,)
        + dims_in[axis_at + 1 :]
    )


def reduce_pieces(arrays, axes_at, shift_bits, count_bits, bit_order, across):
    dp_at = lax.axis_index("dp")
    blocks = [
        split_bits(array_in, axis_at, count_bits) for array_in, axis_at in zip(arrays, axes_at)
    ]
    for bit_at in bit_order:
        own_bit = dp_at >> shift_bits + bit_at & 1
        kept_half = [
            lax.dynamic_slice_in_dim(block_in, own_bit, 1, axis_at + count_bits - 1 - bit_at)
            for block_in, axis_at in zip(blocks, axes_at)
        ]
        sent_half = [
            lax.dynamic_slice_in_dim(block_in, 1 - own_bit, 1, axis_at + count_bits - 1 - bit_at)
            for block_in, axis_at in zip(blocks, axes_at)
        ]
        if across:
            received = swapped(
                (
                    shortened(sent_half[0]),
                    shortened(sent_half[1]),
                    shortened(sent_half[2]),
                    shortened(sent_half[3]),
                ),
                "dp",
                shift_bits + bit_at,
            )
        else:
            received = swapped(
                (
                    shortened(sent_half[0]),
                    shortened(sent_half[1]),
                    shortened(sent_half[2]),
                    shortened(sent_half[3]),
                ),
                "dp",
                shift_bits + bit_at,
            )
        blocks = [own_part + other_part for own_part, other_part in zip(kept_half, received)]
    return [
        block_in.reshape(
            array_in.shape[:axis_at]
            + (array_in.shape[axis_at] >> count_bits,)
            + array_in.shape[axis_at + 1 :]
        )
        for block_in, array_in, axis_at in zip(blocks, arrays, axes_at)
    ]


def adam_update(gradient, first_old, second_old):
    first_new = BETA_FIRST * first_old + (1.0 - BETA_FIRST) * gradient
    second_new = BETA_SECOND * second_old + (1.0 - BETA_SECOND) * gradient * gradient
    update = (
        first_new
        / (1.0 - BETA_FIRST**STEP_COUNT)
        / (jnp.sqrt(second_new / (1.0 - BETA_SECOND**STEP_COUNT)) + ADAM_EPSILON)
    )
    return (update, first_new, second_new)


def per_device(
    patches,
    noise_draw,
    timesteps,
    labels,
    w_attn,
    w_mlp,
    w_mod,
    w_embed,
    biases,
    momentum_attn,
    momentum_mlp,
    momentum_mod,
    momentum_embed,
    momentum_bias,
    first_attn,
    second_attn,
    first_mlp,
    second_mlp,
    first_mod,
    second_mod,
    first_embed,
    second_embed,
    first_bias,
    second_bias,
):
    shards = lax.axis_size("tensor")
    shard_at = lax.axis_index("tensor")
    dp_count = lax.axis_size("dp")
    dp_at = lax.axis_index("dp")
    group_at = dp_at % GROUPS
    stretches = dp_count // GROUPS
    stretch = dp_at // GROUPS
    layer_span = LB * D
    col_width = w_attn.shape[3]
    row_width = w_attn.shape[2]
    mod_width = w_mod.shape[2]
    latents = dp_count * patches.shape[0]
    everyone = ("tensor", "dp")

    stamps, marks = lax.all_gather(jnp.stack([timesteps, labels]), "dp", axis=1, tiled=True)
    embed_low = w_embed.astype(LOW_TYPE)
    conditioners = NCLS + FREQ + D + PATCH_IN
    embed_all = lax.all_gather(
        jnp.concatenate([embed_low[:conditioners], embed_low[-PATCH_IN:]]), "dp", axis=1, tiled=True
    )
    class_table = embed_all[:NCLS]
    first_time = embed_all[NCLS : NCLS + FREQ]
    second_time = embed_all[NCLS + FREQ : NCLS + FREQ + D]
    patch_map = embed_all[NCLS + FREQ + D : conditioners]
    head_map = embed_all[conditioners:]
    attn_all, mlp_all = ([], [])
    for layer_at in range(L):
        attn_local = jnp.transpose(w_attn[layer_at], (1, 0, 2)).reshape(row_width, 4 * col_width)
        local = jnp.concatenate([attn_local[None], w_mlp[layer_at]]).astype(LOW_TYPE)
        whole = lax.all_gather(local, everyone, axis=1, tiled=True)
        whole = whole.reshape(3, shards, D, -1)
        attn_all.append(
            jnp.transpose(whole[0].reshape(shards, D, 4, col_width), (2, 1, 0, 3)).reshape(4, D, D)
        )
        mlp_all.append(whole[1:])

    bias_flat = biases.reshape(-1)
    bias_tail = bias_flat[L * layer_span :]
    freq_low = frequencies(stamps).astype(LOW_TYPE)
    hidden_time = product(freq_low, first_time) + bias_tail[D : 2 * D]
    smooth_time = jax.nn.silu(hidden_time).astype(LOW_TYPE)
    class_picks = (marks[:, None] == jnp.arange(NCLS, dtype=jnp.int32)[None, :]).astype(LOW_TYPE)
    condition = (
        product(smooth_time, second_time)
        + bias_tail[2 * D : 3 * D]
        + product(class_picks, class_table)
    )
    cond_act = jax.nn.silu(condition).astype(LOW_TYPE)
    mod_low = w_mod.astype(LOW_TYPE)
    final_low = embed_low[conditioners:-PATCH_IN]
    final_width = final_low.shape[0] // shards
    cond_rows = lax.dynamic_slice_in_dim(cond_act, dp_at * row_width, row_width, 1)
    mod_cols = jnp.concatenate(
        [product(cond_rows, mod_low[layer_at]) for layer_at in range(L)]
        + [
            product_t(
                cond_rows, lax.dynamic_slice_in_dim(final_low, shard_at * final_width, final_width, 0)
            )
        ],
        axis=1,
    )
    mod_cols = lax.psum_scatter(mod_cols, "dp", scatter_dimension=0, tiled=True)
    mod_all = own_latents(
        jnp.swapaxes(lax.all_gather(mod_cols.astype(LOW_TYPE), "tensor"), 0, 1)
    ).astype(jnp.float32)
    mod_parts = []
    for layer_at in range(L):
        modulation = (
            mod_all[:, :, layer_at * mod_width : (layer_at + 1) * mod_width].reshape(-1, 6 * D)
            + bias_flat[layer_at * layer_span + 4 * D + FF : (layer_at + 1) * layer_span]
        )
        mod_parts.append(
            [modulation[:, None, part_at * D : (part_at + 1) * D] for part_at in range(6)]
        )
    final_mod = mod_all[:, :, L * mod_width :].reshape(-1, 2 * D) + bias_tail[3 * D : 5 * D]

    patches_own, noise_own = (own_latents(patches), own_latents(noise_draw))
    signal = own_latents(signal_levels(timesteps)[:, None])[:, :, None]
    noised = (jnp.sqrt(signal) * patches_own + jnp.sqrt(1.0 - signal) * noise_own).astype(LOW_TYPE)
    stream = product(noised, patch_map) + bias_tail[:D] + positions()
    saved_states = []
    for layer_at in range(L):
        stream, kept_state = layer_forward(
            stream,
            mod_parts[layer_at],
            attn_all[layer_at],
            mlp_all[layer_at],
            bias_flat[layer_at * layer_span : (layer_at + 1) * layer_span],
        )
        saved_states.append(kept_state)
    normed_last, inverse_last = normalize(stream)
    hidden_last = (normed_last * (1.0 + final_mod[:, None, D:]) + final_mod[:, None, :D]).astype(
        LOW_TYPE
    )
    predicted = product_t(hidden_last, head_map)
    errors = predicted - noise_own
    elements = dp_count // GROUPS * patches.shape[0] * S * PATCH_IN
    loss_here = jnp.sum(errors * errors) / elements
    grad_pred = (2.0 * errors / elements).astype(LOW_TYPE)
    grad_head = weight_grad(grad_pred, hidden_last)
    grad_hidden = product(grad_pred, head_map)
    grad_final = jnp.concatenate(
        [jnp.sum(grad_hidden, 1), jnp.sum(grad_hidden * normed_last, 1)], axis=1
    ).astype(LOW_TYPE)
    grad_stream = normalize_back(
        grad_hidden * (1.0 + final_mod[:, None, D:]), normed_last, inverse_last
    )
    attn_list, mlp_list, mod_list, bias_list = ([None] * L, [None] * L, [None] * L, [None] * L)
    for layer_at in range(L - 1, -1, -1):
        (
            grad_stream,
            attn_list[layer_at],
            mlp_list[layer_at],
            mod_list[layer_at],
            bias_list[layer_at],
        ) = layer_backward(
            grad_stream,
            mod_parts[layer_at],
            attn_all[layer_at],
            mlp_all[layer_at],
            saved_states[layer_at],
        )
    grad_patch = weight_grad(noised, grad_stream.astype(LOW_TYPE))
    mine = patches_own.shape[0]
    vectors = jnp.concatenate(
        [grad_now.reshape(-1) for grad_now in mod_list]
        + [grad_final.reshape(-1)]
        + [grad_now.astype(LOW_TYPE) for grad_now in bias_list]
        + [
            jnp.sum(grad_stream, (0, 1)).astype(LOW_TYPE),
            grad_patch.astype(LOW_TYPE).reshape(-1),
            grad_head.astype(LOW_TYPE).reshape(-1),
        ]
    )
    gathered = lax.all_gather(vectors, ("dp", "tensor"))
    devices = dp_count * shards
    offset = 0

    def taken(width):
        nonlocal offset
        offset += width
        return gathered[:, offset - width : offset]

    grad_mods = [
        natural_order(taken(mine * 6 * D).reshape(devices, mine, 6 * D), stretches)
        for layer_at in range(L)
    ]
    grad_finals = natural_order(taken(mine * 2 * D).reshape(devices, mine, 2 * D), stretches)

    def group_sums(part):
        shaped = part.astype(jnp.float32).reshape(stretches, 2, 2, 2, shards // 2, -1)
        return jnp.sum(shaped, (0, 2, 4)).reshape(GROUPS, -1)

    layer_bias = 7 * D + FF - 3 * D
    bias_sums = [group_sums(taken(layer_bias)) for layer_at in range(L)]
    patch_bias = group_sums(taken(D))
    patch_sums = group_sums(taken(PATCH_IN * D)).reshape(GROUPS, PATCH_IN, D)
    head_sums = group_sums(taken(PATCH_IN * D)).reshape(GROUPS, PATCH_IN, D)

    own_mods = [
        lax.dynamic_slice_in_dim(grad_now, shard_at * mod_width, mod_width, 1)
        for grad_now in grad_mods
    ]
    grad_cond_parts = sum(
        product_t(own_mods[layer_at], mod_low[layer_at]) for layer_at in range(L)
    )
    grad_cond_act = lax.psum(grad_cond_parts.astype(jnp.bfloat16), "tensor").astype(
        jnp.float32
    ) + product(grad_finals, final_low)
    condition_rows = lax.dynamic_slice_in_dim(condition, dp_at * row_width, row_width, 1)
    grad_condition = lax.all_gather(
        jax.vjp(jax.nn.silu, condition_rows)[1](grad_cond_act)[0].astype(LOW_TYPE),
        "dp",
        axis=1,
        tiled=True,
    )
    grad_smooth = product_t(grad_condition, second_time)
    grad_hidden_time = jax.vjp(jax.nn.silu, hidden_time)[1](grad_smooth)[0].astype(LOW_TYPE)

    def of_group(value):
        shaped = value.reshape((stretches, GROUPS, latents // dp_count) + value.shape[1:])
        return picked_at(shaped, group_at, 1).reshape((-1,) + value.shape[1:])

    def of_stretch(value):
        width = value.shape[-1] // stretches
        return lax.dynamic_slice_in_dim(value, stretch * width, width, value.ndim - 1)

    def latent_sums(value):
        shaped = value.astype(jnp.float32).reshape(stretches, GROUPS, latents // dp_count, -1)
        return jnp.sum(shaped, (0, 2))

    grad_condition_own = of_stretch(of_group(grad_condition))
    cond_own = of_stretch(of_group(cond_act))
    grad_embed = jnp.concatenate(
        [
            weight_grad(of_group(class_picks), grad_condition_own),
            weight_grad(of_group(freq_low), of_stretch(of_group(grad_hidden_time))),
            weight_grad(of_group(smooth_time), grad_condition_own),
            of_stretch(picked_at(patch_sums, group_at, 0)),
            weight_grad(of_group(grad_finals), cond_own),
            of_stretch(picked_at(head_sums, group_at, 0)),
        ],
        0,
    )
    grad_mod_map = jnp.stack([weight_grad(cond_own, of_group(grad_now)) for grad_now in own_mods])
    bias_groups = jnp.concatenate(
        [
            part
            for layer_at in range(L)
            for part in (bias_sums[layer_at], latent_sums(grad_mods[layer_at]))
        ]
        + [
            patch_bias,
            latent_sums(grad_hidden_time),
            latent_sums(grad_condition),
            latent_sums(grad_finals),
        ],
        axis=1,
    )
    attn_now = jnp.stack(
        [
            jnp.transpose(part.reshape(-1, 4, col_width), (1, 0, 2)).astype(jnp.float32)
            for part in attn_list
        ]
    )
    reduced = [attn_now, jnp.stack(mlp_list).astype(jnp.float32), grad_mod_map, grad_embed]
    squares = (
        jnp.sum(reduced[0] * reduced[0])
        + jnp.sum(reduced[1] * reduced[1])
        + jnp.sum(reduced[2] * reduced[2])
        + jnp.sum(reduced[3] * reduced[3]) / shards
    )
    picked = (jnp.arange(GROUPS, dtype=jnp.int32) == group_at).astype(jnp.float32)
    totals = lax.psum(
        jnp.concatenate([picked * squares, jnp.reshape(loss_here, (1,))]), ("dp", "tensor")
    )
    group_norms = jnp.sqrt(totals[:GROUPS] + jnp.sum(bias_groups * bias_groups, 1))
    clip_scale = CLIP_NORM / (group_norms + 1e-06)
    own_scale = jnp.sum(picked * clip_scale)
    shift_group = GROUPS.bit_length() - 1
    weights_in = (w_attn, w_mlp, w_mod, w_embed)
    momenta_in = (momentum_attn, momentum_mlp, momentum_mod, momentum_embed)
    firsts_in = (first_attn, first_mlp, first_mod, first_embed)
    seconds_in = (second_attn, second_mlp, second_mod, second_embed)
    updates, new_firsts, new_seconds = ([], [], [])
    for index_at in range(4):
        update, first_new, second_new = adam_update(
            reduced[index_at] * own_scale, firsts_in[index_at], seconds_in[index_at]
        )
        updates.append(update)
        new_firsts.append(first_new)
        new_seconds.append(second_new)
    summed = reduce_pieces(updates, (2, 2, 1, 1), 0, shift_group, list(range(shift_group)), True)
    new_weights, new_momenta = ([], [])
    for index_at in range(4):
        outer_grad = LEARN_RATE * (summed[index_at] / GROUPS + WEIGHT_DECAY * weights_in[index_at])
        momentum_new = OUTER_MOMENTUM * momenta_in[index_at] + outer_grad
        new_weights.append(
            weights_in[index_at] - OUTER_RATE * (outer_grad + OUTER_MOMENTUM * momentum_new)
        )
        new_momenta.append(momentum_new)
    clipped_bias = bias_groups * clip_scale[:, None]
    bias_updates, bias_first, bias_second = adam_update(
        clipped_bias, first_bias.reshape(GROUPS, -1), second_bias.reshape(GROUPS, -1)
    )
    outer_bias = LEARN_RATE * (jnp.mean(bias_updates, 0) + WEIGHT_DECAY * bias_flat)
    bias_momentum = OUTER_MOMENTUM * momentum_bias.reshape(-1) + outer_bias
    bias_new = bias_flat - OUTER_RATE * (outer_bias + OUTER_MOMENTUM * bias_momentum)
    return (
        totals[GROUPS] / GROUPS,
        group_norms,
        clipped_bias.reshape(first_bias.shape),
        new_weights[0],
        new_weights[1],
        new_weights[2],
        new_weights[3],
        bias_new.reshape(biases.shape),
        new_momenta[0],
        new_momenta[1],
        new_momenta[2],
        new_momenta[3],
        bias_momentum.reshape(biases.shape),
        new_firsts[0],
        new_seconds[0],
        new_firsts[1],
        new_seconds[1],
        new_firsts[2],
        new_seconds[2],
        new_firsts[3],
        new_seconds[3],
        bias_first.reshape(first_bias.shape),
        bias_second.reshape(second_bias.shape),
    )


def solution(mesh):
    placed = (
        P("dp", None, None),
        P("dp", None, None),
        P("dp"),
        P("dp"),
        P(None, None, "dp", "tensor"),
        P(None, None, "dp", "tensor"),
        P(None, "dp", "tensor"),
        P(None, "dp"),
        P(),
        P(None, None, "dp", "tensor"),
        P(None, None, "dp", "tensor"),
        P(None, "dp", "tensor"),
        P(None, "dp"),
        P(),
        P(None, None, "dp", "tensor"),
        P(None, None, "dp", "tensor"),
        P(None, None, "dp", "tensor"),
        P(None, None, "dp", "tensor"),
        P(None, "dp", "tensor"),
        P(None, "dp", "tensor"),
        P(None, "dp"),
        P(None, "dp"),
        P(),
        P(),
    )
    return jax.shard_map(
        per_device,
        mesh=mesh,
        in_specs=placed,
        out_specs=(
            P(),
            P(),
            P(),
            P(None, None, "dp", "tensor"),
            P(None, None, "dp", "tensor"),
            P(None, "dp", "tensor"),
            P(None, "dp"),
            P(),
            P(None, None, "dp", "tensor"),
            P(None, None, "dp", "tensor"),
            P(None, "dp", "tensor"),
            P(None, "dp"),
            P(),
            P(None, None, "dp", "tensor"),
            P(None, None, "dp", "tensor"),
            P(None, None, "dp", "tensor"),
            P(None, None, "dp", "tensor"),
            P(None, "dp", "tensor"),
            P(None, "dp", "tensor"),
            P(None, "dp"),
            P(None, "dp"),
            P(),
            P(),
        ),
        check_vma=False,
    )
```

```python
import jax
import jax.numpy as jnp
from jax import lax
from jax.sharding import PartitionSpec as P

D = 768
HD = 64
FF = 3072
NCLS = 1000
FREQ = 256
PATCH_IN = 16
SIDE = 16
L = 2
GROUPS = 4
STEP_COUNT = 10
NSTEPS = 1000
S = 256
LB = 14


LOW_TYPE = jnp.bfloat16
LEARN_RATE = 0.03
WEIGHT_DECAY = 0.1
BETA_FIRST = 0.9
BETA_SECOND = 0.95
ADAM_EPSILON = 1e-08
CLIP_NORM = 0.02
OUTER_RATE = 0.7
OUTER_MOMENTUM = 0.9


def shortened(shard):
    return jax.tree.map(lambda a: a.astype(jnp.bfloat16) if a.dtype == jnp.float32 else a, shard)


def swapped(value, axis, bit):
    mask = 2**bit
    pairs = [(source, source ^ mask) for source in range(lax.axis_size(axis))]
    return lax.ppermute(value, axis, pairs)


def product(left, right):
    return jnp.dot(left, right, preferred_element_type=jnp.float32)


def product_t(left, right):
    return lax.dot_general(
        left, right, (((left.ndim - 1,), (1,)), ((), ())), preferred_element_type=jnp.float32
    )


def weight_grad(inputs, grads_out):
    leading = tuple(range(inputs.ndim - 1))
    return lax.dot_general(
        inputs, grads_out, ((leading, leading), ((), ())), preferred_element_type=jnp.float32
    )


def normalize(values):
    centred = values - jnp.mean(values, -1, keepdims=True)
    inverse = lax.rsqrt(jnp.mean(centred * centred, -1, keepdims=True) + 1e-06)
    return (centred * inverse, inverse)


def normalize_back(grad_in, normed, inverse):
    return inverse * (
        grad_in
        - jnp.mean(grad_in, -1, keepdims=True)
        - normed * jnp.mean(grad_in * normed, -1, keepdims=True)
    )


def gelu_tanh(values):
    return jax.nn.gelu(values, approximate=True)


def positions():
    quarter = D // 4
    omegas = 1.0 / 10000.0 ** (jnp.arange(quarter, dtype=jnp.float32) / quarter)
    places = jnp.arange(S, dtype=jnp.int32)
    across = (places % SIDE).astype(jnp.float32)[:, None] * omegas[None, :]
    downward = (places // SIDE).astype(jnp.float32)[:, None] * omegas[None, :]
    return jnp.concatenate(
        [jnp.sin(across), jnp.cos(across), jnp.sin(downward), jnp.cos(downward)], axis=1
    )


def frequencies(stamps):
    half_width = FREQ // 2
    freq_rates = jnp.exp(-jnp.log(10000.0) * jnp.arange(half_width, dtype=jnp.float32) / half_width)
    angles = stamps.astype(jnp.float32)[:, None] * freq_rates[None, :]
    return jnp.concatenate([jnp.cos(angles), jnp.sin(angles)], axis=1)


def signal_levels(stamps):
    noise_rates = jnp.linspace(0.0001, 0.02, NSTEPS, dtype=jnp.float32)
    kept_share = jnp.cumprod(1.0 - noise_rates)
    matches = stamps[:, None] == jnp.arange(NSTEPS, dtype=jnp.int32)[None, :]
    return jnp.sum(jnp.where(matches, kept_share[None, :], 0.0), axis=1)


def embed_parts(matrix):
    bounds = [
        NCLS,
        NCLS + FREQ,
        NCLS + FREQ + D,
        NCLS + FREQ + D + PATCH_IN,
        NCLS + FREQ + 3 * D + PATCH_IN,
    ]
    return (
        matrix[: bounds[0]],
        matrix[bounds[0] : bounds[1]],
        matrix[bounds[1] : bounds[2]],
        matrix[bounds[2] : bounds[3]],
        matrix[bounds[3] : bounds[4]],
        matrix[bounds[4] :],
    )


def split_heads(array_in):
    return array_in.reshape(array_in.shape[:2] + (array_in.shape[2] // HD, HD))


def head_scores(queries, key_rows):
    return jnp.einsum(
        "nqhd,nkhd->nhqk",
        split_heads(queries),
        split_heads(key_rows),
        preferred_element_type=jnp.float32,
    ) * HD ** (-0.5)


def attend(queries, key_rows, values):
    scores = head_scores(queries, key_rows)
    highest = jnp.max(scores, -1, keepdims=True)
    log_total = highest + jnp.log(jnp.sum(jnp.exp(scores - highest), -1, keepdims=True))
    weights = jnp.exp(scores - log_total).astype(LOW_TYPE)
    output = jnp.einsum(
        "nhqk,nkhd->nqhd", weights, split_heads(values), preferred_element_type=jnp.float32
    )
    return (output.reshape(queries.shape), log_total)


def attend_back(queries, key_rows, values, log_total, grad_out):
    weights = jnp.exp(head_scores(queries, key_rows) - log_total)
    grad_heads = split_heads(grad_out)
    grad_values = jnp.einsum(
        "nhqk,nqhd->nkhd", weights.astype(LOW_TYPE), grad_heads, preferred_element_type=jnp.float32
    )
    grad_weights = jnp.einsum(
        "nqhd,nkhd->nhqk", grad_heads, split_heads(values), preferred_element_type=jnp.float32
    )
    grad_scores = (
        weights * (grad_weights - jnp.sum(weights * grad_weights, -1, keepdims=True))
    ).astype(LOW_TYPE)
    grad_queries = jnp.einsum(
        "nhqk,nkhd->nqhd", grad_scores, split_heads(key_rows), preferred_element_type=jnp.float32
    ) * HD ** (-0.5)
    grad_keys = jnp.einsum(
        "nhqk,nqhd->nkhd", grad_scores, split_heads(queries), preferred_element_type=jnp.float32
    ) * HD ** (-0.5)
    return (
        grad_queries.reshape(queries.shape).astype(LOW_TYPE),
        grad_keys.reshape(queries.shape).astype(LOW_TYPE),
        grad_values.reshape(queries.shape).astype(LOW_TYPE),
    )


def place(vector_all, piece_in, offset):
    return lax.dynamic_update_slice_in_dim(vector_all, piece_in, offset, 0)


def flipped(value, masks):
    shards = lax.axis_size("tensor")
    count = lax.axis_size("dp") * shards
    pairs = [(source, source ^ masks[source // shards & 1]) for source in range(count)]
    return lax.ppermute(value, ("dp", "tensor"), pairs)


def picked_at(value, index_at, axis):
    return lax.dynamic_index_in_dim(value, index_at, axis, keepdims=False)


def layer_forward(stream, mod_parts, attn_now, mlp_now, bias_layer):
    width_all = stream.shape[-1]
    normed_one, inverse_one = normalize(stream)
    hidden_one = (normed_one * (1.0 + mod_parts[1]) + mod_parts[0]).astype(LOW_TYPE)
    queries = (product(hidden_one, attn_now[0]) + bias_layer[:width_all]).astype(LOW_TYPE)
    key_rows = product(hidden_one, attn_now[1]).astype(LOW_TYPE)
    values = (product(hidden_one, attn_now[2]) + bias_layer[width_all : 2 * width_all]).astype(
        LOW_TYPE
    )
    attended, log_total = attend(queries, key_rows, values)
    attended = attended.astype(LOW_TYPE)
    branch_one = product_t(attended, attn_now[3]) + bias_layer[2 * width_all : 3 * width_all]
    middle = stream + mod_parts[2] * branch_one
    normed_two, inverse_two = normalize(middle)
    hidden_two = (normed_two * (1.0 + mod_parts[4]) + mod_parts[3]).astype(LOW_TYPE)
    unit_width = mlp_now[0][0].shape[-1]
    before = [
        product(hidden_two, mlp_now[0][unit_at])
        + bias_layer[3 * width_all + unit_at * unit_width : 3 * width_all + (unit_at + 1) * unit_width]
        for unit_at in range(len(mlp_now[0]))
    ]
    activated = [gelu_tanh(part).astype(LOW_TYPE) for part in before]
    branch_two = bias_layer[3 * width_all + FF : 4 * width_all + FF] + sum(
        product_t(part, mlp_now[1][unit_at]) for unit_at, part in enumerate(activated)
    )
    result = middle + mod_parts[5] * branch_two
    kept_state = (
        normed_one,
        inverse_one,
        hidden_one,
        queries,
        key_rows,
        values,
        log_total,
        attended,
        branch_one,
        normed_two,
        inverse_two,
        hidden_two,
        before,
        activated,
        branch_two,
    )
    return (result, kept_state)


def exchanged(value, mask):
    count = lax.axis_size("dp") * lax.axis_size("tensor")
    return lax.ppermute(value, ("dp", "tensor"), [(source, source ^ mask) for source in range(count)])


def half_of(value, axis, bit):
    width = value.shape[axis] // 2
    return lax.dynamic_slice_in_dim(value, bit * width, width, axis)


def summed_low(left, right):
    return (left.astype(jnp.float32) + right.astype(jnp.float32)).astype(LOW_TYPE)


def rows_halved(value):
    stretch = lax.axis_index("dp") // GROUPS
    stretches = lax.axis_size("dp") // GROUPS
    for bit_at in reversed(range(stretches.bit_length() - 1)):
        bit = stretch >> bit_at & 1
        received = exchanged(
            half_of(value, 0, 1 - bit), lax.axis_size("tensor") * GROUPS << bit_at
        )
        value = summed_low(half_of(value, 0, bit), received)
    return value


def columns_halved(sent, kept):
    return summed_low(kept, exchanged(sent, 1))


def unit_halved(first, second):
    picked = (lax.axis_index("tensor") & 1) == 1
    return columns_halved(jnp.where(picked, first, second), jnp.where(picked, second, first))


def pair_halved(first, second):
    bit = lax.axis_index("tensor") & 1

    def halves(bit_now):
        return jnp.concatenate([half_of(first, 1, bit_now), half_of(second, 1, bit_now)], 1)

    return columns_halved(halves(1 - bit), halves(bit))


def core_summed(sent, kept):
    return [
        summed_low(own, exchanged(other, lax.axis_size("tensor"))) for other, own in zip(sent, kept)
    ]


def homeward(values):
    shards = lax.axis_size("tensor")
    pairs = []
    for source in range(lax.axis_size("dp") * shards):
        core, high = (source // shards & 1, source % shards >> 1)
        pairs.append((source, source ^ (core ^ high) * (shards + shards // 2)))
    return [lax.ppermute(value, ("dp", "tensor"), pairs) for value in values]


def mlp_second(totals):
    up_zero, up_one, down_zero, down_one = totals
    return [rows_halved(up_zero), rows_halved(up_one), unit_halved(down_zero, down_one)]


def mlp_third(totals):
    up_zero, up_one, down = totals
    return [unit_halved(up_zero, up_one), rows_halved(down)]


def attn_second(totals):
    query_key, value_map, out_map = totals
    return [rows_halved(query_key), pair_halved(value_map, out_map)]


def attn_third(totals):
    query_key, value_out = totals
    width = query_key.shape[1] // 2
    return [pair_halved(query_key[:, :width], query_key[:, width:]), rows_halved(value_out)]


def tied(value, flows):
    return lax.optimization_barrier((value, flows))


def layer_backward(grad_out, mod_parts, attn_now, mlp_now, kept_state, flows):
    (
        normed_one,
        inverse_one,
        hidden_one,
        queries,
        key_rows,
        values,
        log_total,
        attended,
        branch_one,
        normed_two,
        inverse_two,
        hidden_two,
        saved_pre,
        activated,
        branch_two,
    ) = kept_state
    core = lax.axis_index("dp") & 1
    pair = len(activated) // 2
    if flows:
        flows = [mlp_second(flows[0]), flows[1]]
        grad_out, flows = tied(grad_out, flows)
    grad_gate_two = jnp.sum(grad_out * branch_two, 1)
    downward = grad_out * mod_parts[5]
    down_low = downward.astype(LOW_TYPE)
    grad_pre = [
        jax.vjp(gelu_tanh, part)[1](product(down_low, mlp_now[1][unit_at]))[0].astype(LOW_TYPE)
        for unit_at, part in enumerate(saved_pre)
    ]

    def unit_grads(side):
        picked = core == side
        up = [jnp.where(picked, grad_pre[at + pair], grad_pre[at]) for at in range(pair)]
        down = [jnp.where(picked, activated[at + pair], activated[at]) for at in range(pair)]
        return [weight_grad(hidden_two, part).astype(LOW_TYPE) for part in up] + [
            weight_grad(down_low, part).astype(LOW_TYPE) for part in down
        ]

    sent = unit_grads(0)
    if flows:
        flows = [mlp_third(flows[0]), attn_second(flows[1])]
        sent, flows = tied(sent, flows)
    mlp_sums = core_summed(sent, unit_grads(1))
    grad_hidden_two = sum(
        product_t(part, mlp_now[0][unit_at]) for unit_at, part in enumerate(grad_pre)
    )
    grad_middle = grad_out + normalize_back(
        grad_hidden_two * (1.0 + mod_parts[4]), normed_two, inverse_two
    )
    grad_gate_one = jnp.sum(grad_middle * branch_one, 1)
    upward = grad_middle * mod_parts[2]
    up_low, mlp_sums = tied(upward.astype(LOW_TYPE), mlp_sums)
    grad_attended = product(up_low, attn_now[3]).astype(LOW_TYPE)
    grad_queries, grad_keys, grad_values = attend_back(
        queries, key_rows, values, log_total, grad_attended
    )
    if flows:
        flows = [homeward(flows[0]), attn_third(flows[1])]
        grad_queries, flows = tied(grad_queries, flows)

    def map_grads(side):
        both = jnp.concatenate([half_of(grad_queries, 2, side), half_of(grad_keys, 2, side)], 2)
        return [
            weight_grad(hidden_one, both).astype(LOW_TYPE),
            weight_grad(hidden_one, half_of(grad_values, 2, side)).astype(LOW_TYPE),
            weight_grad(up_low, half_of(attended, 2, side)).astype(LOW_TYPE),
        ]

    attn_sums = core_summed(map_grads(1 - core), map_grads(core))
    grad_hidden_one = (
        product_t(grad_queries, attn_now[0])
        + product_t(grad_keys, attn_now[1])
        + product_t(grad_values, attn_now[2])
    )
    grad_stream = grad_middle + normalize_back(
        grad_hidden_one * (1.0 + mod_parts[1]), normed_one, inverse_one
    )
    grad_modulation = jnp.concatenate(
        [
            jnp.sum(grad_hidden_one, 1),
            jnp.sum(grad_hidden_one * normed_one, 1),
            grad_gate_one,
            jnp.sum(grad_hidden_two, 1),
            jnp.sum(grad_hidden_two * normed_two, 1),
            grad_gate_two,
        ],
        axis=1,
    ).astype(LOW_TYPE)
    bias_grad = jnp.concatenate(
        [
            jnp.sum(grad_queries.astype(jnp.float32), (0, 1)),
            jnp.sum(grad_values.astype(jnp.float32), (0, 1)),
            jnp.sum(upward, (0, 1)),
        ]
        + [jnp.sum(part.astype(jnp.float32), (0, 1)) for part in grad_pre]
        + [jnp.sum(downward, (0, 1))]
    )
    return (grad_stream, [mlp_sums, attn_sums], flows, grad_modulation, bias_grad)


def own_latents(value):
    shards = lax.axis_size("tensor")
    low_bit, shard_at = (lax.axis_index("dp") & 1, lax.axis_index("tensor"))
    count = value.shape[0] // shards
    base = (shard_at & 1) * 2
    mine = lax.dynamic_slice_in_dim(value, (base + low_bit) * count, count, 0)
    theirs = lax.dynamic_slice_in_dim(value, (base + 1 - low_bit) * count, count, 0)
    received = flipped(theirs, (shards, shards))
    return jnp.where(shard_at >> 1 == low_bit, mine, received)


def natural_order(gathered, stretches):
    shaped = gathered.reshape((stretches, 2, 2, 2, 2) + gathered.shape[1:])
    moved = jnp.moveaxis(shaped, 2, 4)
    return moved.reshape((-1,) + gathered.shape[2:])


def split_bits(array_in, axis_at, count_bits):
    dims_in = array_in.shape
    return array_in.reshape(
        dims_in[:axis_at]
        + (2,) * count_bits
        + (dims_in[axis_at] >> count_bits,)
        + dims_in[axis_at + 1 :]
    )


def reduce_pieces(arrays, axes_at, shift_bits, count_bits, bit_order, across):
    dp_at = lax.axis_index("dp")
    blocks = [
        split_bits(array_in, axis_at, count_bits) for array_in, axis_at in zip(arrays, axes_at)
    ]
    for bit_at in bit_order:
        own_bit = dp_at >> shift_bits + bit_at & 1
        kept_half = [
            lax.dynamic_slice_in_dim(block_in, own_bit, 1, axis_at + count_bits - 1 - bit_at)
            for block_in, axis_at in zip(blocks, axes_at)
        ]
        sent_half = [
            lax.dynamic_slice_in_dim(block_in, 1 - own_bit, 1, axis_at + count_bits - 1 - bit_at)
            for block_in, axis_at in zip(blocks, axes_at)
        ]
        if across:
            received = swapped(
                (
                    shortened(sent_half[0]),
                    shortened(sent_half[1]),
                    shortened(sent_half[2]),
                    shortened(sent_half[3]),
                ),
                "dp",
                shift_bits + bit_at,
            )
        else:
            received = swapped(
                (
                    shortened(sent_half[0]),
                    shortened(sent_half[1]),
                    shortened(sent_half[2]),
                    shortened(sent_half[3]),
                ),
                "dp",
                shift_bits + bit_at,
            )
        blocks = [own_part + other_part for own_part, other_part in zip(kept_half, received)]
    return [
        block_in.reshape(
            array_in.shape[:axis_at]
            + (array_in.shape[axis_at] >> count_bits,)
            + array_in.shape[axis_at + 1 :]
        )
        for block_in, array_in, axis_at in zip(blocks, arrays, axes_at)
    ]


def adam_update(gradient, first_old, second_old):
    first_new = BETA_FIRST * first_old + (1.0 - BETA_FIRST) * gradient
    second_new = BETA_SECOND * second_old + (1.0 - BETA_SECOND) * gradient * gradient
    update = (
        first_new
        / (1.0 - BETA_FIRST**STEP_COUNT)
        / (jnp.sqrt(second_new / (1.0 - BETA_SECOND**STEP_COUNT)) + ADAM_EPSILON)
    )
    return (update, first_new, second_new)


def per_device(
    patches,
    noise_draw,
    timesteps,
    labels,
    w_attn,
    w_mlp,
    w_mod,
    w_embed,
    biases,
    momentum_attn,
    momentum_mlp,
    momentum_mod,
    momentum_embed,
    momentum_bias,
    first_attn,
    second_attn,
    first_mlp,
    second_mlp,
    first_mod,
    second_mod,
    first_embed,
    second_embed,
    first_bias,
    second_bias,
):
    shards = lax.axis_size("tensor")
    shard_at = lax.axis_index("tensor")
    dp_count = lax.axis_size("dp")
    dp_at = lax.axis_index("dp")
    group_at = dp_at % GROUPS
    stretches = dp_count // GROUPS
    stretch = dp_at // GROUPS
    layer_span = LB * D
    col_width = w_attn.shape[3]
    row_width = w_attn.shape[2]
    mod_width = w_mod.shape[2]
    latents = dp_count * patches.shape[0]
    everyone = ("tensor", "dp")

    stamps, marks = lax.all_gather(jnp.stack([timesteps, labels]), "dp", axis=1, tiled=True)
    embed_low = w_embed.astype(LOW_TYPE)
    conditioners = NCLS + FREQ + D + PATCH_IN
    first_map = embed_low[NCLS : NCLS + FREQ]
    second_map = embed_low[NCLS + FREQ : NCLS + FREQ + D]

    def attn_local(layer_at):
        return jnp.transpose(w_attn[layer_at], (1, 0, 2)).reshape(1, row_width, 4 * col_width)

    def attn_whole(gathered):
        shaped = gathered.reshape(shards, D, 4, col_width)
        return jnp.transpose(shaped, (2, 1, 0, 3)).reshape(4, D, D)

    first_local = [attn_local(layer_at) for layer_at in range(L)] + list(w_mlp[: L - 1])
    first_local = jnp.concatenate(
        [part.astype(LOW_TYPE).reshape(-1, row_width, 4 * col_width) for part in first_local]
    )
    first_whole = lax.all_gather(first_local, everyone, axis=1, tiled=True)
    last_whole = lax.all_gather(w_mlp[L - 1].astype(LOW_TYPE), everyone, axis=1, tiled=True)
    attn_all = [attn_whole(first_whole[layer_at]) for layer_at in range(L)]
    units_whole = first_whole.reshape(-1, shards, D, 4 * col_width)
    mlp_all = [
        [[units_whole[L + 2 * layer_at + kind, at] for at in range(shards)] for kind in range(2)]
        for layer_at in range(L - 1)
    ]
    last_whole = last_whole.reshape(2, shards, D, -1)
    mlp_all.append([[last_whole[kind, at] for at in range(shards)] for kind in range(2)])

    bias_flat = biases.reshape(-1)
    bias_tail = bias_flat[L * layer_span :]
    freq_low = frequencies(stamps).astype(LOW_TYPE)

    def own_columns(vector):
        return lax.dynamic_slice_in_dim(vector, dp_at * row_width, row_width, 0)

    hidden_cols = product(freq_low, first_map) + own_columns(bias_tail[D : 2 * D])
    gathered_cols = lax.all_gather(
        jnp.concatenate(
            [
                hidden_cols,
                w_embed[conditioners - PATCH_IN : conditioners],
                w_embed[-PATCH_IN:],
            ]
        ),
        "dp",
        axis=1,
        tiled=True,
    )
    hidden_time = gathered_cols[:latents]
    patch_map = gathered_cols[latents : latents + PATCH_IN].astype(LOW_TYPE)
    head_map = gathered_cols[latents + PATCH_IN :].astype(LOW_TYPE)
    smooth_time = jax.nn.silu(hidden_time).astype(LOW_TYPE)
    class_picks = (marks[:, None] == jnp.arange(NCLS, dtype=jnp.int32)[None, :]).astype(LOW_TYPE)
    condition_rows = (
        product(smooth_time, second_map)
        + own_columns(bias_tail[2 * D : 3 * D])
        + product(class_picks, embed_low[:NCLS])
    )
    cond_rows = jax.nn.silu(condition_rows).astype(LOW_TYPE)
    mod_low = w_mod.astype(LOW_TYPE)
    final_low = embed_low[conditioners:-PATCH_IN]
    final_width = final_low.shape[0] // shards
    mod_cols = jnp.concatenate(
        [product(cond_rows, mod_low[layer_at]) for layer_at in range(L)]
        + [
            product_t(
                cond_rows, lax.dynamic_slice_in_dim(final_low, shard_at * final_width, final_width, 0)
            )
        ],
        axis=1,
    )
    mod_cols = lax.psum_scatter(mod_cols, "dp", scatter_dimension=0, tiled=True)
    mod_all = own_latents(
        jnp.swapaxes(lax.all_gather(mod_cols.astype(LOW_TYPE), "tensor"), 0, 1)
    ).astype(jnp.float32)
    mod_parts = []
    for layer_at in range(L):
        modulation = (
            mod_all[:, :, layer_at * mod_width : (layer_at + 1) * mod_width].reshape(-1, 6 * D)
            + bias_flat[layer_at * layer_span + 4 * D + FF : (layer_at + 1) * layer_span]
        )
        mod_parts.append(
            [modulation[:, None, part_at * D : (part_at + 1) * D] for part_at in range(6)]
        )
    final_mod = mod_all[:, :, L * mod_width :].reshape(-1, 2 * D) + bias_tail[3 * D : 5 * D]

    patches_own, noise_own = (own_latents(patches), own_latents(noise_draw))
    signal = own_latents(signal_levels(timesteps)[:, None])[:, :, None]
    noised = (jnp.sqrt(signal) * patches_own + jnp.sqrt(1.0 - signal) * noise_own).astype(LOW_TYPE)
    stream = product(noised, patch_map) + bias_tail[:D] + positions()
    saved_states = []
    for layer_at in range(L):
        stream, kept_state = layer_forward(
            stream,
            mod_parts[layer_at],
            attn_all[layer_at],
            mlp_all[layer_at],
            bias_flat[layer_at * layer_span : (layer_at + 1) * layer_span],
        )
        saved_states.append(kept_state)
    normed_last, inverse_last = normalize(stream)
    hidden_last = (normed_last * (1.0 + final_mod[:, None, D:]) + final_mod[:, None, :D]).astype(
        LOW_TYPE
    )
    predicted = product_t(hidden_last, head_map)
    errors = predicted - noise_own
    elements = dp_count // GROUPS * patches.shape[0] * S * PATCH_IN
    loss_here = jnp.sum(errors * errors) / elements
    grad_pred = (2.0 * errors / elements).astype(LOW_TYPE)
    grad_head = weight_grad(grad_pred, hidden_last)
    grad_hidden = product(grad_pred, head_map)
    grad_final = jnp.concatenate(
        [jnp.sum(grad_hidden, 1), jnp.sum(grad_hidden * normed_last, 1)], axis=1
    ).astype(LOW_TYPE)
    grad_stream = normalize_back(
        grad_hidden * (1.0 + final_mod[:, None, D:]), normed_last, inverse_last
    )
    mod_list, bias_list, sums_list, flows = ([None] * L, [None] * L, [None] * L, None)
    late, grad_stream = tied(jnp.concatenate([second_map, cond_rows]), grad_stream)
    late = lax.all_gather(late, "dp", axis=1, tiled=True)
    second_time, cond_act = (late[:D], late[D:])
    for layer_at in range(L - 1, -1, -1):
        grad_stream, fresh, flows, mod_list[layer_at], bias_list[layer_at] = layer_backward(
            grad_stream,
            mod_parts[layer_at],
            attn_all[layer_at],
            mlp_all[layer_at],
            saved_states[layer_at],
            flows,
        )
        if flows:
            sums_list[layer_at + 1] = [flows[0], homeward(flows[1])]
        flows = fresh
    sums_list[0] = [
        homeward(mlp_third(mlp_second(flows[0]))),
        homeward(attn_third(attn_second(flows[1]))),
    ]
    grad_patch = weight_grad(noised, grad_stream.astype(LOW_TYPE))
    mine = patches_own.shape[0]
    vectors = jnp.concatenate(
        [grad_now.reshape(-1) for grad_now in mod_list]
        + [grad_final.reshape(-1)]
        + [grad_now.astype(LOW_TYPE) for grad_now in bias_list]
        + [
            jnp.sum(grad_stream, (0, 1)).astype(LOW_TYPE),
            grad_patch.astype(LOW_TYPE).reshape(-1),
            grad_head.astype(LOW_TYPE).reshape(-1),
        ]
    )
    gathered = lax.all_gather(vectors, ("dp", "tensor"))
    devices = dp_count * shards
    offset = 0

    def taken(width):
        nonlocal offset
        offset += width
        return gathered[:, offset - width : offset]

    grad_mods = [
        natural_order(taken(mine * 6 * D).reshape(devices, mine, 6 * D), stretches)
        for layer_at in range(L)
    ]
    grad_finals = natural_order(taken(mine * 2 * D).reshape(devices, mine, 2 * D), stretches)

    def group_sums(part):
        shaped = part.astype(jnp.float32).reshape(stretches, 2, 2, 2, shards // 2, -1)
        return jnp.sum(shaped, (0, 2, 4)).reshape(GROUPS, -1)

    layer_bias = 7 * D + FF - 3 * D
    bias_sums = [group_sums(taken(layer_bias)) for layer_at in range(L)]
    patch_bias = group_sums(taken(D))
    patch_sums = group_sums(taken(PATCH_IN * D)).reshape(GROUPS, PATCH_IN, D)
    head_sums = group_sums(taken(PATCH_IN * D)).reshape(GROUPS, PATCH_IN, D)

    own_mods = [
        lax.dynamic_slice_in_dim(grad_now, shard_at * mod_width, mod_width, 1)
        for grad_now in grad_mods
    ]
    grad_cond_parts = sum(
        product_t(own_mods[layer_at], mod_low[layer_at]) for layer_at in range(L)
    )
    grad_cond_act = jnp.sum(
        lax.all_gather(grad_cond_parts.astype(LOW_TYPE), "tensor").astype(jnp.float32), 0
    ) + product(grad_finals, final_low)
    grad_condition = lax.all_gather(
        jax.vjp(jax.nn.silu, condition_rows)[1](grad_cond_act)[0].astype(LOW_TYPE),
        "dp",
        axis=1,
        tiled=True,
    )
    grad_smooth = product_t(grad_condition, second_time)
    grad_hidden_time = jax.vjp(jax.nn.silu, hidden_time)[1](grad_smooth)[0].astype(LOW_TYPE)

    def of_group(value):
        shaped = value.reshape((stretches, GROUPS, latents // dp_count) + value.shape[1:])
        return picked_at(shaped, group_at, 1).reshape((-1,) + value.shape[1:])

    def of_stretch(value):
        width = value.shape[-1] // stretches
        return lax.dynamic_slice_in_dim(value, stretch * width, width, value.ndim - 1)

    def latent_sums(value):
        shaped = value.astype(jnp.float32).reshape(stretches, GROUPS, latents // dp_count, -1)
        return jnp.sum(shaped, (0, 2))

    grad_condition_own = of_stretch(of_group(grad_condition))
    cond_own = of_stretch(of_group(cond_act))
    grad_embed = jnp.concatenate(
        [
            weight_grad(of_group(class_picks), grad_condition_own),
            weight_grad(of_group(freq_low), of_stretch(of_group(grad_hidden_time))),
            weight_grad(of_group(smooth_time), grad_condition_own),
            of_stretch(picked_at(patch_sums, group_at, 0)),
            weight_grad(of_group(grad_finals), cond_own),
            of_stretch(picked_at(head_sums, group_at, 0)),
        ],
        0,
    )
    grad_mod_map = jnp.stack([weight_grad(cond_own, of_group(grad_now)) for grad_now in own_mods])
    bias_groups = jnp.concatenate(
        [
            part
            for layer_at in range(L)
            for part in (bias_sums[layer_at], latent_sums(grad_mods[layer_at]))
        ]
        + [
            patch_bias,
            latent_sums(grad_hidden_time),
            latent_sums(grad_condition),
            latent_sums(grad_finals),
        ],
        axis=1,
    )
    attn_now = jnp.stack(
        [
            jnp.stack(
                [part[:, at * col_width : (at + 1) * col_width] for part in sums[1] for at in (0, 1)]
            )
            for sums in sums_list
        ]
    ).astype(jnp.float32)
    mlp_now = jnp.stack([jnp.stack(sums[0]) for sums in sums_list]).astype(jnp.float32)
    reduced = [attn_now, mlp_now, grad_mod_map, grad_embed]
    squares = (
        jnp.sum(reduced[0] * reduced[0])
        + jnp.sum(reduced[1] * reduced[1])
        + jnp.sum(reduced[2] * reduced[2])
        + jnp.sum(reduced[3] * reduced[3]) / shards
    )
    picked = (jnp.arange(GROUPS, dtype=jnp.int32) == group_at).astype(jnp.float32)
    totals = jnp.sum(
        lax.all_gather(
            jnp.concatenate([picked * squares, jnp.reshape(loss_here, (1,))]), ("dp", "tensor")
        ),
        0,
    )
    group_norms = jnp.sqrt(totals[:GROUPS] + jnp.sum(bias_groups * bias_groups, 1))
    clip_scale = CLIP_NORM / (group_norms + 1e-06)
    own_scale = jnp.sum(picked * clip_scale)
    shift_group = GROUPS.bit_length() - 1
    weights_in = (w_attn, w_mlp, w_mod, w_embed)
    momenta_in = (momentum_attn, momentum_mlp, momentum_mod, momentum_embed)
    firsts_in = (first_attn, first_mlp, first_mod, first_embed)
    seconds_in = (second_attn, second_mlp, second_mod, second_embed)
    updates, new_firsts, new_seconds = ([], [], [])
    for index_at in range(4):
        update, first_new, second_new = adam_update(
            reduced[index_at] * own_scale, firsts_in[index_at], seconds_in[index_at]
        )
        updates.append(update)
        new_firsts.append(first_new)
        new_seconds.append(second_new)
    summed = reduce_pieces(updates, (2, 2, 1, 1), 0, shift_group, list(range(shift_group)), True)
    new_weights, new_momenta = ([], [])
    for index_at in range(4):
        outer_grad = LEARN_RATE * (summed[index_at] / GROUPS + WEIGHT_DECAY * weights_in[index_at])
        momentum_new = OUTER_MOMENTUM * momenta_in[index_at] + outer_grad
        new_weights.append(
            weights_in[index_at] - OUTER_RATE * (outer_grad + OUTER_MOMENTUM * momentum_new)
        )
        new_momenta.append(momentum_new)
    clipped_bias = bias_groups * clip_scale[:, None]
    bias_updates, bias_first, bias_second = adam_update(
        clipped_bias, first_bias.reshape(GROUPS, -1), second_bias.reshape(GROUPS, -1)
    )
    outer_bias = LEARN_RATE * (jnp.mean(bias_updates, 0) + WEIGHT_DECAY * bias_flat)
    bias_momentum = OUTER_MOMENTUM * momentum_bias.reshape(-1) + outer_bias
    bias_new = bias_flat - OUTER_RATE * (outer_bias + OUTER_MOMENTUM * bias_momentum)
    return (
        totals[GROUPS] / GROUPS,
        group_norms,
        clipped_bias.reshape(first_bias.shape),
        new_weights[0],
        new_weights[1],
        new_weights[2],
        new_weights[3],
        bias_new.reshape(biases.shape),
        new_momenta[0],
        new_momenta[1],
        new_momenta[2],
        new_momenta[3],
        bias_momentum.reshape(biases.shape),
        new_firsts[0],
        new_seconds[0],
        new_firsts[1],
        new_seconds[1],
        new_firsts[2],
        new_seconds[2],
        new_firsts[3],
        new_seconds[3],
        bias_first.reshape(first_bias.shape),
        bias_second.reshape(second_bias.shape),
    )


def solution(mesh):
    placed = (
        P("dp", None, None),
        P("dp", None, None),
        P("dp"),
        P("dp"),
        P(None, None, "dp", "tensor"),
        P(None, None, "dp", "tensor"),
        P(None, "dp", "tensor"),
        P(None, "dp"),
        P(),
        P(None, None, "dp", "tensor"),
        P(None, None, "dp", "tensor"),
        P(None, "dp", "tensor"),
        P(None, "dp"),
        P(),
        P(None, None, "dp", "tensor"),
        P(None, None, "dp", "tensor"),
        P(None, None, "dp", "tensor"),
        P(None, None, "dp", "tensor"),
        P(None, "dp", "tensor"),
        P(None, "dp", "tensor"),
        P(None, "dp"),
        P(None, "dp"),
        P(),
        P(),
    )
    return jax.shard_map(
        per_device,
        mesh=mesh,
        in_specs=placed,
        out_specs=(
            P(),
            P(),
            P(),
            P(None, None, "dp", "tensor"),
            P(None, None, "dp", "tensor"),
            P(None, "dp", "tensor"),
            P(None, "dp"),
            P(),
            P(None, None, "dp", "tensor"),
            P(None, None, "dp", "tensor"),
            P(None, "dp", "tensor"),
            P(None, "dp"),
            P(),
            P(None, None, "dp", "tensor"),
            P(None, None, "dp", "tensor"),
            P(None, None, "dp", "tensor"),
            P(None, None, "dp", "tensor"),
            P(None, "dp", "tensor"),
            P(None, "dp", "tensor"),
            P(None, "dp"),
            P(None, "dp"),
            P(),
            P(),
        ),
        check_vma=False,
    )
```

```python
import jax
import jax.numpy as jnp
from jax import lax
from jax.experimental import pallas as pl
from jax.sharding import PartitionSpec as P

D = 768
HD = 64
FF = 3072
NCLS = 1000
FREQ = 256
PATCH_IN = 16
SIDE = 16
L = 2
GROUPS = 4
STEP_COUNT = 10
NSTEPS = 1000
S = 256
LB = 14


LOW_TYPE = jnp.bfloat16
LEARN_RATE = 0.03
WEIGHT_DECAY = 0.1
BETA_FIRST = 0.9
BETA_SECOND = 0.95
ADAM_EPSILON = 1e-08
CLIP_NORM = 0.02
OUTER_RATE = 0.7
OUTER_MOMENTUM = 0.9


def shortened(shard):
    return jax.tree.map(lambda a: a.astype(jnp.bfloat16) if a.dtype == jnp.float32 else a, shard)


def swapped(value, axis, bit):
    mask = 2**bit
    pairs = [(source, source ^ mask) for source in range(lax.axis_size(axis))]
    return lax.ppermute(value, axis, pairs)


def product(left, right):
    return jnp.dot(left, right, preferred_element_type=jnp.float32)


def product_t(left, right):
    return lax.dot_general(
        left, right, (((left.ndim - 1,), (1,)), ((), ())), preferred_element_type=jnp.float32
    )


def weight_grad(inputs, grads_out):
    leading = tuple(range(inputs.ndim - 1))
    return lax.dot_general(
        inputs, grads_out, ((leading, leading), ((), ())), preferred_element_type=jnp.float32
    )


def normalize(values):
    centred = values - jnp.mean(values, -1, keepdims=True)
    inverse = lax.rsqrt(jnp.mean(centred * centred, -1, keepdims=True) + 1e-06)
    return (centred * inverse, inverse)


def normalize_back(grad_in, normed, inverse):
    return inverse * (
        grad_in
        - jnp.mean(grad_in, -1, keepdims=True)
        - normed * jnp.mean(grad_in * normed, -1, keepdims=True)
    )


def gelu_tanh(values):
    return jax.nn.gelu(values, approximate=True)


def positions():
    quarter = D // 4
    omegas = 1.0 / 10000.0 ** (jnp.arange(quarter, dtype=jnp.float32) / quarter)
    places = jnp.arange(S, dtype=jnp.int32)
    across = (places % SIDE).astype(jnp.float32)[:, None] * omegas[None, :]
    downward = (places // SIDE).astype(jnp.float32)[:, None] * omegas[None, :]
    return jnp.concatenate(
        [jnp.sin(across), jnp.cos(across), jnp.sin(downward), jnp.cos(downward)], axis=1
    )


def frequencies(stamps):
    half_width = FREQ // 2
    freq_rates = jnp.exp(-jnp.log(10000.0) * jnp.arange(half_width, dtype=jnp.float32) / half_width)
    angles = stamps.astype(jnp.float32)[:, None] * freq_rates[None, :]
    return jnp.concatenate([jnp.cos(angles), jnp.sin(angles)], axis=1)


def signal_levels(stamps):
    noise_rates = jnp.linspace(0.0001, 0.02, NSTEPS, dtype=jnp.float32)
    kept_share = jnp.cumprod(1.0 - noise_rates)
    matches = stamps[:, None] == jnp.arange(NSTEPS, dtype=jnp.int32)[None, :]
    return jnp.sum(jnp.where(matches, kept_share[None, :], 0.0), axis=1)


def embed_parts(matrix):
    bounds = [
        NCLS,
        NCLS + FREQ,
        NCLS + FREQ + D,
        NCLS + FREQ + D + PATCH_IN,
        NCLS + FREQ + 3 * D + PATCH_IN,
    ]
    return (
        matrix[: bounds[0]],
        matrix[bounds[0] : bounds[1]],
        matrix[bounds[1] : bounds[2]],
        matrix[bounds[2] : bounds[3]],
        matrix[bounds[3] : bounds[4]],
        matrix[bounds[4] :],
    )


def split_heads(array_in):
    return array_in.reshape(array_in.shape[:2] + (array_in.shape[2] // HD, HD))


def head_scores(queries, key_rows):
    return jnp.einsum(
        "nqhd,nkhd->nhqk",
        split_heads(queries),
        split_heads(key_rows),
        preferred_element_type=jnp.float32,
    ) * HD ** (-0.5)


def attend(queries, key_rows, values):
    scores = head_scores(queries, key_rows)
    highest = jnp.max(scores, -1, keepdims=True)
    log_total = highest + jnp.log(jnp.sum(jnp.exp(scores - highest), -1, keepdims=True))
    weights = jnp.exp(scores - log_total).astype(LOW_TYPE)
    output = jnp.einsum(
        "nhqk,nkhd->nqhd", weights, split_heads(values), preferred_element_type=jnp.float32
    )
    return (output.reshape(queries.shape), log_total)


def attend_back(queries, key_rows, values, log_total, grad_out):
    weights = jnp.exp(head_scores(queries, key_rows) - log_total)
    grad_heads = split_heads(grad_out)
    grad_values = jnp.einsum(
        "nhqk,nqhd->nkhd", weights.astype(LOW_TYPE), grad_heads, preferred_element_type=jnp.float32
    )
    grad_weights = jnp.einsum(
        "nqhd,nkhd->nhqk", grad_heads, split_heads(values), preferred_element_type=jnp.float32
    )
    grad_scores = (
        weights * (grad_weights - jnp.sum(weights * grad_weights, -1, keepdims=True))
    ).astype(LOW_TYPE)
    grad_queries = jnp.einsum(
        "nhqk,nkhd->nqhd", grad_scores, split_heads(key_rows), preferred_element_type=jnp.float32
    ) * HD ** (-0.5)
    grad_keys = jnp.einsum(
        "nhqk,nqhd->nkhd", grad_scores, split_heads(queries), preferred_element_type=jnp.float32
    ) * HD ** (-0.5)
    return (
        grad_queries.reshape(queries.shape).astype(LOW_TYPE),
        grad_keys.reshape(queries.shape).astype(LOW_TYPE),
        grad_values.reshape(queries.shape).astype(LOW_TYPE),
    )


def place(vector_all, piece_in, offset):
    return lax.dynamic_update_slice_in_dim(vector_all, piece_in, offset, 0)


def flipped(value, masks):
    shards = lax.axis_size("tensor")
    count = lax.axis_size("dp") * shards
    pairs = [(source, source ^ masks[source // shards & 1]) for source in range(count)]
    return lax.ppermute(value, ("dp", "tensor"), pairs)


def picked_at(value, index_at, axis):
    return lax.dynamic_index_in_dim(value, index_at, axis, keepdims=False)


def layer_forward(stream, mod_parts, attn_now, mlp_now, bias_layer):
    width_all = stream.shape[-1]
    normed_one, inverse_one = normalize(stream)
    hidden_one = (normed_one * (1.0 + mod_parts[1]) + mod_parts[0]).astype(LOW_TYPE)
    queries = (product(hidden_one, attn_now[0]) + bias_layer[:width_all]).astype(LOW_TYPE)
    key_rows = product(hidden_one, attn_now[1]).astype(LOW_TYPE)
    values = (product(hidden_one, attn_now[2]) + bias_layer[width_all : 2 * width_all]).astype(
        LOW_TYPE
    )
    attended, log_total = attend(queries, key_rows, values)
    attended = attended.astype(LOW_TYPE)
    branch_one = product_t(attended, attn_now[3]) + bias_layer[2 * width_all : 3 * width_all]
    middle = stream + mod_parts[2] * branch_one
    normed_two, inverse_two = normalize(middle)
    hidden_two = (normed_two * (1.0 + mod_parts[4]) + mod_parts[3]).astype(LOW_TYPE)
    unit_width = mlp_now[0][0].shape[-1]
    before = [
        product(hidden_two, mlp_now[0][unit_at])
        + bias_layer[3 * width_all + unit_at * unit_width : 3 * width_all + (unit_at + 1) * unit_width]
        for unit_at in range(len(mlp_now[0]))
    ]
    activated = [gelu_tanh(part).astype(LOW_TYPE) for part in before]
    branch_two = bias_layer[3 * width_all + FF : 4 * width_all + FF] + sum(
        product_t(part, mlp_now[1][unit_at]) for unit_at, part in enumerate(activated)
    )
    result = middle + mod_parts[5] * branch_two
    kept_state = (
        normed_one,
        inverse_one,
        hidden_one,
        queries,
        key_rows,
        values,
        log_total,
        attended,
        branch_one,
        normed_two,
        inverse_two,
        hidden_two,
        before,
        activated,
        branch_two,
    )
    return (result, kept_state)


def exchanged(value, mask):
    count = lax.axis_size("dp") * lax.axis_size("tensor")
    return lax.ppermute(value, ("dp", "tensor"), [(source, source ^ mask) for source in range(count)])


def half_of(value, axis, bit):
    width = value.shape[axis] // 2
    return lax.dynamic_slice_in_dim(value, bit * width, width, axis)


def summed_low(left, right):
    return (left.astype(jnp.float32) + right.astype(jnp.float32)).astype(LOW_TYPE)


def rows_halved(value):
    stretch = lax.axis_index("dp") // GROUPS
    stretches = lax.axis_size("dp") // GROUPS
    for bit_at in reversed(range(stretches.bit_length() - 1)):
        bit = stretch >> bit_at & 1
        received = exchanged(
            half_of(value, 0, 1 - bit), lax.axis_size("tensor") * GROUPS << bit_at
        )
        value = summed_low(half_of(value, 0, bit), received)
    return value


def columns_halved(sent, kept):
    return summed_low(kept, exchanged(sent, 1))


def unit_halved(first, second):
    picked = (lax.axis_index("tensor") & 1) == 1
    return columns_halved(jnp.where(picked, first, second), jnp.where(picked, second, first))


def pair_halved(first, second):
    bit = lax.axis_index("tensor") & 1

    def halves(bit_now):
        return jnp.concatenate([half_of(first, 1, bit_now), half_of(second, 1, bit_now)], 1)

    return columns_halved(halves(1 - bit), halves(bit))


def core_summed(sent, kept):
    return [
        summed_low(own, exchanged(other, lax.axis_size("tensor"))) for other, own in zip(sent, kept)
    ]


def homeward(values):
    shards = lax.axis_size("tensor")
    pairs = []
    for source in range(lax.axis_size("dp") * shards):
        core, high = (source // shards & 1, source % shards >> 1)
        pairs.append((source, source ^ (core ^ high) * (shards + shards // 2)))
    return [lax.ppermute(value, ("dp", "tensor"), pairs) for value in values]


def mlp_second(totals):
    up_zero, up_one, down_zero, down_one = totals
    return [rows_halved(up_zero), rows_halved(up_one), unit_halved(down_zero, down_one)]


def mlp_third(totals):
    up_zero, up_one, down = totals
    return [unit_halved(up_zero, up_one), rows_halved(down)]


def attn_second(totals):
    query_key, value_map, out_map = totals
    return [rows_halved(query_key), pair_halved(value_map, out_map)]


def attn_third(totals):
    query_key, value_out = totals
    width = query_key.shape[1] // 2
    return [pair_halved(query_key[:, :width], query_key[:, width:]), rows_halved(value_out)]


def attn_maps(gathered, layer_at):
    shards, rows_all, width_all = gathered.shape[1:]
    width, rows = (width_all // 4, rows_all // 4)

    def kernel(gathered_ref, maps_ref):
        for kind in range(4):
            maps_ref[kind] = jnp.concatenate(
                [
                    gathered_ref[0, shard][:, kind * width : (kind + 1) * width]
                    for shard in range(shards)
                ],
                axis=1,
            )

    return pl.pallas_call(
        kernel,
        grid=(4,),
        in_specs=[
            pl.BlockSpec((1, shards, rows, width_all), lambda at: (layer_at, 0, at, 0)),
        ],
        out_specs=pl.BlockSpec((4, rows, shards * width), lambda at: (0, at, 0)),
        out_shape=jax.ShapeDtypeStruct((4, rows_all, shards * width), gathered.dtype),
        name="attn_maps",
    )(gathered)


def tied(value, flows):
    return lax.optimization_barrier((value, flows))


def layer_backward(grad_out, mod_parts, attn_now, mlp_now, kept_state, flows):
    (
        normed_one,
        inverse_one,
        hidden_one,
        queries,
        key_rows,
        values,
        log_total,
        attended,
        branch_one,
        normed_two,
        inverse_two,
        hidden_two,
        saved_pre,
        activated,
        branch_two,
    ) = kept_state
    core = lax.axis_index("dp") & 1
    pair = len(activated) // 2
    if flows:
        flows = [mlp_second(flows[0]), flows[1]]
        grad_out, flows = tied(grad_out, flows)
    grad_gate_two = jnp.sum(grad_out * branch_two, 1)
    downward = grad_out * mod_parts[5]
    down_low = downward.astype(LOW_TYPE)
    grad_pre = [
        jax.vjp(gelu_tanh, part)[1](product(down_low, mlp_now[1][unit_at]))[0].astype(LOW_TYPE)
        for unit_at, part in enumerate(saved_pre)
    ]

    def unit_grads(side):
        picked = core == side
        up = [jnp.where(picked, grad_pre[at + pair], grad_pre[at]) for at in range(pair)]
        down = [jnp.where(picked, activated[at + pair], activated[at]) for at in range(pair)]
        return [weight_grad(hidden_two, part).astype(LOW_TYPE) for part in up] + [
            weight_grad(down_low, part).astype(LOW_TYPE) for part in down
        ]

    sent = unit_grads(0)
    if flows:
        flows = [mlp_third(flows[0]), attn_second(flows[1])]
        sent, flows = tied(sent, flows)
    mlp_sums = core_summed(sent, unit_grads(1))
    grad_hidden_two = sum(
        product_t(part, mlp_now[0][unit_at]) for unit_at, part in enumerate(grad_pre)
    )
    grad_middle = grad_out + normalize_back(
        grad_hidden_two * (1.0 + mod_parts[4]), normed_two, inverse_two
    )
    grad_gate_one = jnp.sum(grad_middle * branch_one, 1)
    upward = grad_middle * mod_parts[2]
    up_low, mlp_sums = tied(upward.astype(LOW_TYPE), mlp_sums)
    grad_attended = product(up_low, attn_now[3]).astype(LOW_TYPE)
    grad_queries, grad_keys, grad_values = attend_back(
        queries, key_rows, values, log_total, grad_attended
    )
    if flows:
        flows = [homeward(flows[0]), attn_third(flows[1])]
        grad_queries, flows = tied(grad_queries, flows)

    def map_grads(side):
        both = jnp.concatenate([half_of(grad_queries, 2, side), half_of(grad_keys, 2, side)], 2)
        return [
            weight_grad(hidden_one, both).astype(LOW_TYPE),
            weight_grad(hidden_one, half_of(grad_values, 2, side)).astype(LOW_TYPE),
            weight_grad(up_low, half_of(attended, 2, side)).astype(LOW_TYPE),
        ]

    attn_sums = core_summed(map_grads(1 - core), map_grads(core))
    grad_hidden_one = (
        product_t(grad_queries, attn_now[0])
        + product_t(grad_keys, attn_now[1])
        + product_t(grad_values, attn_now[2])
    )
    grad_stream = grad_middle + normalize_back(
        grad_hidden_one * (1.0 + mod_parts[1]), normed_one, inverse_one
    )
    grad_modulation = jnp.concatenate(
        [
            jnp.sum(grad_hidden_one, 1),
            jnp.sum(grad_hidden_one * normed_one, 1),
            grad_gate_one,
            jnp.sum(grad_hidden_two, 1),
            jnp.sum(grad_hidden_two * normed_two, 1),
            grad_gate_two,
        ],
        axis=1,
    ).astype(LOW_TYPE)
    bias_grad = jnp.concatenate(
        [
            jnp.sum(grad_queries.astype(jnp.float32), (0, 1)),
            jnp.sum(grad_values.astype(jnp.float32), (0, 1)),
            jnp.sum(upward, (0, 1)),
        ]
        + [jnp.sum(part.astype(jnp.float32), (0, 1)) for part in grad_pre]
        + [jnp.sum(downward, (0, 1))]
    )
    return (grad_stream, [mlp_sums, attn_sums], flows, grad_modulation, bias_grad)


def own_latents(value):
    shards = lax.axis_size("tensor")
    low_bit, shard_at = (lax.axis_index("dp") & 1, lax.axis_index("tensor"))
    count = value.shape[0] // shards
    base = (shard_at & 1) * 2
    mine = lax.dynamic_slice_in_dim(value, (base + low_bit) * count, count, 0)
    theirs = lax.dynamic_slice_in_dim(value, (base + 1 - low_bit) * count, count, 0)
    received = flipped(theirs, (shards, shards))
    return jnp.where(shard_at >> 1 == low_bit, mine, received)


def natural_order(gathered, stretches):
    shaped = gathered.reshape((stretches, 2, 2, 2, 2) + gathered.shape[1:])
    moved = jnp.moveaxis(shaped, 2, 4)
    return moved.reshape((-1,) + gathered.shape[2:])


def split_bits(array_in, axis_at, count_bits):
    dims_in = array_in.shape
    return array_in.reshape(
        dims_in[:axis_at]
        + (2,) * count_bits
        + (dims_in[axis_at] >> count_bits,)
        + dims_in[axis_at + 1 :]
    )


def group_step(block, axis_at, count_bits, bit_at):
    own_bit = lax.axis_index("dp") >> bit_at & 1
    at = axis_at + count_bits - 1 - bit_at
    sent = shortened(lax.dynamic_slice_in_dim(block, 1 - own_bit, 1, at))
    return lax.dynamic_slice_in_dim(block, own_bit, 1, at) + swapped(sent, "dp", bit_at)


def adam_update(gradient, first_old, second_old):
    first_new = BETA_FIRST * first_old + (1.0 - BETA_FIRST) * gradient
    second_new = BETA_SECOND * second_old + (1.0 - BETA_SECOND) * gradient * gradient
    update = (
        first_new
        / (1.0 - BETA_FIRST**STEP_COUNT)
        / (jnp.sqrt(second_new / (1.0 - BETA_SECOND**STEP_COUNT)) + ADAM_EPSILON)
    )
    return (update, first_new, second_new)


def per_device(
    patches,
    noise_draw,
    timesteps,
    labels,
    w_attn,
    w_mlp,
    w_mod,
    w_embed,
    biases,
    momentum_attn,
    momentum_mlp,
    momentum_mod,
    momentum_embed,
    momentum_bias,
    first_attn,
    second_attn,
    first_mlp,
    second_mlp,
    first_mod,
    second_mod,
    first_embed,
    second_embed,
    first_bias,
    second_bias,
):
    shards = lax.axis_size("tensor")
    shard_at = lax.axis_index("tensor")
    dp_count = lax.axis_size("dp")
    dp_at = lax.axis_index("dp")
    group_at = dp_at % GROUPS
    stretches = dp_count // GROUPS
    stretch = dp_at // GROUPS
    layer_span = LB * D
    col_width = w_attn.shape[3]
    row_width = w_attn.shape[2]
    mod_width = w_mod.shape[2]
    latents = dp_count * patches.shape[0]
    everyone = ("tensor", "dp")

    stamps, marks = lax.all_gather(jnp.stack([timesteps, labels]), "dp", axis=1, tiled=True)
    embed_low = w_embed.astype(LOW_TYPE)
    conditioners = NCLS + FREQ + D + PATCH_IN
    first_map = embed_low[NCLS : NCLS + FREQ]
    second_map = embed_low[NCLS + FREQ : NCLS + FREQ + D]

    def attn_local(layer_at):
        return jnp.transpose(w_attn[layer_at], (1, 0, 2)).reshape(1, row_width, 4 * col_width)

    first_local = [attn_local(layer_at) for layer_at in range(L)] + list(w_mlp[: L - 1])
    first_local = jnp.concatenate(
        [part.astype(LOW_TYPE).reshape(-1, row_width, 4 * col_width) for part in first_local]
    )
    first_whole = lax.all_gather(first_local, everyone, axis=1, tiled=True)
    last_whole = lax.all_gather(w_mlp[L - 1].astype(LOW_TYPE), everyone, axis=1, tiled=True)
    units_whole = first_whole.reshape(-1, shards, D, 4 * col_width)
    attn_all = [attn_maps(units_whole, layer_at) for layer_at in range(L)]
    mlp_all = [
        [[units_whole[L + 2 * layer_at + kind, at] for at in range(shards)] for kind in range(2)]
        for layer_at in range(L - 1)
    ]
    last_whole = last_whole.reshape(2, shards, D, -1)
    mlp_all.append([[last_whole[kind, at] for at in range(shards)] for kind in range(2)])

    bias_flat = biases.reshape(-1)
    bias_tail = bias_flat[L * layer_span :]
    freq_low = frequencies(stamps).astype(LOW_TYPE)

    def own_columns(vector):
        return lax.dynamic_slice_in_dim(vector, dp_at * row_width, row_width, 0)

    hidden_cols = product(freq_low, first_map) + own_columns(bias_tail[D : 2 * D])
    gathered_cols = lax.all_gather(
        jnp.concatenate(
            [
                hidden_cols,
                w_embed[conditioners - PATCH_IN : conditioners],
                w_embed[-PATCH_IN:],
            ]
        ),
        "dp",
        axis=1,
        tiled=True,
    )
    hidden_time = gathered_cols[:latents]
    patch_map = gathered_cols[latents : latents + PATCH_IN].astype(LOW_TYPE)
    head_map = gathered_cols[latents + PATCH_IN :].astype(LOW_TYPE)
    smooth_time = jax.nn.silu(hidden_time).astype(LOW_TYPE)
    class_picks = (marks[:, None] == jnp.arange(NCLS, dtype=jnp.int32)[None, :]).astype(LOW_TYPE)
    condition_rows = (
        product(smooth_time, second_map)
        + own_columns(bias_tail[2 * D : 3 * D])
        + product(class_picks, embed_low[:NCLS])
    )
    cond_rows = jax.nn.silu(condition_rows).astype(LOW_TYPE)
    mod_low = w_mod.astype(LOW_TYPE)
    final_low = embed_low[conditioners:-PATCH_IN]
    final_width = final_low.shape[0] // shards
    mod_cols = jnp.concatenate(
        [product(cond_rows, mod_low[layer_at]) for layer_at in range(L)]
        + [
            product_t(
                cond_rows, lax.dynamic_slice_in_dim(final_low, shard_at * final_width, final_width, 0)
            )
        ],
        axis=1,
    )
    mod_cols = lax.psum_scatter(mod_cols, "dp", scatter_dimension=0, tiled=True)
    mod_all = own_latents(
        jnp.swapaxes(lax.all_gather(mod_cols.astype(LOW_TYPE), "tensor"), 0, 1)
    ).astype(jnp.float32)
    mod_parts = []
    for layer_at in range(L):
        modulation = (
            mod_all[:, :, layer_at * mod_width : (layer_at + 1) * mod_width].reshape(-1, 6 * D)
            + bias_flat[layer_at * layer_span + 4 * D + FF : (layer_at + 1) * layer_span]
        )
        mod_parts.append(
            [modulation[:, None, part_at * D : (part_at + 1) * D] for part_at in range(6)]
        )
    final_mod = mod_all[:, :, L * mod_width :].reshape(-1, 2 * D) + bias_tail[3 * D : 5 * D]

    patches_own, noise_own = (own_latents(patches), own_latents(noise_draw))
    signal = own_latents(signal_levels(timesteps)[:, None])[:, :, None]
    noised = (jnp.sqrt(signal) * patches_own + jnp.sqrt(1.0 - signal) * noise_own).astype(LOW_TYPE)
    stream = product(noised, patch_map) + bias_tail[:D] + positions()
    saved_states = []
    for layer_at in range(L):
        stream, kept_state = layer_forward(
            stream,
            mod_parts[layer_at],
            attn_all[layer_at],
            mlp_all[layer_at],
            bias_flat[layer_at * layer_span : (layer_at + 1) * layer_span],
        )
        saved_states.append(kept_state)
    normed_last, inverse_last = normalize(stream)
    hidden_last = (normed_last * (1.0 + final_mod[:, None, D:]) + final_mod[:, None, :D]).astype(
        LOW_TYPE
    )
    predicted = product_t(hidden_last, head_map)
    errors = predicted - noise_own
    elements = dp_count // GROUPS * patches.shape[0] * S * PATCH_IN
    loss_here = jnp.sum(errors * errors) / elements
    grad_pred = (2.0 * errors / elements).astype(LOW_TYPE)
    grad_head = weight_grad(grad_pred, hidden_last)
    grad_hidden = product(grad_pred, head_map)
    grad_final = jnp.concatenate(
        [jnp.sum(grad_hidden, 1), jnp.sum(grad_hidden * normed_last, 1)], axis=1
    ).astype(LOW_TYPE)
    grad_stream = normalize_back(
        grad_hidden * (1.0 + final_mod[:, None, D:]), normed_last, inverse_last
    )
    mod_list, bias_list, sums_list, flows = ([None] * L, [None] * L, [None] * L, None)
    late, grad_stream = tied(jnp.concatenate([second_map, cond_rows]), grad_stream)
    late = lax.all_gather(late, "dp", axis=1, tiled=True)
    second_time, cond_act = (late[:D], late[D:])
    for layer_at in range(L - 1, -1, -1):
        grad_stream, fresh, flows, mod_list[layer_at], bias_list[layer_at] = layer_backward(
            grad_stream,
            mod_parts[layer_at],
            attn_all[layer_at],
            mlp_all[layer_at],
            saved_states[layer_at],
            flows,
        )
        if flows:
            sums_list[layer_at + 1] = [flows[0], homeward(flows[1])]
        flows = fresh
    last_mlp = homeward(mlp_third(mlp_second(flows[0])))
    last_attn = attn_third(attn_second(flows[1]))
    grad_patch = weight_grad(noised, grad_stream.astype(LOW_TYPE))
    mine = patches_own.shape[0]
    early = jnp.concatenate(
        [grad_now.reshape(-1) for grad_now in mod_list[1:]]
        + [grad_final.reshape(-1)]
        + [grad_now.astype(LOW_TYPE) for grad_now in bias_list[1:]]
        + [grad_head.astype(LOW_TYPE).reshape(-1)]
    )
    late_part = jnp.concatenate(
        [
            mod_list[0].reshape(-1),
            bias_list[0].astype(LOW_TYPE),
            jnp.sum(grad_stream, (0, 1)).astype(LOW_TYPE),
            grad_patch.astype(LOW_TYPE).reshape(-1),
        ]
    )
    devices = dp_count * shards

    def cutter(vectors):
        gathered = lax.all_gather(vectors, ("dp", "tensor"))
        offset = 0

        def taken(width):
            nonlocal offset
            offset += width
            return gathered[:, offset - width : offset]

        return taken

    take_early, take_late = (cutter(early), cutter(late_part))
    takers = [take_late] + [take_early] * (L - 1)
    grad_mods = [
        natural_order(taker(mine * 6 * D).reshape(devices, mine, 6 * D), stretches)
        for taker in takers
    ]
    grad_finals = natural_order(take_early(mine * 2 * D).reshape(devices, mine, 2 * D), stretches)

    def group_sums(part):
        shaped = part.astype(jnp.float32).reshape(stretches, 2, 2, 2, shards // 2, -1)
        return jnp.sum(shaped, (0, 2, 4)).reshape(GROUPS, -1)

    layer_bias = 7 * D + FF - 3 * D
    bias_sums = [group_sums(taker(layer_bias)) for taker in takers]
    patch_bias = group_sums(take_late(D))
    patch_sums = group_sums(take_late(PATCH_IN * D)).reshape(GROUPS, PATCH_IN, D)
    head_sums = group_sums(take_early(PATCH_IN * D)).reshape(GROUPS, PATCH_IN, D)

    own_mods = [
        lax.dynamic_slice_in_dim(grad_now, shard_at * mod_width, mod_width, 1)
        for grad_now in grad_mods
    ]
    grad_cond_parts = sum(
        product_t(own_mods[layer_at], mod_low[layer_at]) for layer_at in range(L)
    )
    grad_cond_act = jnp.sum(
        lax.all_gather(grad_cond_parts.astype(LOW_TYPE), "tensor").astype(jnp.float32), 0
    ) + product(grad_finals, final_low)
    grad_condition = lax.all_gather(
        jax.vjp(jax.nn.silu, condition_rows)[1](grad_cond_act)[0].astype(LOW_TYPE),
        "dp",
        axis=1,
        tiled=True,
    )
    grad_smooth = product_t(grad_condition, second_time)
    grad_hidden_time = jax.vjp(jax.nn.silu, hidden_time)[1](grad_smooth)[0].astype(LOW_TYPE)

    def of_group(value):
        shaped = value.reshape((stretches, GROUPS, latents // dp_count) + value.shape[1:])
        return picked_at(shaped, group_at, 1).reshape((-1,) + value.shape[1:])

    def of_stretch(value):
        width = value.shape[-1] // stretches
        return lax.dynamic_slice_in_dim(value, stretch * width, width, value.ndim - 1)

    def latent_sums(value):
        shaped = value.astype(jnp.float32).reshape(stretches, GROUPS, latents // dp_count, -1)
        return jnp.sum(shaped, (0, 2))

    grad_condition_own = of_stretch(of_group(grad_condition))
    cond_own = of_stretch(of_group(cond_act))
    grad_embed = jnp.concatenate(
        [
            weight_grad(of_group(class_picks), grad_condition_own),
            weight_grad(of_group(freq_low), of_stretch(of_group(grad_hidden_time))),
            weight_grad(of_group(smooth_time), grad_condition_own),
            of_stretch(picked_at(patch_sums, group_at, 0)),
            weight_grad(of_group(grad_finals), cond_own),
            of_stretch(picked_at(head_sums, group_at, 0)),
        ],
        0,
    )
    grad_mod_map = jnp.stack([weight_grad(cond_own, of_group(grad_now)) for grad_now in own_mods])
    bias_groups = jnp.concatenate(
        [
            part
            for layer_at in range(L)
            for part in (bias_sums[layer_at], latent_sums(grad_mods[layer_at]))
        ]
        + [
            patch_bias,
            latent_sums(grad_hidden_time),
            latent_sums(grad_condition),
            latent_sums(grad_finals),
        ],
        axis=1,
    )
    side_squares = jnp.sum(grad_mod_map * grad_mod_map) + jnp.sum(grad_embed * grad_embed) / shards
    bias_squares = jnp.sum(bias_groups * bias_groups, 1)
    last_attn, (side_squares, bias_squares) = tied(last_attn, (side_squares, bias_squares))
    sums_list[0] = [last_mlp, homeward(last_attn)]
    attn_now = jnp.stack(
        [
            jnp.stack(
                [part[:, at * col_width : (at + 1) * col_width] for part in sums[1] for at in (0, 1)]
            )
            for sums in sums_list
        ]
    ).astype(jnp.float32)
    mlp_now = jnp.stack([jnp.stack(sums[0]) for sums in sums_list]).astype(jnp.float32)
    reduced = [attn_now, mlp_now, grad_mod_map, grad_embed]
    squares = (
        jnp.sum(reduced[0] * reduced[0])
        + jnp.sum(reduced[1] * reduced[1])
        + side_squares
    )
    picked = (jnp.arange(GROUPS, dtype=jnp.int32) == group_at).astype(jnp.float32)
    local_totals = jnp.concatenate(
        [picked * squares, jnp.full((GROUPS,), loss_here), jnp.zeros((128 - 2 * GROUPS,))]
    )
    totals = jnp.sum(
        lax.all_gather(
            jnp.broadcast_to(local_totals, (8, 128)), ("dp", "tensor"), axis=0, tiled=True
        ).reshape(-1, 8, 128)[:, 0],
        0,
    )
    group_norms = jnp.sqrt(totals[:GROUPS] + bias_squares)
    clip_scale = CLIP_NORM / (group_norms + 1e-06)
    own_scale = jnp.sum(picked * clip_scale)
    shift_group = GROUPS.bit_length() - 1
    weights_in = (w_attn, w_mlp, w_mod, w_embed)
    momenta_in = (momentum_attn, momentum_mlp, momentum_mod, momentum_embed)
    firsts_in = (first_attn, first_mlp, first_mod, first_embed)
    seconds_in = (second_attn, second_mlp, second_mod, second_embed)
    axes_at = (2, 2, 1, 1)
    steps, new_firsts, new_seconds = ([], [], [])
    for index_at in range(4):
        grad_now = reduced[index_at]
        if index_at >= 2:
            grad_now, steps[index_at - 2] = tied(grad_now, steps[index_at - 2])
        update, first_new, second_new = adam_update(
            grad_now * own_scale, firsts_in[index_at], seconds_in[index_at]
        )
        axis_at = axes_at[index_at]
        steps.append(group_step(split_bits(update, axis_at, shift_group), axis_at, shift_group, 0))
        new_firsts.append(first_new)
        new_seconds.append(second_new)
    summed = []
    for index_at in range(4):
        block = steps[index_at]
        for bit_at in range(1, shift_group):
            block = group_step(block, axes_at[index_at], shift_group, bit_at)
        summed.append(block.reshape(weights_in[index_at].shape))
    new_weights, new_momenta = ([], [])
    for index_at in range(4):
        outer_grad = LEARN_RATE * (summed[index_at] / GROUPS + WEIGHT_DECAY * weights_in[index_at])
        momentum_new = OUTER_MOMENTUM * momenta_in[index_at] + outer_grad
        new_weights.append(
            weights_in[index_at] - OUTER_RATE * (outer_grad + OUTER_MOMENTUM * momentum_new)
        )
        new_momenta.append(momentum_new)
    clipped_bias = bias_groups * clip_scale[:, None]
    bias_updates, bias_first, bias_second = adam_update(
        clipped_bias, first_bias.reshape(GROUPS, -1), second_bias.reshape(GROUPS, -1)
    )
    outer_bias = LEARN_RATE * (jnp.mean(bias_updates, 0) + WEIGHT_DECAY * bias_flat)
    bias_momentum = OUTER_MOMENTUM * momentum_bias.reshape(-1) + outer_bias
    bias_new = bias_flat - OUTER_RATE * (outer_bias + OUTER_MOMENTUM * bias_momentum)
    return (
        totals[GROUPS] / GROUPS,
        group_norms,
        clipped_bias.reshape(first_bias.shape),
        new_weights[0],
        new_weights[1],
        new_weights[2],
        new_weights[3],
        bias_new.reshape(biases.shape),
        new_momenta[0],
        new_momenta[1],
        new_momenta[2],
        new_momenta[3],
        bias_momentum.reshape(biases.shape),
        new_firsts[0],
        new_seconds[0],
        new_firsts[1],
        new_seconds[1],
        new_firsts[2],
        new_seconds[2],
        new_firsts[3],
        new_seconds[3],
        bias_first.reshape(first_bias.shape),
        bias_second.reshape(second_bias.shape),
    )


def solution(mesh):
    placed = (
        P("dp", None, None),
        P("dp", None, None),
        P("dp"),
        P("dp"),
        P(None, None, "dp", "tensor"),
        P(None, None, "dp", "tensor"),
        P(None, "dp", "tensor"),
        P(None, "dp"),
        P(),
        P(None, None, "dp", "tensor"),
        P(None, None, "dp", "tensor"),
        P(None, "dp", "tensor"),
        P(None, "dp"),
        P(),
        P(None, None, "dp", "tensor"),
        P(None, None, "dp", "tensor"),
        P(None, None, "dp", "tensor"),
        P(None, None, "dp", "tensor"),
        P(None, "dp", "tensor"),
        P(None, "dp", "tensor"),
        P(None, "dp"),
        P(None, "dp"),
        P(),
        P(),
    )
    return jax.shard_map(
        per_device,
        mesh=mesh,
        in_specs=placed,
        out_specs=(
            P(),
            P(),
            P(),
            P(None, None, "dp", "tensor"),
            P(None, None, "dp", "tensor"),
            P(None, "dp", "tensor"),
            P(None, "dp"),
            P(),
            P(None, None, "dp", "tensor"),
            P(None, None, "dp", "tensor"),
            P(None, "dp", "tensor"),
            P(None, "dp"),
            P(),
            P(None, None, "dp", "tensor"),
            P(None, None, "dp", "tensor"),
            P(None, None, "dp", "tensor"),
            P(None, None, "dp", "tensor"),
            P(None, "dp", "tensor"),
            P(None, "dp", "tensor"),
            P(None, "dp"),
            P(None, "dp"),
            P(),
            P(),
        ),
        check_vma=False,
    )
```

```python
import jax
import jax.numpy as jnp
from jax import lax
from jax.experimental import pallas as pl
from jax.sharding import PartitionSpec as P

D = 768
HD = 64
FF = 3072
NCLS = 1000
FREQ = 256
PATCH_IN = 16
SIDE = 16
L = 2
GROUPS = 4
STEP_COUNT = 10
NSTEPS = 1000
S = 256
LB = 14


LOW_TYPE = jnp.bfloat16
LEARN_RATE = 0.03
WEIGHT_DECAY = 0.1
BETA_FIRST = 0.9
BETA_SECOND = 0.95
ADAM_EPSILON = 1e-08
CLIP_NORM = 0.02
OUTER_RATE = 0.7
OUTER_MOMENTUM = 0.9


def shortened(shard):
    return jax.tree.map(lambda a: a.astype(jnp.bfloat16) if a.dtype == jnp.float32 else a, shard)


def swapped(value, axis, bit):
    mask = 2**bit
    pairs = [(source, source ^ mask) for source in range(lax.axis_size(axis))]
    return lax.ppermute(value, axis, pairs)


def product(left, right):
    return jnp.dot(left, right, preferred_element_type=jnp.float32)


def product_t(left, right):
    return lax.dot_general(
        left, right, (((left.ndim - 1,), (1,)), ((), ())), preferred_element_type=jnp.float32
    )


def weight_grad(inputs, grads_out):
    leading = tuple(range(inputs.ndim - 1))
    return lax.dot_general(
        inputs, grads_out, ((leading, leading), ((), ())), preferred_element_type=jnp.float32
    )


def normalize(values):
    centred = values - jnp.mean(values, -1, keepdims=True)
    inverse = lax.rsqrt(jnp.mean(centred * centred, -1, keepdims=True) + 1e-06)
    return (centred * inverse, inverse)


def normalize_back(grad_in, normed, inverse):
    return inverse * (
        grad_in
        - jnp.mean(grad_in, -1, keepdims=True)
        - normed * jnp.mean(grad_in * normed, -1, keepdims=True)
    )


def gelu_tanh(values):
    return jax.nn.gelu(values, approximate=True)


def positions():
    quarter = D // 4
    omegas = 1.0 / 10000.0 ** (jnp.arange(quarter, dtype=jnp.float32) / quarter)
    places = jnp.arange(S, dtype=jnp.int32)
    across = (places % SIDE).astype(jnp.float32)[:, None] * omegas[None, :]
    downward = (places // SIDE).astype(jnp.float32)[:, None] * omegas[None, :]
    return jnp.concatenate(
        [jnp.sin(across), jnp.cos(across), jnp.sin(downward), jnp.cos(downward)], axis=1
    )


def frequencies(stamps):
    half_width = FREQ // 2
    freq_rates = jnp.exp(-jnp.log(10000.0) * jnp.arange(half_width, dtype=jnp.float32) / half_width)
    angles = stamps.astype(jnp.float32)[:, None] * freq_rates[None, :]
    return jnp.concatenate([jnp.cos(angles), jnp.sin(angles)], axis=1)


def signal_levels(stamps):
    noise_rates = jnp.linspace(0.0001, 0.02, NSTEPS, dtype=jnp.float32)
    kept_share = jnp.cumprod(1.0 - noise_rates)
    matches = stamps[:, None] == jnp.arange(NSTEPS, dtype=jnp.int32)[None, :]
    return jnp.sum(jnp.where(matches, kept_share[None, :], 0.0), axis=1)


def embed_parts(matrix):
    bounds = [
        NCLS,
        NCLS + FREQ,
        NCLS + FREQ + D,
        NCLS + FREQ + D + PATCH_IN,
        NCLS + FREQ + 3 * D + PATCH_IN,
    ]
    return (
        matrix[: bounds[0]],
        matrix[bounds[0] : bounds[1]],
        matrix[bounds[1] : bounds[2]],
        matrix[bounds[2] : bounds[3]],
        matrix[bounds[3] : bounds[4]],
        matrix[bounds[4] :],
    )


def split_heads(array_in):
    return array_in.reshape(array_in.shape[:2] + (array_in.shape[2] // HD, HD))


def head_scores(queries, key_rows):
    return jnp.einsum(
        "nqhd,nkhd->nhqk",
        split_heads(queries),
        split_heads(key_rows),
        preferred_element_type=jnp.float32,
    ) * HD ** (-0.5)


def attend(queries, key_rows, values):
    scores = head_scores(queries, key_rows)
    highest = jnp.max(scores, -1, keepdims=True)
    log_total = highest + jnp.log(jnp.sum(jnp.exp(scores - highest), -1, keepdims=True))
    weights = jnp.exp(scores - log_total).astype(LOW_TYPE)
    output = jnp.einsum(
        "nhqk,nkhd->nqhd", weights, split_heads(values), preferred_element_type=jnp.float32
    )
    return (output.reshape(queries.shape), log_total)


def attend_back(queries, key_rows, values, log_total, grad_out):
    weights = jnp.exp(head_scores(queries, key_rows) - log_total)
    grad_heads = split_heads(grad_out)
    grad_values = jnp.einsum(
        "nhqk,nqhd->nkhd", weights.astype(LOW_TYPE), grad_heads, preferred_element_type=jnp.float32
    )
    grad_weights = jnp.einsum(
        "nqhd,nkhd->nhqk", grad_heads, split_heads(values), preferred_element_type=jnp.float32
    )
    grad_scores = (
        weights * (grad_weights - jnp.sum(weights * grad_weights, -1, keepdims=True))
    ).astype(LOW_TYPE)
    grad_queries = jnp.einsum(
        "nhqk,nkhd->nqhd", grad_scores, split_heads(key_rows), preferred_element_type=jnp.float32
    ) * HD ** (-0.5)
    grad_keys = jnp.einsum(
        "nhqk,nqhd->nkhd", grad_scores, split_heads(queries), preferred_element_type=jnp.float32
    ) * HD ** (-0.5)
    return (
        grad_queries.reshape(queries.shape).astype(LOW_TYPE),
        grad_keys.reshape(queries.shape).astype(LOW_TYPE),
        grad_values.reshape(queries.shape).astype(LOW_TYPE),
    )


def place(vector_all, piece_in, offset):
    return lax.dynamic_update_slice_in_dim(vector_all, piece_in, offset, 0)


def flipped(value, masks):
    shards = lax.axis_size("tensor")
    count = lax.axis_size("dp") * shards
    pairs = [(source, source ^ masks[source // shards & 1]) for source in range(count)]
    return lax.ppermute(value, ("dp", "tensor"), pairs)


def picked_at(value, index_at, axis):
    return lax.dynamic_index_in_dim(value, index_at, axis, keepdims=False)


def layer_forward(stream, mod_parts, attn_now, mlp_now, bias_layer):
    width_all = stream.shape[-1]
    normed_one, inverse_one = normalize(stream)
    hidden_one = (normed_one * (1.0 + mod_parts[1]) + mod_parts[0]).astype(LOW_TYPE)
    queries = (product(hidden_one, attn_now[0]) + bias_layer[:width_all]).astype(LOW_TYPE)
    key_rows = product(hidden_one, attn_now[1]).astype(LOW_TYPE)
    values = (product(hidden_one, attn_now[2]) + bias_layer[width_all : 2 * width_all]).astype(
        LOW_TYPE
    )
    attended, log_total = attend(queries, key_rows, values)
    attended = attended.astype(LOW_TYPE)
    branch_one = product_t(attended, attn_now[3]) + bias_layer[2 * width_all : 3 * width_all]
    middle = stream + mod_parts[2] * branch_one
    normed_two, inverse_two = normalize(middle)
    hidden_two = (normed_two * (1.0 + mod_parts[4]) + mod_parts[3]).astype(LOW_TYPE)
    unit_width = mlp_now[0][0].shape[-1]
    before = [
        product(hidden_two, mlp_now[0][unit_at])
        + bias_layer[3 * width_all + unit_at * unit_width : 3 * width_all + (unit_at + 1) * unit_width]
        for unit_at in range(len(mlp_now[0]))
    ]
    activated = [gelu_tanh(part).astype(LOW_TYPE) for part in before]
    branch_two = bias_layer[3 * width_all + FF : 4 * width_all + FF] + sum(
        product_t(part, mlp_now[1][unit_at]) for unit_at, part in enumerate(activated)
    )
    result = middle + mod_parts[5] * branch_two
    kept_state = (
        normed_one,
        inverse_one,
        hidden_one,
        queries,
        key_rows,
        values,
        log_total,
        attended,
        branch_one,
        normed_two,
        inverse_two,
        hidden_two,
        before,
        activated,
        branch_two,
    )
    return (result, kept_state)


def exchanged(value, mask):
    count = lax.axis_size("dp") * lax.axis_size("tensor")
    return lax.ppermute(value, ("dp", "tensor"), [(source, source ^ mask) for source in range(count)])


def half_of(value, axis, bit):
    width = value.shape[axis] // 2
    return lax.dynamic_slice_in_dim(value, bit * width, width, axis)


def summed_low(left, right):
    return (left.astype(jnp.float32) + right.astype(jnp.float32)).astype(LOW_TYPE)


def rows_halved(value):
    stretch = lax.axis_index("dp") // GROUPS
    stretches = lax.axis_size("dp") // GROUPS
    for bit_at in reversed(range(stretches.bit_length() - 1)):
        bit = stretch >> bit_at & 1
        received = exchanged(
            half_of(value, 0, 1 - bit), lax.axis_size("tensor") * GROUPS << bit_at
        )
        value = summed_low(half_of(value, 0, bit), received)
    return value


def columns_halved(sent, kept):
    return summed_low(kept, exchanged(sent, 1))


def unit_halved(first, second):
    picked = (lax.axis_index("tensor") & 1) == 1
    return columns_halved(jnp.where(picked, first, second), jnp.where(picked, second, first))


def pair_halved(first, second):
    bit = lax.axis_index("tensor") & 1

    def halves(bit_now):
        return jnp.concatenate([half_of(first, 1, bit_now), half_of(second, 1, bit_now)], 1)

    return columns_halved(halves(1 - bit), halves(bit))


def core_summed(sent, kept):
    return [
        summed_low(own, exchanged(other, lax.axis_size("tensor"))) for other, own in zip(sent, kept)
    ]


def homeward(values):
    shards = lax.axis_size("tensor")
    pairs = []
    for source in range(lax.axis_size("dp") * shards):
        core, high = (source // shards & 1, source % shards >> 1)
        pairs.append((source, source ^ (core ^ high) * (shards + shards // 2)))
    return [lax.ppermute(value, ("dp", "tensor"), pairs) for value in values]


def squared(values):
    return sum(jnp.sum(jnp.square(value.astype(jnp.float32))) for value in values)


def mlp_second(totals):
    up_zero, up_one, down_zero, down_one = totals
    return [rows_halved(up_zero), rows_halved(up_one), unit_halved(down_zero, down_one)]


def mlp_third(totals):
    up_zero, up_one, down = totals
    return [unit_halved(up_zero, up_one), rows_halved(down)]


def attn_second(totals):
    query_key, value_map, out_map = totals
    return [rows_halved(query_key), pair_halved(value_map, out_map)]


def attn_third(totals):
    query_key, value_out = totals
    width = query_key.shape[1] // 2
    return [pair_halved(query_key[:, :width], query_key[:, width:]), rows_halved(value_out)]


def attn_maps(gathered, layer_at):
    shards, rows_all, width_all = gathered.shape[1:]
    width, rows = (width_all // 4, rows_all // 4)

    def kernel(gathered_ref, maps_ref):
        for kind in range(4):
            maps_ref[kind] = jnp.concatenate(
                [
                    gathered_ref[0, shard][:, kind * width : (kind + 1) * width]
                    for shard in range(shards)
                ],
                axis=1,
            )

    return pl.pallas_call(
        kernel,
        grid=(4,),
        in_specs=[
            pl.BlockSpec((1, shards, rows, width_all), lambda at: (layer_at, 0, at, 0)),
        ],
        out_specs=pl.BlockSpec((4, rows, shards * width), lambda at: (0, at, 0)),
        out_shape=jax.ShapeDtypeStruct((4, rows_all, shards * width), gathered.dtype),
        name="attn_maps",
    )(gathered)


def tied(value, flows):
    return lax.optimization_barrier((value, flows))


def layer_backward(grad_out, mod_parts, attn_now, mlp_now, kept_state, flows):
    (
        normed_one,
        inverse_one,
        hidden_one,
        queries,
        key_rows,
        values,
        log_total,
        attended,
        branch_one,
        normed_two,
        inverse_two,
        hidden_two,
        saved_pre,
        activated,
        branch_two,
    ) = kept_state
    core = lax.axis_index("dp") & 1
    pair = len(activated) // 2
    if flows:
        flows = [mlp_second(flows[0]), flows[1]]
        grad_out, flows = tied(grad_out, flows)
    grad_gate_two = jnp.sum(grad_out * branch_two, 1)
    downward = grad_out * mod_parts[5]
    down_low = downward.astype(LOW_TYPE)
    grad_pre = [
        jax.vjp(gelu_tanh, part)[1](product(down_low, mlp_now[1][unit_at]))[0].astype(LOW_TYPE)
        for unit_at, part in enumerate(saved_pre)
    ]

    def unit_grads(side):
        picked = core == side
        up = [jnp.where(picked, grad_pre[at + pair], grad_pre[at]) for at in range(pair)]
        down = [jnp.where(picked, activated[at + pair], activated[at]) for at in range(pair)]
        return [weight_grad(hidden_two, part).astype(LOW_TYPE) for part in up] + [
            weight_grad(down_low, part).astype(LOW_TYPE) for part in down
        ]

    sent = unit_grads(0)
    if flows:
        flows = [mlp_third(flows[0]), attn_second(flows[1])]
        sent, flows = tied(sent, flows)
    mlp_sums = core_summed(sent, unit_grads(1))
    grad_hidden_two = sum(
        product_t(part, mlp_now[0][unit_at]) for unit_at, part in enumerate(grad_pre)
    )
    grad_middle = grad_out + normalize_back(
        grad_hidden_two * (1.0 + mod_parts[4]), normed_two, inverse_two
    )
    grad_gate_one = jnp.sum(grad_middle * branch_one, 1)
    upward = grad_middle * mod_parts[2]
    up_low, mlp_sums = tied(upward.astype(LOW_TYPE), mlp_sums)
    grad_attended = product(up_low, attn_now[3]).astype(LOW_TYPE)
    grad_queries, grad_keys, grad_values = attend_back(
        queries, key_rows, values, log_total, grad_attended
    )
    if flows:
        flows = [homeward(flows[0]), attn_third(flows[1]), squared(flows[0])]
        grad_queries, flows = tied(grad_queries, flows)

    def map_grads(side):
        both = jnp.concatenate([half_of(grad_queries, 2, side), half_of(grad_keys, 2, side)], 2)
        return [
            weight_grad(hidden_one, both).astype(LOW_TYPE),
            weight_grad(hidden_one, half_of(grad_values, 2, side)).astype(LOW_TYPE),
            weight_grad(up_low, half_of(attended, 2, side)).astype(LOW_TYPE),
        ]

    attn_sums = core_summed(map_grads(1 - core), map_grads(core))
    grad_hidden_one = (
        product_t(grad_queries, attn_now[0])
        + product_t(grad_keys, attn_now[1])
        + product_t(grad_values, attn_now[2])
    )
    grad_stream = grad_middle + normalize_back(
        grad_hidden_one * (1.0 + mod_parts[1]), normed_one, inverse_one
    )
    grad_modulation = jnp.concatenate(
        [
            jnp.sum(grad_hidden_one, 1),
            jnp.sum(grad_hidden_one * normed_one, 1),
            grad_gate_one,
            jnp.sum(grad_hidden_two, 1),
            jnp.sum(grad_hidden_two * normed_two, 1),
            grad_gate_two,
        ],
        axis=1,
    ).astype(LOW_TYPE)
    bias_grad = jnp.concatenate(
        [
            jnp.sum(grad_queries.astype(jnp.float32), (0, 1)),
            jnp.sum(grad_values.astype(jnp.float32), (0, 1)),
            jnp.sum(upward, (0, 1)),
        ]
        + [jnp.sum(part.astype(jnp.float32), (0, 1)) for part in grad_pre]
        + [jnp.sum(downward, (0, 1))]
    )
    return (grad_stream, [mlp_sums, attn_sums], flows, grad_modulation, bias_grad)


def own_latents(value):
    shards = lax.axis_size("tensor")
    low_bit, shard_at = (lax.axis_index("dp") & 1, lax.axis_index("tensor"))
    count = value.shape[0] // shards
    base = (shard_at & 1) * 2
    mine = lax.dynamic_slice_in_dim(value, (base + low_bit) * count, count, 0)
    theirs = lax.dynamic_slice_in_dim(value, (base + 1 - low_bit) * count, count, 0)
    received = flipped(theirs, (shards, shards))
    return jnp.where(shard_at >> 1 == low_bit, mine, received)


def natural_order(gathered, stretches):
    shaped = gathered.reshape((stretches, 2, 2, 2, 2) + gathered.shape[1:])
    moved = jnp.moveaxis(shaped, 2, 4)
    return moved.reshape((-1,) + gathered.shape[2:])


def split_bits(array_in, axis_at, count_bits):
    dims_in = array_in.shape
    return array_in.reshape(
        dims_in[:axis_at]
        + (2,) * count_bits
        + (dims_in[axis_at] >> count_bits,)
        + dims_in[axis_at + 1 :]
    )


def group_step(block, axis_at, count_bits, bit_at):
    own_bit = lax.axis_index("dp") >> bit_at & 1
    at = axis_at + count_bits - 1 - bit_at
    sent = shortened(lax.dynamic_slice_in_dim(block, 1 - own_bit, 1, at))
    return lax.dynamic_slice_in_dim(block, own_bit, 1, at) + swapped(sent, "dp", bit_at)


def adam_update(gradient, first_old, second_old):
    first_new = BETA_FIRST * first_old + (1.0 - BETA_FIRST) * gradient
    second_new = BETA_SECOND * second_old + (1.0 - BETA_SECOND) * gradient * gradient
    update = (
        first_new
        / (1.0 - BETA_FIRST**STEP_COUNT)
        / (jnp.sqrt(second_new / (1.0 - BETA_SECOND**STEP_COUNT)) + ADAM_EPSILON)
    )
    return (update, first_new, second_new)


def per_device(
    patches,
    noise_draw,
    timesteps,
    labels,
    w_attn,
    w_mlp,
    w_mod,
    w_embed,
    biases,
    momentum_attn,
    momentum_mlp,
    momentum_mod,
    momentum_embed,
    momentum_bias,
    first_attn,
    second_attn,
    first_mlp,
    second_mlp,
    first_mod,
    second_mod,
    first_embed,
    second_embed,
    first_bias,
    second_bias,
):
    shards = lax.axis_size("tensor")
    shard_at = lax.axis_index("tensor")
    dp_count = lax.axis_size("dp")
    dp_at = lax.axis_index("dp")
    group_at = dp_at % GROUPS
    stretches = dp_count // GROUPS
    stretch = dp_at // GROUPS
    layer_span = LB * D
    col_width = w_attn.shape[3]
    row_width = w_attn.shape[2]
    mod_width = w_mod.shape[2]
    latents = dp_count * patches.shape[0]
    everyone = ("tensor", "dp")

    stamps, marks = lax.all_gather(jnp.stack([timesteps, labels]), "dp", axis=1, tiled=True)
    embed_low = w_embed.astype(LOW_TYPE)
    conditioners = NCLS + FREQ + D + PATCH_IN
    first_map = embed_low[NCLS : NCLS + FREQ]
    second_map = embed_low[NCLS + FREQ : NCLS + FREQ + D]

    def attn_local(layer_at):
        return jnp.transpose(w_attn[layer_at], (1, 0, 2)).reshape(1, row_width, 4 * col_width)

    first_local = [attn_local(layer_at) for layer_at in range(L)] + list(w_mlp[: L - 1])
    first_local = jnp.concatenate(
        [part.astype(LOW_TYPE).reshape(-1, row_width, 4 * col_width) for part in first_local]
    )
    first_whole = lax.all_gather(first_local, everyone, axis=1, tiled=True)
    last_whole = lax.all_gather(w_mlp[L - 1].astype(LOW_TYPE), everyone, axis=1, tiled=True)
    units_whole = first_whole.reshape(-1, shards, D, 4 * col_width)
    attn_all = [attn_maps(units_whole, layer_at) for layer_at in range(L)]
    mlp_all = [
        [[units_whole[L + 2 * layer_at + kind, at] for at in range(shards)] for kind in range(2)]
        for layer_at in range(L - 1)
    ]
    last_whole = last_whole.reshape(2, shards, D, -1)
    mlp_all.append([[last_whole[kind, at] for at in range(shards)] for kind in range(2)])

    bias_flat = biases.reshape(-1)
    bias_tail = bias_flat[L * layer_span :]
    freq_low = frequencies(stamps).astype(LOW_TYPE)

    def own_columns(vector):
        return lax.dynamic_slice_in_dim(vector, dp_at * row_width, row_width, 0)

    hidden_cols = product(freq_low, first_map) + own_columns(bias_tail[D : 2 * D])
    gathered_cols = lax.all_gather(
        jnp.concatenate(
            [
                hidden_cols,
                w_embed[conditioners - PATCH_IN : conditioners],
                w_embed[-PATCH_IN:],
            ]
        ),
        "dp",
        axis=1,
        tiled=True,
    )
    hidden_time = gathered_cols[:latents]
    patch_map = gathered_cols[latents : latents + PATCH_IN].astype(LOW_TYPE)
    head_map = gathered_cols[latents + PATCH_IN :].astype(LOW_TYPE)
    smooth_time = jax.nn.silu(hidden_time).astype(LOW_TYPE)
    class_picks = (marks[:, None] == jnp.arange(NCLS, dtype=jnp.int32)[None, :]).astype(LOW_TYPE)
    condition_rows = (
        product(smooth_time, second_map)
        + own_columns(bias_tail[2 * D : 3 * D])
        + product(class_picks, embed_low[:NCLS])
    )
    cond_rows = jax.nn.silu(condition_rows).astype(LOW_TYPE)
    mod_low = w_mod.astype(LOW_TYPE)
    final_low = embed_low[conditioners:-PATCH_IN]
    final_width = final_low.shape[0] // shards
    mod_cols = jnp.concatenate(
        [product(cond_rows, mod_low[layer_at]) for layer_at in range(L)]
        + [
            product_t(
                cond_rows, lax.dynamic_slice_in_dim(final_low, shard_at * final_width, final_width, 0)
            )
        ],
        axis=1,
    )
    mod_cols = lax.psum_scatter(mod_cols, "dp", scatter_dimension=0, tiled=True)
    mod_all = own_latents(
        jnp.swapaxes(lax.all_gather(mod_cols.astype(LOW_TYPE), "tensor"), 0, 1)
    ).astype(jnp.float32)
    mod_parts = []
    for layer_at in range(L):
        modulation = (
            mod_all[:, :, layer_at * mod_width : (layer_at + 1) * mod_width].reshape(-1, 6 * D)
            + bias_flat[layer_at * layer_span + 4 * D + FF : (layer_at + 1) * layer_span]
        )
        mod_parts.append(
            [modulation[:, None, part_at * D : (part_at + 1) * D] for part_at in range(6)]
        )
    final_mod = mod_all[:, :, L * mod_width :].reshape(-1, 2 * D) + bias_tail[3 * D : 5 * D]

    patches_own, noise_own = (own_latents(patches), own_latents(noise_draw))
    signal = own_latents(signal_levels(timesteps)[:, None])[:, :, None]
    noised = (jnp.sqrt(signal) * patches_own + jnp.sqrt(1.0 - signal) * noise_own).astype(LOW_TYPE)
    stream = product(noised, patch_map) + bias_tail[:D] + positions()
    saved_states = []
    for layer_at in range(L):
        stream, kept_state = layer_forward(
            stream,
            mod_parts[layer_at],
            attn_all[layer_at],
            mlp_all[layer_at],
            bias_flat[layer_at * layer_span : (layer_at + 1) * layer_span],
        )
        saved_states.append(kept_state)
    normed_last, inverse_last = normalize(stream)
    hidden_last = (normed_last * (1.0 + final_mod[:, None, D:]) + final_mod[:, None, :D]).astype(
        LOW_TYPE
    )
    predicted = product_t(hidden_last, head_map)
    errors = predicted - noise_own
    elements = dp_count // GROUPS * patches.shape[0] * S * PATCH_IN
    loss_here = jnp.sum(errors * errors) / elements
    grad_pred = (2.0 * errors / elements).astype(LOW_TYPE)
    grad_head = weight_grad(grad_pred, hidden_last)
    grad_hidden = product(grad_pred, head_map)
    grad_final = jnp.concatenate(
        [jnp.sum(grad_hidden, 1), jnp.sum(grad_hidden * normed_last, 1)], axis=1
    ).astype(LOW_TYPE)
    grad_stream = normalize_back(
        grad_hidden * (1.0 + final_mod[:, None, D:]), normed_last, inverse_last
    )
    mod_list, bias_list, sums_list, flows = ([None] * L, [None] * L, [None] * L, None)
    moved_squares = 0.0
    late, grad_stream = tied(jnp.concatenate([second_map, cond_rows]), grad_stream)
    late = lax.all_gather(late, "dp", axis=1, tiled=True)
    second_time, cond_act = (late[:D], late[D:])
    for layer_at in range(L - 1, -1, -1):
        grad_stream, fresh, flows, mod_list[layer_at], bias_list[layer_at] = layer_backward(
            grad_stream,
            mod_parts[layer_at],
            attn_all[layer_at],
            mlp_all[layer_at],
            saved_states[layer_at],
            flows,
        )
        if flows:
            sums_list[layer_at + 1] = [flows[0], homeward(flows[1])]
            moved_squares = moved_squares + flows[2] + squared(flows[1])
        flows = fresh
    last_mlp = mlp_third(mlp_second(flows[0]))
    last_attn = attn_third(attn_second(flows[1]))
    moved_squares = moved_squares + squared(last_mlp) + squared(last_attn)
    last_mlp = homeward(last_mlp)
    grad_patch = weight_grad(noised, grad_stream.astype(LOW_TYPE))
    mine = patches_own.shape[0]
    early = jnp.concatenate(
        [grad_now.reshape(-1) for grad_now in mod_list[1:]]
        + [grad_final.reshape(-1)]
        + [grad_now.astype(LOW_TYPE) for grad_now in bias_list[1:]]
        + [grad_head.astype(LOW_TYPE).reshape(-1)]
    )
    late_part = jnp.concatenate(
        [
            mod_list[0].reshape(-1),
            bias_list[0].astype(LOW_TYPE),
            jnp.sum(grad_stream, (0, 1)).astype(LOW_TYPE),
            grad_patch.astype(LOW_TYPE).reshape(-1),
        ]
    )
    devices = dp_count * shards

    def cutter(vectors):
        gathered = lax.all_gather(vectors, ("dp", "tensor"))
        offset = 0

        def taken(width):
            nonlocal offset
            offset += width
            return gathered[:, offset - width : offset]

        return taken

    take_early, take_late = (cutter(early), cutter(late_part))
    takers = [take_late] + [take_early] * (L - 1)
    grad_mods = [
        natural_order(taker(mine * 6 * D).reshape(devices, mine, 6 * D), stretches)
        for taker in takers
    ]
    grad_finals = natural_order(take_early(mine * 2 * D).reshape(devices, mine, 2 * D), stretches)

    def group_sums(part):
        shaped = part.astype(jnp.float32).reshape(stretches, 2, 2, 2, shards // 2, -1)
        return jnp.sum(shaped, (0, 2, 4)).reshape(GROUPS, -1)

    layer_bias = 7 * D + FF - 3 * D
    bias_sums = [group_sums(taker(layer_bias)) for taker in takers]
    patch_bias = group_sums(take_late(D))
    patch_sums = group_sums(take_late(PATCH_IN * D)).reshape(GROUPS, PATCH_IN, D)
    head_sums = group_sums(take_early(PATCH_IN * D)).reshape(GROUPS, PATCH_IN, D)

    own_mods = [
        lax.dynamic_slice_in_dim(grad_now, shard_at * mod_width, mod_width, 1)
        for grad_now in grad_mods
    ]
    grad_cond_parts = sum(
        product_t(own_mods[layer_at], mod_low[layer_at]) for layer_at in range(L)
    )
    grad_cond_act = jnp.sum(
        lax.all_gather(grad_cond_parts.astype(LOW_TYPE), "tensor").astype(jnp.float32), 0
    ) + product(grad_finals, final_low)
    grad_condition = lax.all_gather(
        jax.vjp(jax.nn.silu, condition_rows)[1](grad_cond_act)[0].astype(LOW_TYPE),
        "dp",
        axis=1,
        tiled=True,
    )
    grad_smooth = product_t(grad_condition, second_time)
    grad_hidden_time = jax.vjp(jax.nn.silu, hidden_time)[1](grad_smooth)[0].astype(LOW_TYPE)

    def of_group(value):
        shaped = value.reshape((stretches, GROUPS, latents // dp_count) + value.shape[1:])
        return picked_at(shaped, group_at, 1).reshape((-1,) + value.shape[1:])

    def of_stretch(value):
        width = value.shape[-1] // stretches
        return lax.dynamic_slice_in_dim(value, stretch * width, width, value.ndim - 1)

    def latent_sums(value):
        shaped = value.astype(jnp.float32).reshape(stretches, GROUPS, latents // dp_count, -1)
        return jnp.sum(shaped, (0, 2))

    grad_condition_own = of_stretch(of_group(grad_condition))
    cond_own = of_stretch(of_group(cond_act))
    grad_embed = jnp.concatenate(
        [
            weight_grad(of_group(class_picks), grad_condition_own),
            weight_grad(of_group(freq_low), of_stretch(of_group(grad_hidden_time))),
            weight_grad(of_group(smooth_time), grad_condition_own),
            of_stretch(picked_at(patch_sums, group_at, 0)),
            weight_grad(of_group(grad_finals), cond_own),
            of_stretch(picked_at(head_sums, group_at, 0)),
        ],
        0,
    )
    grad_mod_map = jnp.stack([weight_grad(cond_own, of_group(grad_now)) for grad_now in own_mods])
    bias_groups = jnp.concatenate(
        [
            part
            for layer_at in range(L)
            for part in (bias_sums[layer_at], latent_sums(grad_mods[layer_at]))
        ]
        + [
            patch_bias,
            latent_sums(grad_hidden_time),
            latent_sums(grad_condition),
            latent_sums(grad_finals),
        ],
        axis=1,
    )
    side_squares = jnp.sum(grad_mod_map * grad_mod_map) + jnp.sum(grad_embed * grad_embed) / shards
    bias_squares = jnp.sum(bias_groups * bias_groups, 1)
    last_attn, (side_squares, bias_squares) = tied(last_attn, (side_squares, bias_squares))
    sums_list[0] = [last_mlp, homeward(last_attn)]
    attn_now = jnp.stack(
        [
            jnp.stack(
                [part[:, at * col_width : (at + 1) * col_width] for part in sums[1] for at in (0, 1)]
            )
            for sums in sums_list
        ]
    ).astype(jnp.float32)
    mlp_now = jnp.stack([jnp.stack(sums[0]) for sums in sums_list]).astype(jnp.float32)
    reduced = [attn_now, mlp_now, grad_mod_map, grad_embed]
    groups_here = jnp.arange(GROUPS, dtype=jnp.int32)
    picked = (groups_here == group_at).astype(jnp.float32)
    moved_group = (dp_at - (dp_at & 1) + (shard_at >> 1)) % GROUPS
    moved_picked = (groups_here == moved_group).astype(jnp.float32)
    totals = jnp.concatenate(
        [
            picked * side_squares + moved_picked * moved_squares,
            jnp.full((GROUPS,), loss_here),
            jnp.zeros((128 - 2 * GROUPS,)),
        ]
    )
    for axis in ("tensor", "dp"):
        rows_now = lax.all_gather(jnp.broadcast_to(totals, (8, 128)), axis, axis=0, tiled=True)
        totals = jnp.sum(rows_now.reshape(-1, 8, 128)[:, 0], 0)
    group_norms = jnp.sqrt(totals[:GROUPS] + bias_squares)
    clip_scale = CLIP_NORM / (group_norms + 1e-06)
    own_scale = jnp.sum(picked * clip_scale)
    shift_group = GROUPS.bit_length() - 1
    weights_in = (w_attn, w_mlp, w_mod, w_embed)
    momenta_in = (momentum_attn, momentum_mlp, momentum_mod, momentum_embed)
    firsts_in = (first_attn, first_mlp, first_mod, first_embed)
    seconds_in = (second_attn, second_mlp, second_mod, second_embed)
    axes_at = (2, 2, 1, 1)
    steps, summed, new_firsts, new_seconds = ([None] * 4, [None] * 4, [None] * 4, [None] * 4)

    def crossed(index_at):
        block = steps[index_at]
        for bit_at in range(1, shift_group):
            block = group_step(block, axes_at[index_at], shift_group, bit_at)
        return block.reshape(weights_in[index_at].shape)

    for index_at in (1, 0, 2, 3):
        grad_now = reduced[index_at]
        if index_at == 2:
            grad_now, steps[1] = tied(grad_now, steps[1])
        if index_at == 3:
            summed[1] = crossed(1)
            grad_now, (summed[1], steps[0]) = tied(grad_now, (summed[1], steps[0]))
        update, new_firsts[index_at], new_seconds[index_at] = adam_update(
            grad_now * own_scale, firsts_in[index_at], seconds_in[index_at]
        )
        axis_at = axes_at[index_at]
        steps[index_at] = group_step(
            split_bits(update, axis_at, shift_group), axis_at, shift_group, 0
        )
    for index_at in (0, 2, 3):
        summed[index_at] = crossed(index_at)
    new_weights, new_momenta = ([], [])
    for index_at in range(4):
        outer_grad = LEARN_RATE * (summed[index_at] / GROUPS + WEIGHT_DECAY * weights_in[index_at])
        momentum_new = OUTER_MOMENTUM * momenta_in[index_at] + outer_grad
        new_weights.append(
            weights_in[index_at] - OUTER_RATE * (outer_grad + OUTER_MOMENTUM * momentum_new)
        )
        new_momenta.append(momentum_new)
    clipped_bias = bias_groups * clip_scale[:, None]
    bias_updates, bias_first, bias_second = adam_update(
        clipped_bias, first_bias.reshape(GROUPS, -1), second_bias.reshape(GROUPS, -1)
    )
    outer_bias = LEARN_RATE * (jnp.mean(bias_updates, 0) + WEIGHT_DECAY * bias_flat)
    bias_momentum = OUTER_MOMENTUM * momentum_bias.reshape(-1) + outer_bias
    bias_new = bias_flat - OUTER_RATE * (outer_bias + OUTER_MOMENTUM * bias_momentum)
    return (
        totals[GROUPS] / GROUPS,
        group_norms,
        clipped_bias.reshape(first_bias.shape),
        new_weights[0],
        new_weights[1],
        new_weights[2],
        new_weights[3],
        bias_new.reshape(biases.shape),
        new_momenta[0],
        new_momenta[1],
        new_momenta[2],
        new_momenta[3],
        bias_momentum.reshape(biases.shape),
        new_firsts[0],
        new_seconds[0],
        new_firsts[1],
        new_seconds[1],
        new_firsts[2],
        new_seconds[2],
        new_firsts[3],
        new_seconds[3],
        bias_first.reshape(first_bias.shape),
        bias_second.reshape(second_bias.shape),
    )


def solution(mesh):
    placed = (
        P("dp", None, None),
        P("dp", None, None),
        P("dp"),
        P("dp"),
        P(None, None, "dp", "tensor"),
        P(None, None, "dp", "tensor"),
        P(None, "dp", "tensor"),
        P(None, "dp"),
        P(),
        P(None, None, "dp", "tensor"),
        P(None, None, "dp", "tensor"),
        P(None, "dp", "tensor"),
        P(None, "dp"),
        P(),
        P(None, None, "dp", "tensor"),
        P(None, None, "dp", "tensor"),
        P(None, None, "dp", "tensor"),
        P(None, None, "dp", "tensor"),
        P(None, "dp", "tensor"),
        P(None, "dp", "tensor"),
        P(None, "dp"),
        P(None, "dp"),
        P(),
        P(),
    )
    return jax.shard_map(
        per_device,
        mesh=mesh,
        in_specs=placed,
        out_specs=(
            P(),
            P(),
            P(),
            P(None, None, "dp", "tensor"),
            P(None, None, "dp", "tensor"),
            P(None, "dp", "tensor"),
            P(None, "dp"),
            P(),
            P(None, None, "dp", "tensor"),
            P(None, None, "dp", "tensor"),
            P(None, "dp", "tensor"),
            P(None, "dp"),
            P(),
            P(None, None, "dp", "tensor"),
            P(None, None, "dp", "tensor"),
            P(None, None, "dp", "tensor"),
            P(None, None, "dp", "tensor"),
            P(None, "dp", "tensor"),
            P(None, "dp", "tensor"),
            P(None, "dp"),
            P(None, "dp"),
            P(),
            P(),
        ),
        check_vma=False,
    )
```

```python
import jax
import jax.numpy as jnp
from jax import lax
from jax.experimental import pallas as pl
from jax.sharding import PartitionSpec as P

D = 768
HD = 64
FF = 3072
NCLS = 1000
FREQ = 256
PATCH_IN = 16
SIDE = 16
L = 2
GROUPS = 4
STEP_COUNT = 10
NSTEPS = 1000
S = 256
LB = 14


LOW_TYPE = jnp.bfloat16
LEARN_RATE = 0.03
WEIGHT_DECAY = 0.1
BETA_FIRST = 0.9
BETA_SECOND = 0.95
ADAM_EPSILON = 1e-08
CLIP_NORM = 0.02
OUTER_RATE = 0.7
OUTER_MOMENTUM = 0.9


def shortened(shard):
    return jax.tree.map(lambda a: a.astype(jnp.bfloat16) if a.dtype == jnp.float32 else a, shard)


def swapped(value, axis, bit):
    mask = 2**bit
    pairs = [(source, source ^ mask) for source in range(lax.axis_size(axis))]
    return lax.ppermute(value, axis, pairs)


def product(left, right):
    return jnp.dot(left, right, preferred_element_type=jnp.float32)


def product_t(left, right):
    return lax.dot_general(
        left, right, (((left.ndim - 1,), (1,)), ((), ())), preferred_element_type=jnp.float32
    )


def weight_grad(inputs, grads_out):
    leading = tuple(range(inputs.ndim - 1))
    return lax.dot_general(
        inputs, grads_out, ((leading, leading), ((), ())), preferred_element_type=jnp.float32
    )


def normalize(values):
    centred = values - jnp.mean(values, -1, keepdims=True)
    inverse = lax.rsqrt(jnp.mean(centred * centred, -1, keepdims=True) + 1e-06)
    return (centred * inverse, inverse)


def normalize_back(grad_in, normed, inverse):
    return inverse * (
        grad_in
        - jnp.mean(grad_in, -1, keepdims=True)
        - normed * jnp.mean(grad_in * normed, -1, keepdims=True)
    )


def gelu_tanh(values):
    return jax.nn.gelu(values, approximate=True)


def positions():
    quarter = D // 4
    omegas = 1.0 / 10000.0 ** (jnp.arange(quarter, dtype=jnp.float32) / quarter)
    places = jnp.arange(S, dtype=jnp.int32)
    across = (places % SIDE).astype(jnp.float32)[:, None] * omegas[None, :]
    downward = (places // SIDE).astype(jnp.float32)[:, None] * omegas[None, :]
    return jnp.concatenate(
        [jnp.sin(across), jnp.cos(across), jnp.sin(downward), jnp.cos(downward)], axis=1
    )


def frequencies(stamps):
    half_width = FREQ // 2
    freq_rates = jnp.exp(-jnp.log(10000.0) * jnp.arange(half_width, dtype=jnp.float32) / half_width)
    angles = stamps.astype(jnp.float32)[:, None] * freq_rates[None, :]
    return jnp.concatenate([jnp.cos(angles), jnp.sin(angles)], axis=1)


def signal_levels(stamps):
    noise_rates = jnp.linspace(0.0001, 0.02, NSTEPS, dtype=jnp.float32)
    kept_share = jnp.cumprod(1.0 - noise_rates)
    matches = stamps[:, None] == jnp.arange(NSTEPS, dtype=jnp.int32)[None, :]
    return jnp.sum(jnp.where(matches, kept_share[None, :], 0.0), axis=1)


def embed_parts(matrix):
    bounds = [
        NCLS,
        NCLS + FREQ,
        NCLS + FREQ + D,
        NCLS + FREQ + D + PATCH_IN,
        NCLS + FREQ + 3 * D + PATCH_IN,
    ]
    return (
        matrix[: bounds[0]],
        matrix[bounds[0] : bounds[1]],
        matrix[bounds[1] : bounds[2]],
        matrix[bounds[2] : bounds[3]],
        matrix[bounds[3] : bounds[4]],
        matrix[bounds[4] :],
    )


def split_heads(array_in):
    return array_in.reshape(array_in.shape[:2] + (array_in.shape[2] // HD, HD))


def head_scores(queries, key_rows):
    return jnp.einsum(
        "nqhd,nkhd->nhqk",
        split_heads(queries),
        split_heads(key_rows),
        preferred_element_type=jnp.float32,
    ) * HD ** (-0.5)


def attend(queries, key_rows, values):
    scores = head_scores(queries, key_rows)
    highest = jnp.max(scores, -1, keepdims=True)
    log_total = highest + jnp.log(jnp.sum(jnp.exp(scores - highest), -1, keepdims=True))
    weights = jnp.exp(scores - log_total).astype(LOW_TYPE)
    output = jnp.einsum(
        "nhqk,nkhd->nqhd", weights, split_heads(values), preferred_element_type=jnp.float32
    )
    return (output.reshape(queries.shape), log_total)


def attend_back(queries, key_rows, values, log_total, grad_out):
    weights = jnp.exp(head_scores(queries, key_rows) - log_total)
    grad_heads = split_heads(grad_out)
    grad_values = jnp.einsum(
        "nhqk,nqhd->nkhd", weights.astype(LOW_TYPE), grad_heads, preferred_element_type=jnp.float32
    )
    grad_weights = jnp.einsum(
        "nqhd,nkhd->nhqk", grad_heads, split_heads(values), preferred_element_type=jnp.float32
    )
    grad_scores = (
        weights * (grad_weights - jnp.sum(weights * grad_weights, -1, keepdims=True))
    ).astype(LOW_TYPE)
    grad_queries = jnp.einsum(
        "nhqk,nkhd->nqhd", grad_scores, split_heads(key_rows), preferred_element_type=jnp.float32
    ) * HD ** (-0.5)
    grad_keys = jnp.einsum(
        "nhqk,nqhd->nkhd", grad_scores, split_heads(queries), preferred_element_type=jnp.float32
    ) * HD ** (-0.5)
    return (
        grad_queries.reshape(queries.shape).astype(LOW_TYPE),
        grad_keys.reshape(queries.shape).astype(LOW_TYPE),
        grad_values.reshape(queries.shape).astype(LOW_TYPE),
    )


def place(vector_all, piece_in, offset):
    return lax.dynamic_update_slice_in_dim(vector_all, piece_in, offset, 0)


def flipped(value, masks):
    shards = lax.axis_size("tensor")
    count = lax.axis_size("dp") * shards
    pairs = [(source, source ^ masks[source // shards & 1]) for source in range(count)]
    return lax.ppermute(value, ("dp", "tensor"), pairs)


def picked_at(value, index_at, axis):
    return lax.dynamic_index_in_dim(value, index_at, axis, keepdims=False)


def layer_forward(stream, mod_parts, attn_now, mlp_now, bias_layer):
    width_all = stream.shape[-1]
    normed_one, inverse_one = normalize(stream)
    hidden_one = (normed_one * (1.0 + mod_parts[1]) + mod_parts[0]).astype(LOW_TYPE)
    queries = (product(hidden_one, attn_now[0]) + bias_layer[:width_all]).astype(LOW_TYPE)
    key_rows = product(hidden_one, attn_now[1]).astype(LOW_TYPE)
    values = (product(hidden_one, attn_now[2]) + bias_layer[width_all : 2 * width_all]).astype(
        LOW_TYPE
    )
    attended, log_total = attend(queries, key_rows, values)
    attended = attended.astype(LOW_TYPE)
    branch_one = product_t(attended, attn_now[3]) + bias_layer[2 * width_all : 3 * width_all]
    middle = stream + mod_parts[2] * branch_one
    normed_two, inverse_two = normalize(middle)
    hidden_two = (normed_two * (1.0 + mod_parts[4]) + mod_parts[3]).astype(LOW_TYPE)
    unit_width = mlp_now[0][0].shape[-1]
    before = [
        product(hidden_two, mlp_now[0][unit_at])
        + bias_layer[3 * width_all + unit_at * unit_width : 3 * width_all + (unit_at + 1) * unit_width]
        for unit_at in range(len(mlp_now[0]))
    ]
    activated = [gelu_tanh(part).astype(LOW_TYPE) for part in before]
    branch_two = bias_layer[3 * width_all + FF : 4 * width_all + FF] + sum(
        product_t(part, mlp_now[1][unit_at]) for unit_at, part in enumerate(activated)
    )
    result = middle + mod_parts[5] * branch_two
    kept_state = (
        normed_one,
        inverse_one,
        hidden_one,
        queries,
        key_rows,
        values,
        log_total,
        attended,
        branch_one,
        normed_two,
        inverse_two,
        hidden_two,
        before,
        activated,
        branch_two,
    )
    return (result, kept_state)


def exchanged(value, mask):
    count = lax.axis_size("dp") * lax.axis_size("tensor")
    return lax.ppermute(value, ("dp", "tensor"), [(source, source ^ mask) for source in range(count)])


def half_of(value, axis, bit):
    width = value.shape[axis] // 2
    return lax.dynamic_slice_in_dim(value, bit * width, width, axis)


def summed_low(left, right):
    return (left.astype(jnp.float32) + right.astype(jnp.float32)).astype(LOW_TYPE)


def rows_halved(value):
    stretch = lax.axis_index("dp") // GROUPS
    stretches = lax.axis_size("dp") // GROUPS
    for bit_at in reversed(range(stretches.bit_length() - 1)):
        bit = stretch >> bit_at & 1
        received = exchanged(
            half_of(value, 0, 1 - bit), lax.axis_size("tensor") * GROUPS << bit_at
        )
        value = summed_low(half_of(value, 0, bit), received)
    return value


def columns_halved(sent, kept):
    return summed_low(kept, exchanged(sent, 1))


def unit_halved(first, second):
    picked = (lax.axis_index("tensor") & 1) == 1
    return columns_halved(jnp.where(picked, first, second), jnp.where(picked, second, first))


def pair_halved(first, second):
    bit = lax.axis_index("tensor") & 1

    def halves(bit_now):
        return jnp.concatenate([half_of(first, 1, bit_now), half_of(second, 1, bit_now)], 1)

    return columns_halved(halves(1 - bit), halves(bit))


def core_summed(sent, kept):
    return [
        summed_low(own, exchanged(other, lax.axis_size("tensor"))) for other, own in zip(sent, kept)
    ]


def homeward(values):
    shards = lax.axis_size("tensor")
    pairs = []
    for source in range(lax.axis_size("dp") * shards):
        core, high = (source // shards & 1, source % shards >> 1)
        pairs.append((source, source ^ (core ^ high) * (shards + shards // 2)))
    return [lax.ppermute(value, ("dp", "tensor"), pairs) for value in values]


def squared(values):
    return sum(jnp.sum(jnp.square(value.astype(jnp.float32))) for value in values)


def mlp_second(totals):
    up_zero, up_one, down_zero, down_one = totals
    return [rows_halved(up_zero), rows_halved(up_one), unit_halved(down_zero, down_one)]


def mlp_third(totals):
    up_zero, up_one, down = totals
    return [unit_halved(up_zero, up_one), rows_halved(down)]


def attn_second(totals):
    query_key, value_map, out_map = totals
    return [rows_halved(query_key), pair_halved(value_map, out_map)]


def attn_third(totals):
    query_key, value_out = totals
    width = query_key.shape[1] // 2
    return [pair_halved(query_key[:, :width], query_key[:, width:]), rows_halved(value_out)]


def attn_maps(gathered, layer_at):
    shards, rows_all, width_all = gathered.shape[1:]
    width, rows = (width_all // 4, rows_all // 4)

    def kernel(gathered_ref, maps_ref):
        for kind in range(4):
            maps_ref[kind] = jnp.concatenate(
                [
                    gathered_ref[0, shard][:, kind * width : (kind + 1) * width]
                    for shard in range(shards)
                ],
                axis=1,
            )

    return pl.pallas_call(
        kernel,
        grid=(4,),
        in_specs=[
            pl.BlockSpec((1, shards, rows, width_all), lambda at: (layer_at, 0, at, 0)),
        ],
        out_specs=pl.BlockSpec((4, rows, shards * width), lambda at: (0, at, 0)),
        out_shape=jax.ShapeDtypeStruct((4, rows_all, shards * width), gathered.dtype),
        name="attn_maps",
    )(gathered)


def tied(value, flows):
    return lax.optimization_barrier((value, flows))


def layer_backward(grad_out, mod_parts, attn_now, mlp_now, kept_state, flows):
    (
        normed_one,
        inverse_one,
        hidden_one,
        queries,
        key_rows,
        values,
        log_total,
        attended,
        branch_one,
        normed_two,
        inverse_two,
        hidden_two,
        saved_pre,
        activated,
        branch_two,
    ) = kept_state
    core = lax.axis_index("dp") & 1
    pair = len(activated) // 2
    if flows:
        flows = [mlp_second(flows[0]), flows[1]]
        grad_out, flows = tied(grad_out, flows)
    grad_gate_two = jnp.sum(grad_out * branch_two, 1)
    downward = grad_out * mod_parts[5]
    down_low = downward.astype(LOW_TYPE)
    grad_pre = [
        jax.vjp(gelu_tanh, part)[1](product(down_low, mlp_now[1][unit_at]))[0].astype(LOW_TYPE)
        for unit_at, part in enumerate(saved_pre)
    ]

    def unit_grads(side):
        picked = core == side
        up = [jnp.where(picked, grad_pre[at + pair], grad_pre[at]) for at in range(pair)]
        down = [jnp.where(picked, activated[at + pair], activated[at]) for at in range(pair)]
        return [weight_grad(hidden_two, part).astype(LOW_TYPE) for part in up] + [
            weight_grad(down_low, part).astype(LOW_TYPE) for part in down
        ]

    sent = unit_grads(0)
    mlp_sums = core_summed(sent, unit_grads(1))
    grad_hidden_two = sum(
        product_t(part, mlp_now[0][unit_at]) for unit_at, part in enumerate(grad_pre)
    )
    grad_middle = grad_out + normalize_back(
        grad_hidden_two * (1.0 + mod_parts[4]), normed_two, inverse_two
    )
    grad_gate_one = jnp.sum(grad_middle * branch_one, 1)
    upward = grad_middle * mod_parts[2]
    if flows:
        flows = [mlp_third(flows[0]), attn_second(flows[1])]
    up_low, (mlp_sums, flows) = tied(upward.astype(LOW_TYPE), (mlp_sums, flows))
    grad_attended = product(up_low, attn_now[3]).astype(LOW_TYPE)
    grad_queries, grad_keys, grad_values = attend_back(
        queries, key_rows, values, log_total, grad_attended
    )
    if flows:
        flows = [homeward(flows[0]), attn_third(flows[1]), squared(flows[0])]
        grad_queries, flows = tied(grad_queries, flows)

    def map_grads(side):
        both = jnp.concatenate([half_of(grad_queries, 2, side), half_of(grad_keys, 2, side)], 2)
        return [
            weight_grad(hidden_one, both).astype(LOW_TYPE),
            weight_grad(hidden_one, half_of(grad_values, 2, side)).astype(LOW_TYPE),
            weight_grad(up_low, half_of(attended, 2, side)).astype(LOW_TYPE),
        ]

    attn_sums = core_summed(map_grads(1 - core), map_grads(core))
    grad_hidden_one = (
        product_t(grad_queries, attn_now[0])
        + product_t(grad_keys, attn_now[1])
        + product_t(grad_values, attn_now[2])
    )
    grad_stream = grad_middle + normalize_back(
        grad_hidden_one * (1.0 + mod_parts[1]), normed_one, inverse_one
    )
    grad_modulation = jnp.concatenate(
        [
            jnp.sum(grad_hidden_one, 1),
            jnp.sum(grad_hidden_one * normed_one, 1),
            grad_gate_one,
            jnp.sum(grad_hidden_two, 1),
            jnp.sum(grad_hidden_two * normed_two, 1),
            grad_gate_two,
        ],
        axis=1,
    ).astype(LOW_TYPE)
    bias_grad = jnp.concatenate(
        [
            jnp.sum(grad_queries.astype(jnp.float32), (0, 1)),
            jnp.sum(grad_values.astype(jnp.float32), (0, 1)),
            jnp.sum(upward, (0, 1)),
        ]
        + [jnp.sum(part.astype(jnp.float32), (0, 1)) for part in grad_pre]
        + [jnp.sum(downward, (0, 1))]
    )
    return (grad_stream, [mlp_sums, attn_sums], flows, grad_modulation, bias_grad)


def own_latents(value):
    shards = lax.axis_size("tensor")
    low_bit, shard_at = (lax.axis_index("dp") & 1, lax.axis_index("tensor"))
    count = value.shape[0] // shards
    base = (shard_at & 1) * 2
    mine = lax.dynamic_slice_in_dim(value, (base + low_bit) * count, count, 0)
    theirs = lax.dynamic_slice_in_dim(value, (base + 1 - low_bit) * count, count, 0)
    received = flipped(theirs, (shards, shards))
    return jnp.where(shard_at >> 1 == low_bit, mine, received)


def natural_order(gathered, stretches):
    shaped = gathered.reshape((stretches, 2, 2, 2, 2) + gathered.shape[1:])
    moved = jnp.moveaxis(shaped, 2, 4)
    return moved.reshape((-1,) + gathered.shape[2:])


def split_bits(array_in, axis_at, count_bits):
    dims_in = array_in.shape
    return array_in.reshape(
        dims_in[:axis_at]
        + (2,) * count_bits
        + (dims_in[axis_at] >> count_bits,)
        + dims_in[axis_at + 1 :]
    )


def group_step(block, axis_at, count_bits, bit_at):
    own_bit = lax.axis_index("dp") >> bit_at & 1
    at = axis_at + count_bits - 1 - bit_at
    sent = shortened(lax.dynamic_slice_in_dim(block, 1 - own_bit, 1, at))
    return lax.dynamic_slice_in_dim(block, own_bit, 1, at) + swapped(sent, "dp", bit_at)


def adam_update(gradient, first_old, second_old):
    first_new = BETA_FIRST * first_old + (1.0 - BETA_FIRST) * gradient
    second_new = BETA_SECOND * second_old + (1.0 - BETA_SECOND) * gradient * gradient
    update = (
        first_new
        / (1.0 - BETA_FIRST**STEP_COUNT)
        / (jnp.sqrt(second_new / (1.0 - BETA_SECOND**STEP_COUNT)) + ADAM_EPSILON)
    )
    return (update, first_new, second_new)


def per_device(
    patches,
    noise_draw,
    timesteps,
    labels,
    w_attn,
    w_mlp,
    w_mod,
    w_embed,
    biases,
    momentum_attn,
    momentum_mlp,
    momentum_mod,
    momentum_embed,
    momentum_bias,
    first_attn,
    second_attn,
    first_mlp,
    second_mlp,
    first_mod,
    second_mod,
    first_embed,
    second_embed,
    first_bias,
    second_bias,
):
    shards = lax.axis_size("tensor")
    shard_at = lax.axis_index("tensor")
    dp_count = lax.axis_size("dp")
    dp_at = lax.axis_index("dp")
    group_at = dp_at % GROUPS
    stretches = dp_count // GROUPS
    stretch = dp_at // GROUPS
    layer_span = LB * D
    col_width = w_attn.shape[3]
    row_width = w_attn.shape[2]
    mod_width = w_mod.shape[2]
    latents = dp_count * patches.shape[0]
    everyone = ("tensor", "dp")

    stamps, marks = lax.all_gather(jnp.stack([timesteps, labels]), "dp", axis=1, tiled=True)
    embed_low = w_embed.astype(LOW_TYPE)
    conditioners = NCLS + FREQ + D + PATCH_IN
    first_map = embed_low[NCLS : NCLS + FREQ]
    second_map = embed_low[NCLS + FREQ : NCLS + FREQ + D]

    def attn_local(layer_at):
        return jnp.transpose(w_attn[layer_at], (1, 0, 2)).reshape(1, row_width, 4 * col_width)

    first_local = [attn_local(layer_at) for layer_at in range(L)] + list(w_mlp[: L - 1])
    first_local = jnp.concatenate(
        [part.astype(LOW_TYPE).reshape(-1, row_width, 4 * col_width) for part in first_local]
    )
    first_whole = lax.all_gather(first_local, everyone, axis=1, tiled=True)
    last_whole = lax.all_gather(w_mlp[L - 1].astype(LOW_TYPE), everyone, axis=1, tiled=True)
    units_whole = first_whole.reshape(-1, shards, D, 4 * col_width)
    attn_all = [attn_maps(units_whole, layer_at) for layer_at in range(L)]
    mlp_all = [
        [[units_whole[L + 2 * layer_at + kind, at] for at in range(shards)] for kind in range(2)]
        for layer_at in range(L - 1)
    ]
    last_whole = last_whole.reshape(2, shards, D, -1)
    mlp_all.append([[last_whole[kind, at] for at in range(shards)] for kind in range(2)])

    bias_flat = biases.reshape(-1)
    bias_tail = bias_flat[L * layer_span :]
    freq_low = frequencies(stamps).astype(LOW_TYPE)

    def own_columns(vector):
        return lax.dynamic_slice_in_dim(vector, dp_at * row_width, row_width, 0)

    hidden_cols = product(freq_low, first_map) + own_columns(bias_tail[D : 2 * D])
    gathered_cols = lax.all_gather(
        jnp.concatenate(
            [
                hidden_cols,
                w_embed[conditioners - PATCH_IN : conditioners],
                w_embed[-PATCH_IN:],
            ]
        ),
        "dp",
        axis=1,
        tiled=True,
    )
    hidden_time = gathered_cols[:latents]
    patch_map = gathered_cols[latents : latents + PATCH_IN].astype(LOW_TYPE)
    head_map = gathered_cols[latents + PATCH_IN :].astype(LOW_TYPE)
    smooth_time = jax.nn.silu(hidden_time).astype(LOW_TYPE)
    class_picks = (marks[:, None] == jnp.arange(NCLS, dtype=jnp.int32)[None, :]).astype(LOW_TYPE)
    condition_rows = (
        product(smooth_time, second_map)
        + own_columns(bias_tail[2 * D : 3 * D])
        + product(class_picks, embed_low[:NCLS])
    )
    cond_rows = jax.nn.silu(condition_rows).astype(LOW_TYPE)
    mod_low = w_mod.astype(LOW_TYPE)
    final_low = embed_low[conditioners:-PATCH_IN]
    final_width = final_low.shape[0] // shards
    mod_cols = jnp.concatenate(
        [product(cond_rows, mod_low[layer_at]) for layer_at in range(L)]
        + [
            product_t(
                cond_rows, lax.dynamic_slice_in_dim(final_low, shard_at * final_width, final_width, 0)
            )
        ],
        axis=1,
    )
    mod_cols = lax.psum_scatter(mod_cols, "dp", scatter_dimension=0, tiled=True)
    mod_all = own_latents(
        jnp.swapaxes(lax.all_gather(mod_cols.astype(LOW_TYPE), "tensor"), 0, 1)
    ).astype(jnp.float32)
    mod_parts = []
    for layer_at in range(L):
        modulation = (
            mod_all[:, :, layer_at * mod_width : (layer_at + 1) * mod_width].reshape(-1, 6 * D)
            + bias_flat[layer_at * layer_span + 4 * D + FF : (layer_at + 1) * layer_span]
        )
        mod_parts.append(
            [modulation[:, None, part_at * D : (part_at + 1) * D] for part_at in range(6)]
        )
    final_mod = mod_all[:, :, L * mod_width :].reshape(-1, 2 * D) + bias_tail[3 * D : 5 * D]

    patches_own, noise_own = (own_latents(patches), own_latents(noise_draw))
    signal = own_latents(signal_levels(timesteps)[:, None])[:, :, None]
    noised = (jnp.sqrt(signal) * patches_own + jnp.sqrt(1.0 - signal) * noise_own).astype(LOW_TYPE)
    stream = product(noised, patch_map) + bias_tail[:D] + positions()
    saved_states = []
    for layer_at in range(L):
        stream, kept_state = layer_forward(
            stream,
            mod_parts[layer_at],
            attn_all[layer_at],
            mlp_all[layer_at],
            bias_flat[layer_at * layer_span : (layer_at + 1) * layer_span],
        )
        saved_states.append(kept_state)
    normed_last, inverse_last = normalize(stream)
    hidden_last = (normed_last * (1.0 + final_mod[:, None, D:]) + final_mod[:, None, :D]).astype(
        LOW_TYPE
    )
    predicted = product_t(hidden_last, head_map)
    errors = predicted - noise_own
    elements = dp_count // GROUPS * patches.shape[0] * S * PATCH_IN
    loss_here = jnp.sum(errors * errors) / elements
    grad_pred = (2.0 * errors / elements).astype(LOW_TYPE)
    grad_head = weight_grad(grad_pred, hidden_last)
    grad_hidden = product(grad_pred, head_map)
    grad_final = jnp.concatenate(
        [jnp.sum(grad_hidden, 1), jnp.sum(grad_hidden * normed_last, 1)], axis=1
    ).astype(LOW_TYPE)
    grad_stream = normalize_back(
        grad_hidden * (1.0 + final_mod[:, None, D:]), normed_last, inverse_last
    )
    mod_list, bias_list, sums_list, flows = ([None] * L, [None] * L, [None] * L, None)
    moved_squares = 0.0
    late, grad_stream = tied(jnp.concatenate([second_map, cond_rows]), grad_stream)
    late = lax.all_gather(late, "dp", axis=1, tiled=True)
    second_time, cond_act = (late[:D], late[D:])
    for layer_at in range(L - 1, -1, -1):
        grad_stream, fresh, flows, mod_list[layer_at], bias_list[layer_at] = layer_backward(
            grad_stream,
            mod_parts[layer_at],
            attn_all[layer_at],
            mlp_all[layer_at],
            saved_states[layer_at],
            flows,
        )
        if flows:
            sums_list[layer_at + 1] = [flows[0], homeward(flows[1])]
            moved_squares = moved_squares + flows[2] + squared(flows[1])
        flows = fresh
    last_mlp = mlp_third(mlp_second(flows[0]))
    last_attn = attn_second(flows[1])
    moved_squares = moved_squares + squared(last_mlp)
    grad_patch = weight_grad(noised, grad_stream.astype(LOW_TYPE))
    mine = patches_own.shape[0]
    early = jnp.concatenate(
        [grad_now.reshape(-1) for grad_now in mod_list[1:]]
        + [grad_final.reshape(-1)]
        + [grad_now.astype(LOW_TYPE) for grad_now in bias_list[1:]]
        + [grad_head.astype(LOW_TYPE).reshape(-1)]
    )
    late_part = jnp.concatenate(
        [
            mod_list[0].reshape(-1),
            bias_list[0].astype(LOW_TYPE),
            jnp.sum(grad_stream, (0, 1)).astype(LOW_TYPE),
            grad_patch.astype(LOW_TYPE).reshape(-1),
        ]
    )
    devices = dp_count * shards

    def cutter(vectors):
        gathered = lax.all_gather(vectors, ("dp", "tensor"))
        offset = 0

        def taken(width):
            nonlocal offset
            offset += width
            return gathered[:, offset - width : offset]

        return taken

    take_early, take_late = (cutter(early), cutter(late_part))
    takers = [take_late] + [take_early] * (L - 1)
    grad_mods = [
        natural_order(taker(mine * 6 * D).reshape(devices, mine, 6 * D), stretches)
        for taker in takers
    ]
    grad_finals = natural_order(take_early(mine * 2 * D).reshape(devices, mine, 2 * D), stretches)

    def group_sums(part):
        shaped = part.astype(jnp.float32).reshape(stretches, 2, 2, 2, shards // 2, -1)
        return jnp.sum(shaped, (0, 2, 4)).reshape(GROUPS, -1)

    layer_bias = 7 * D + FF - 3 * D
    bias_sums = [group_sums(taker(layer_bias)) for taker in takers]
    patch_bias = group_sums(take_late(D))
    patch_sums = group_sums(take_late(PATCH_IN * D)).reshape(GROUPS, PATCH_IN, D)
    head_sums = group_sums(take_early(PATCH_IN * D)).reshape(GROUPS, PATCH_IN, D)

    own_mods = [
        lax.dynamic_slice_in_dim(grad_now, shard_at * mod_width, mod_width, 1)
        for grad_now in grad_mods
    ]
    grad_cond_parts = sum(
        product_t(own_mods[layer_at], mod_low[layer_at]) for layer_at in range(L)
    )
    grad_cond_act = jnp.sum(
        lax.all_gather(grad_cond_parts.astype(LOW_TYPE), "tensor").astype(jnp.float32), 0
    ) + product(grad_finals, final_low)
    grad_condition = lax.all_gather(
        jax.vjp(jax.nn.silu, condition_rows)[1](grad_cond_act)[0].astype(LOW_TYPE),
        "dp",
        axis=1,
        tiled=True,
    )
    grad_condition, (last_attn, last_mlp) = tied(grad_condition, (last_attn, last_mlp))
    last_attn = attn_third(last_attn)
    last_mlp = homeward(last_mlp)
    grad_smooth = product_t(grad_condition, second_time)
    grad_hidden_time = jax.vjp(jax.nn.silu, hidden_time)[1](grad_smooth)[0].astype(LOW_TYPE)
    grad_hidden_time, last_attn = tied(grad_hidden_time, last_attn)
    moved_squares = moved_squares + squared(last_attn)

    def of_group(value):
        shaped = value.reshape((stretches, GROUPS, latents // dp_count) + value.shape[1:])
        return picked_at(shaped, group_at, 1).reshape((-1,) + value.shape[1:])

    def of_stretch(value):
        width = value.shape[-1] // stretches
        return lax.dynamic_slice_in_dim(value, stretch * width, width, value.ndim - 1)

    def latent_sums(value):
        shaped = value.astype(jnp.float32).reshape(stretches, GROUPS, latents // dp_count, -1)
        return jnp.sum(shaped, (0, 2))

    grad_condition_own = of_stretch(of_group(grad_condition))
    cond_own = of_stretch(of_group(cond_act))
    grad_embed = jnp.concatenate(
        [
            weight_grad(of_group(class_picks), grad_condition_own),
            weight_grad(of_group(freq_low), of_stretch(of_group(grad_hidden_time))),
            weight_grad(of_group(smooth_time), grad_condition_own),
            of_stretch(picked_at(patch_sums, group_at, 0)),
            weight_grad(of_group(grad_finals), cond_own),
            of_stretch(picked_at(head_sums, group_at, 0)),
        ],
        0,
    )
    grad_mod_map = jnp.stack([weight_grad(cond_own, of_group(grad_now)) for grad_now in own_mods])
    bias_groups = jnp.concatenate(
        [
            part
            for layer_at in range(L)
            for part in (bias_sums[layer_at], latent_sums(grad_mods[layer_at]))
        ]
        + [
            patch_bias,
            latent_sums(grad_hidden_time),
            latent_sums(grad_condition),
            latent_sums(grad_finals),
        ],
        axis=1,
    )
    side_squares = jnp.sum(grad_mod_map * grad_mod_map) + jnp.sum(grad_embed * grad_embed) / shards
    bias_squares = jnp.sum(bias_groups * bias_groups, 1)
    last_attn, (side_squares, bias_squares) = tied(last_attn, (side_squares, bias_squares))
    sums_list[0] = [last_mlp, homeward(last_attn)]
    attn_now = jnp.stack(
        [
            jnp.stack(
                [part[:, at * col_width : (at + 1) * col_width] for part in sums[1] for at in (0, 1)]
            )
            for sums in sums_list
        ]
    ).astype(jnp.float32)
    mlp_now = jnp.stack([jnp.stack(sums[0]) for sums in sums_list]).astype(jnp.float32)
    reduced = [attn_now, mlp_now, grad_mod_map, grad_embed]
    groups_here = jnp.arange(GROUPS, dtype=jnp.int32)
    picked = (groups_here == group_at).astype(jnp.float32)
    moved_group = (dp_at - (dp_at & 1) + (shard_at >> 1)) % GROUPS
    moved_picked = (groups_here == moved_group).astype(jnp.float32)
    totals = jnp.concatenate(
        [
            picked * side_squares + moved_picked * moved_squares,
            jnp.full((GROUPS,), loss_here),
            jnp.zeros((128 - 2 * GROUPS,)),
        ]
    )
    for axis in ("tensor", "dp"):
        rows_now = lax.all_gather(jnp.broadcast_to(totals, (8, 128)), axis, axis=0, tiled=True)
        totals = jnp.sum(rows_now.reshape(-1, 8, 128)[:, 0], 0)
    group_norms = jnp.sqrt(totals[:GROUPS] + bias_squares)
    clip_scale = CLIP_NORM / (group_norms + 1e-06)
    own_scale = jnp.sum(picked * clip_scale)
    shift_group = GROUPS.bit_length() - 1
    weights_in = (w_attn, w_mlp, w_mod, w_embed)
    momenta_in = (momentum_attn, momentum_mlp, momentum_mod, momentum_embed)
    firsts_in = (first_attn, first_mlp, first_mod, first_embed)
    seconds_in = (second_attn, second_mlp, second_mod, second_embed)
    axes_at = (2, 2, 1, 1)
    steps, summed, new_firsts, new_seconds = ([None] * 4, [None] * 4, [None] * 4, [None] * 4)

    def crossed(index_at):
        block = steps[index_at]
        for bit_at in range(1, shift_group):
            block = group_step(block, axes_at[index_at], shift_group, bit_at)
        return block.reshape(weights_in[index_at].shape)

    for index_at in (3, 1, 0, 2):
        grad_now = reduced[index_at]
        if index_at == 0:
            grad_now, steps[3] = tied(grad_now, steps[3])
        if index_at == 2:
            summed[3] = crossed(3)
            grad_now, (summed[3], steps[1]) = tied(grad_now, (summed[3], steps[1]))
        update, new_firsts[index_at], new_seconds[index_at] = adam_update(
            grad_now * own_scale, firsts_in[index_at], seconds_in[index_at]
        )
        axis_at = axes_at[index_at]
        steps[index_at] = group_step(
            split_bits(update, axis_at, shift_group), axis_at, shift_group, 0
        )
    for index_at in (1, 0, 2):
        summed[index_at] = crossed(index_at)
    new_weights, new_momenta = ([], [])
    for index_at in range(4):
        outer_grad = LEARN_RATE * (summed[index_at] / GROUPS + WEIGHT_DECAY * weights_in[index_at])
        momentum_new = OUTER_MOMENTUM * momenta_in[index_at] + outer_grad
        new_weights.append(
            weights_in[index_at] - OUTER_RATE * (outer_grad + OUTER_MOMENTUM * momentum_new)
        )
        new_momenta.append(momentum_new)
    clipped_bias = bias_groups * clip_scale[:, None]
    bias_updates, bias_first, bias_second = adam_update(
        clipped_bias, first_bias.reshape(GROUPS, -1), second_bias.reshape(GROUPS, -1)
    )
    outer_bias = LEARN_RATE * (jnp.mean(bias_updates, 0) + WEIGHT_DECAY * bias_flat)
    bias_momentum = OUTER_MOMENTUM * momentum_bias.reshape(-1) + outer_bias
    bias_new = bias_flat - OUTER_RATE * (outer_bias + OUTER_MOMENTUM * bias_momentum)
    return (
        totals[GROUPS] / GROUPS,
        group_norms,
        clipped_bias.reshape(first_bias.shape),
        new_weights[0],
        new_weights[1],
        new_weights[2],
        new_weights[3],
        bias_new.reshape(biases.shape),
        new_momenta[0],
        new_momenta[1],
        new_momenta[2],
        new_momenta[3],
        bias_momentum.reshape(biases.shape),
        new_firsts[0],
        new_seconds[0],
        new_firsts[1],
        new_seconds[1],
        new_firsts[2],
        new_seconds[2],
        new_firsts[3],
        new_seconds[3],
        bias_first.reshape(first_bias.shape),
        bias_second.reshape(second_bias.shape),
    )


def solution(mesh):
    placed = (
        P("dp", None, None),
        P("dp", None, None),
        P("dp"),
        P("dp"),
        P(None, None, "dp", "tensor"),
        P(None, None, "dp", "tensor"),
        P(None, "dp", "tensor"),
        P(None, "dp"),
        P(),
        P(None, None, "dp", "tensor"),
        P(None, None, "dp", "tensor"),
        P(None, "dp", "tensor"),
        P(None, "dp"),
        P(),
        P(None, None, "dp", "tensor"),
        P(None, None, "dp", "tensor"),
        P(None, None, "dp", "tensor"),
        P(None, None, "dp", "tensor"),
        P(None, "dp", "tensor"),
        P(None, "dp", "tensor"),
        P(None, "dp"),
        P(None, "dp"),
        P(),
        P(),
    )
    return jax.shard_map(
        per_device,
        mesh=mesh,
        in_specs=placed,
        out_specs=(
            P(),
            P(),
            P(),
            P(None, None, "dp", "tensor"),
            P(None, None, "dp", "tensor"),
            P(None, "dp", "tensor"),
            P(None, "dp"),
            P(),
            P(None, None, "dp", "tensor"),
            P(None, None, "dp", "tensor"),
            P(None, "dp", "tensor"),
            P(None, "dp"),
            P(),
            P(None, None, "dp", "tensor"),
            P(None, None, "dp", "tensor"),
            P(None, None, "dp", "tensor"),
            P(None, None, "dp", "tensor"),
            P(None, "dp", "tensor"),
            P(None, "dp", "tensor"),
            P(None, "dp"),
            P(None, "dp"),
            P(),
            P(),
        ),
        check_vma=False,
    )
```

```python
import jax
import jax.numpy as jnp
from jax import lax
from jax.experimental import pallas as pl
from jax.sharding import PartitionSpec as P

D = 768
HD = 64
FF = 3072
NCLS = 1000
FREQ = 256
PATCH_IN = 16
SIDE = 16
L = 2
GROUPS = 4
STEP_COUNT = 10
NSTEPS = 1000
S = 256
LB = 14


LOW_TYPE = jnp.bfloat16
LEARN_RATE = 0.03
WEIGHT_DECAY = 0.1
BETA_FIRST = 0.9
BETA_SECOND = 0.95
ADAM_EPSILON = 1e-08
CLIP_NORM = 0.02
OUTER_RATE = 0.7
OUTER_MOMENTUM = 0.9


def shortened(shard):
    return jax.tree.map(lambda a: a.astype(jnp.bfloat16) if a.dtype == jnp.float32 else a, shard)


def swapped(value, axis, bit):
    mask = 2**bit
    pairs = [(source, source ^ mask) for source in range(lax.axis_size(axis))]
    return lax.ppermute(value, axis, pairs)


def product(left, right):
    return jnp.dot(left, right, preferred_element_type=jnp.float32)


def product_t(left, right):
    return lax.dot_general(
        left, right, (((left.ndim - 1,), (1,)), ((), ())), preferred_element_type=jnp.float32
    )


def weight_grad(inputs, grads_out):
    leading = tuple(range(inputs.ndim - 1))
    return lax.dot_general(
        inputs, grads_out, ((leading, leading), ((), ())), preferred_element_type=jnp.float32
    )


def normalize(values):
    centred = values - jnp.mean(values, -1, keepdims=True)
    inverse = lax.rsqrt(jnp.mean(centred * centred, -1, keepdims=True) + 1e-06)
    return (centred * inverse, inverse)


def normalize_back(grad_in, normed, inverse):
    return inverse * (
        grad_in
        - jnp.mean(grad_in, -1, keepdims=True)
        - normed * jnp.mean(grad_in * normed, -1, keepdims=True)
    )


def gelu_tanh(values):
    return jax.nn.gelu(values, approximate=True)


def positions():
    quarter = D // 4
    omegas = 1.0 / 10000.0 ** (jnp.arange(quarter, dtype=jnp.float32) / quarter)
    places = jnp.arange(S, dtype=jnp.int32)
    across = (places % SIDE).astype(jnp.float32)[:, None] * omegas[None, :]
    downward = (places // SIDE).astype(jnp.float32)[:, None] * omegas[None, :]
    return jnp.concatenate(
        [jnp.sin(across), jnp.cos(across), jnp.sin(downward), jnp.cos(downward)], axis=1
    )


def frequencies(stamps):
    half_width = FREQ // 2
    freq_rates = jnp.exp(-jnp.log(10000.0) * jnp.arange(half_width, dtype=jnp.float32) / half_width)
    angles = stamps.astype(jnp.float32)[:, None] * freq_rates[None, :]
    return jnp.concatenate([jnp.cos(angles), jnp.sin(angles)], axis=1)


def signal_levels(stamps):
    noise_rates = jnp.linspace(0.0001, 0.02, NSTEPS, dtype=jnp.float32)
    kept_share = jnp.cumprod(1.0 - noise_rates)
    matches = stamps[:, None] == jnp.arange(NSTEPS, dtype=jnp.int32)[None, :]
    return jnp.sum(jnp.where(matches, kept_share[None, :], 0.0), axis=1)


def embed_parts(matrix):
    bounds = [
        NCLS,
        NCLS + FREQ,
        NCLS + FREQ + D,
        NCLS + FREQ + D + PATCH_IN,
        NCLS + FREQ + 3 * D + PATCH_IN,
    ]
    return (
        matrix[: bounds[0]],
        matrix[bounds[0] : bounds[1]],
        matrix[bounds[1] : bounds[2]],
        matrix[bounds[2] : bounds[3]],
        matrix[bounds[3] : bounds[4]],
        matrix[bounds[4] :],
    )


def split_heads(array_in):
    return array_in.reshape(array_in.shape[:2] + (array_in.shape[2] // HD, HD))


def head_scores(queries, key_rows):
    return jnp.einsum(
        "nqhd,nkhd->nhqk",
        split_heads(queries),
        split_heads(key_rows),
        preferred_element_type=jnp.float32,
    ) * HD ** (-0.5)


def attend(queries, key_rows, values):
    scores = head_scores(queries, key_rows)
    highest = jnp.max(scores, -1, keepdims=True)
    log_total = highest + jnp.log(jnp.sum(jnp.exp(scores - highest), -1, keepdims=True))
    weights = jnp.exp(scores - log_total).astype(LOW_TYPE)
    output = jnp.einsum(
        "nhqk,nkhd->nqhd", weights, split_heads(values), preferred_element_type=jnp.float32
    )
    return (output.reshape(queries.shape), log_total)


def attend_back(queries, key_rows, values, log_total, grad_out):
    weights = jnp.exp(head_scores(queries, key_rows) - log_total)
    grad_heads = split_heads(grad_out)
    grad_values = jnp.einsum(
        "nhqk,nqhd->nkhd", weights.astype(LOW_TYPE), grad_heads, preferred_element_type=jnp.float32
    )
    grad_weights = jnp.einsum(
        "nqhd,nkhd->nhqk", grad_heads, split_heads(values), preferred_element_type=jnp.float32
    )
    grad_scores = (
        weights * (grad_weights - jnp.sum(weights * grad_weights, -1, keepdims=True))
    ).astype(LOW_TYPE)
    grad_queries = jnp.einsum(
        "nhqk,nkhd->nqhd", grad_scores, split_heads(key_rows), preferred_element_type=jnp.float32
    ) * HD ** (-0.5)
    grad_keys = jnp.einsum(
        "nhqk,nqhd->nkhd", grad_scores, split_heads(queries), preferred_element_type=jnp.float32
    ) * HD ** (-0.5)
    return (
        grad_queries.reshape(queries.shape).astype(LOW_TYPE),
        grad_keys.reshape(queries.shape).astype(LOW_TYPE),
        grad_values.reshape(queries.shape).astype(LOW_TYPE),
    )


def place(vector_all, piece_in, offset):
    return lax.dynamic_update_slice_in_dim(vector_all, piece_in, offset, 0)


def flipped(value, masks):
    shards = lax.axis_size("tensor")
    count = lax.axis_size("dp") * shards
    pairs = [(source, source ^ masks[source // shards & 1]) for source in range(count)]
    return lax.ppermute(value, ("dp", "tensor"), pairs)


def picked_at(value, index_at, axis):
    return lax.dynamic_index_in_dim(value, index_at, axis, keepdims=False)


def layer_forward(stream, mod_parts, attn_now, mlp_now, bias_layer):
    width_all = stream.shape[-1]
    normed_one, inverse_one = normalize(stream)
    hidden_one = (normed_one * (1.0 + mod_parts[1]) + mod_parts[0]).astype(LOW_TYPE)
    queries = (product(hidden_one, attn_now[0]) + bias_layer[:width_all]).astype(LOW_TYPE)
    key_rows = product(hidden_one, attn_now[1]).astype(LOW_TYPE)
    values = (product(hidden_one, attn_now[2]) + bias_layer[width_all : 2 * width_all]).astype(
        LOW_TYPE
    )
    attended, log_total = attend(queries, key_rows, values)
    attended = attended.astype(LOW_TYPE)
    branch_one = product_t(attended, attn_now[3]) + bias_layer[2 * width_all : 3 * width_all]
    middle = stream + mod_parts[2] * branch_one
    normed_two, inverse_two = normalize(middle)
    hidden_two = (normed_two * (1.0 + mod_parts[4]) + mod_parts[3]).astype(LOW_TYPE)
    unit_width = mlp_now[0][0].shape[-1]
    before = [
        product(hidden_two, mlp_now[0][unit_at])
        + bias_layer[3 * width_all + unit_at * unit_width : 3 * width_all + (unit_at + 1) * unit_width]
        for unit_at in range(len(mlp_now[0]))
    ]
    activated = [gelu_tanh(part).astype(LOW_TYPE) for part in before]
    branch_two = bias_layer[3 * width_all + FF : 4 * width_all + FF] + sum(
        product_t(part, mlp_now[1][unit_at]) for unit_at, part in enumerate(activated)
    )
    result = middle + mod_parts[5] * branch_two
    kept_state = (
        normed_one,
        inverse_one,
        hidden_one,
        queries,
        key_rows,
        values,
        log_total,
        attended,
        branch_one,
        normed_two,
        inverse_two,
        hidden_two,
        before,
        activated,
        branch_two,
    )
    return (result, kept_state)


def exchanged(value, mask):
    count = lax.axis_size("dp") * lax.axis_size("tensor")
    return lax.ppermute(value, ("dp", "tensor"), [(source, source ^ mask) for source in range(count)])


def half_of(value, axis, bit):
    width = value.shape[axis] // 2
    return lax.dynamic_slice_in_dim(value, bit * width, width, axis)


def summed_low(left, right):
    return (left.astype(jnp.float32) + right.astype(jnp.float32)).astype(LOW_TYPE)


def rows_halved(value):
    stretch = lax.axis_index("dp") // GROUPS
    stretches = lax.axis_size("dp") // GROUPS
    for bit_at in reversed(range(stretches.bit_length() - 1)):
        bit = stretch >> bit_at & 1
        received = exchanged(
            half_of(value, 0, 1 - bit), lax.axis_size("tensor") * GROUPS << bit_at
        )
        value = summed_low(half_of(value, 0, bit), received)
    return value


def columns_halved(sent, kept):
    return summed_low(kept, exchanged(sent, 1))


def unit_halved(first, second):
    picked = (lax.axis_index("tensor") & 1) == 1
    return columns_halved(jnp.where(picked, first, second), jnp.where(picked, second, first))


def pair_halved(first, second):
    bit = lax.axis_index("tensor") & 1

    def halves(bit_now):
        return jnp.concatenate([half_of(first, 1, bit_now), half_of(second, 1, bit_now)], 1)

    return columns_halved(halves(1 - bit), halves(bit))


def core_summed(sent, kept):
    return [
        summed_low(own, exchanged(other, lax.axis_size("tensor"))) for other, own in zip(sent, kept)
    ]


def homeward(values):
    shards = lax.axis_size("tensor")
    pairs = []
    for source in range(lax.axis_size("dp") * shards):
        core, high = (source // shards & 1, source % shards >> 1)
        pairs.append((source, source ^ (core ^ high) * (shards + shards // 2)))
    return [lax.ppermute(value, ("dp", "tensor"), pairs) for value in values]


def squared(values):
    return sum(jnp.sum(jnp.square(value.astype(jnp.float32))) for value in values)


def mlp_second(totals):
    up_zero, up_one, down_zero, down_one = totals
    return [rows_halved(up_zero), rows_halved(up_one), unit_halved(down_zero, down_one)]


def mlp_third(totals):
    up_zero, up_one, down = totals
    return [unit_halved(up_zero, up_one), rows_halved(down)]


def attn_second(totals):
    query_key, value_map, out_map = totals
    return [rows_halved(query_key), pair_halved(value_map, out_map)]


def attn_third(totals):
    query_key, value_out = totals
    width = query_key.shape[1] // 2
    return [pair_halved(query_key[:, :width], query_key[:, width:]), rows_halved(value_out)]


def attn_maps(gathered, layer_at):
    shards, rows_all, width_all = gathered.shape[1:]
    width, rows = (width_all // 4, rows_all // 4)

    def kernel(gathered_ref, maps_ref):
        for kind in range(4):
            maps_ref[kind] = jnp.concatenate(
                [
                    gathered_ref[0, shard][:, kind * width : (kind + 1) * width]
                    for shard in range(shards)
                ],
                axis=1,
            )

    return pl.pallas_call(
        kernel,
        grid=(4,),
        in_specs=[
            pl.BlockSpec((1, shards, rows, width_all), lambda at: (layer_at, 0, at, 0)),
        ],
        out_specs=pl.BlockSpec((4, rows, shards * width), lambda at: (0, at, 0)),
        out_shape=jax.ShapeDtypeStruct((4, rows_all, shards * width), gathered.dtype),
        name="attn_maps",
    )(gathered)


def tied(value, flows):
    return lax.optimization_barrier((value, flows))


def layer_backward(grad_out, mod_parts, attn_now, mlp_now, kept_state, flows):
    (
        normed_one,
        inverse_one,
        hidden_one,
        queries,
        key_rows,
        values,
        log_total,
        attended,
        branch_one,
        normed_two,
        inverse_two,
        hidden_two,
        saved_pre,
        activated,
        branch_two,
    ) = kept_state
    core = lax.axis_index("dp") & 1
    pair = len(activated) // 2
    if flows:
        flows = [mlp_second(flows[0]), flows[1]]
        grad_out, flows = tied(grad_out, flows)
    grad_gate_two = jnp.sum(grad_out * branch_two, 1)
    downward = grad_out * mod_parts[5]
    down_low = downward.astype(LOW_TYPE)
    grad_pre = [
        jax.vjp(gelu_tanh, part)[1](product(down_low, mlp_now[1][unit_at]))[0].astype(LOW_TYPE)
        for unit_at, part in enumerate(saved_pre)
    ]

    def unit_grads(side):
        picked = core == side
        up = [jnp.where(picked, grad_pre[at + pair], grad_pre[at]) for at in range(pair)]
        down = [jnp.where(picked, activated[at + pair], activated[at]) for at in range(pair)]
        return [weight_grad(hidden_two, part).astype(LOW_TYPE) for part in up] + [
            weight_grad(down_low, part).astype(LOW_TYPE) for part in down
        ]

    sent = unit_grads(0)
    if flows:
        flows = [mlp_third(flows[0]), attn_second(flows[1])]
        sent, flows = tied(sent, flows)
    mlp_sums = core_summed(sent, unit_grads(1))
    grad_hidden_two = sum(
        product_t(part, mlp_now[0][unit_at]) for unit_at, part in enumerate(grad_pre)
    )
    grad_middle = grad_out + normalize_back(
        grad_hidden_two * (1.0 + mod_parts[4]), normed_two, inverse_two
    )
    grad_gate_one = jnp.sum(grad_middle * branch_one, 1)
    upward = grad_middle * mod_parts[2]
    up_low, mlp_sums = tied(upward.astype(LOW_TYPE), mlp_sums)
    grad_attended = product(up_low, attn_now[3]).astype(LOW_TYPE)
    grad_queries, grad_keys, grad_values = attend_back(
        queries, key_rows, values, log_total, grad_attended
    )
    if flows:
        flows = [homeward(flows[0]), attn_third(flows[1]), squared(flows[0])]
        grad_queries, flows = tied(grad_queries, flows)

    def map_grads(side):
        both = jnp.concatenate([half_of(grad_queries, 2, side), half_of(grad_keys, 2, side)], 2)
        return [
            weight_grad(hidden_one, both).astype(LOW_TYPE),
            weight_grad(hidden_one, half_of(grad_values, 2, side)).astype(LOW_TYPE),
            weight_grad(up_low, half_of(attended, 2, side)).astype(LOW_TYPE),
        ]

    attn_sums = core_summed(map_grads(1 - core), map_grads(core))
    grad_hidden_one = (
        product_t(grad_queries, attn_now[0])
        + product_t(grad_keys, attn_now[1])
        + product_t(grad_values, attn_now[2])
    )
    grad_stream = grad_middle + normalize_back(
        grad_hidden_one * (1.0 + mod_parts[1]), normed_one, inverse_one
    )
    grad_modulation = jnp.concatenate(
        [
            jnp.sum(grad_hidden_one, 1),
            jnp.sum(grad_hidden_one * normed_one, 1),
            grad_gate_one,
            jnp.sum(grad_hidden_two, 1),
            jnp.sum(grad_hidden_two * normed_two, 1),
            grad_gate_two,
        ],
        axis=1,
    ).astype(LOW_TYPE)
    bias_grad = jnp.concatenate(
        [
            jnp.sum(grad_queries.astype(jnp.float32), (0, 1)),
            jnp.sum(grad_values.astype(jnp.float32), (0, 1)),
            jnp.sum(upward, (0, 1)),
        ]
        + [jnp.sum(part.astype(jnp.float32), (0, 1)) for part in grad_pre]
        + [jnp.sum(downward, (0, 1))]
    )
    return (grad_stream, [mlp_sums, attn_sums], flows, grad_modulation, bias_grad)


def own_latents(value):
    shards = lax.axis_size("tensor")
    low_bit, shard_at = (lax.axis_index("dp") & 1, lax.axis_index("tensor"))
    count = value.shape[0] // shards
    base = (shard_at & 1) * 2
    mine = lax.dynamic_slice_in_dim(value, (base + low_bit) * count, count, 0)
    theirs = lax.dynamic_slice_in_dim(value, (base + 1 - low_bit) * count, count, 0)
    received = flipped(theirs, (shards, shards))
    return jnp.where(shard_at >> 1 == low_bit, mine, received)


def natural_order(gathered, stretches):
    shaped = gathered.reshape((stretches, 2, 2, 2, 2) + gathered.shape[1:])
    moved = jnp.moveaxis(shaped, 2, 4)
    return moved.reshape((-1,) + gathered.shape[2:])


def split_bits(array_in, axis_at, count_bits):
    dims_in = array_in.shape
    return array_in.reshape(
        dims_in[:axis_at]
        + (2,) * count_bits
        + (dims_in[axis_at] >> count_bits,)
        + dims_in[axis_at + 1 :]
    )


def group_step(block, axis_at, count_bits, bit_at):
    own_bit = lax.axis_index("dp") >> bit_at & 1
    at = axis_at + count_bits - 1 - bit_at
    sent = shortened(lax.dynamic_slice_in_dim(block, 1 - own_bit, 1, at))
    return lax.dynamic_slice_in_dim(block, own_bit, 1, at) + swapped(sent, "dp", bit_at)


def adam_update(gradient, first_old, second_old):
    first_new = BETA_FIRST * first_old + (1.0 - BETA_FIRST) * gradient
    second_new = BETA_SECOND * second_old + (1.0 - BETA_SECOND) * gradient * gradient
    update = (
        first_new
        / (1.0 - BETA_FIRST**STEP_COUNT)
        / (jnp.sqrt(second_new / (1.0 - BETA_SECOND**STEP_COUNT)) + ADAM_EPSILON)
    )
    return (update, first_new, second_new)


def per_device(
    patches,
    noise_draw,
    timesteps,
    labels,
    w_attn,
    w_mlp,
    w_mod,
    w_embed,
    biases,
    momentum_attn,
    momentum_mlp,
    momentum_mod,
    momentum_embed,
    momentum_bias,
    first_attn,
    second_attn,
    first_mlp,
    second_mlp,
    first_mod,
    second_mod,
    first_embed,
    second_embed,
    first_bias,
    second_bias,
):
    shards = lax.axis_size("tensor")
    shard_at = lax.axis_index("tensor")
    dp_count = lax.axis_size("dp")
    dp_at = lax.axis_index("dp")
    group_at = dp_at % GROUPS
    stretches = dp_count // GROUPS
    stretch = dp_at // GROUPS
    layer_span = LB * D
    col_width = w_attn.shape[3]
    row_width = w_attn.shape[2]
    mod_width = w_mod.shape[2]
    latents = dp_count * patches.shape[0]
    everyone = ("tensor", "dp")

    stamps, marks = lax.all_gather(jnp.stack([timesteps, labels]), "dp", axis=1, tiled=True)
    embed_low = w_embed.astype(LOW_TYPE)
    conditioners = NCLS + FREQ + D + PATCH_IN
    first_map = embed_low[NCLS : NCLS + FREQ]
    second_map = embed_low[NCLS + FREQ : NCLS + FREQ + D]

    def attn_local(layer_at):
        return jnp.transpose(w_attn[layer_at], (1, 0, 2)).reshape(1, row_width, 4 * col_width)

    first_local = [attn_local(layer_at) for layer_at in range(L)] + list(w_mlp[: L - 1])
    first_local = jnp.concatenate(
        [part.astype(LOW_TYPE).reshape(-1, row_width, 4 * col_width) for part in first_local]
    )
    first_whole = lax.all_gather(first_local, everyone, axis=1, tiled=True)
    last_whole = lax.all_gather(w_mlp[L - 1].astype(LOW_TYPE), everyone, axis=1, tiled=True)
    units_whole = first_whole.reshape(-1, shards, D, 4 * col_width)
    attn_all = [attn_maps(units_whole, layer_at) for layer_at in range(L)]
    mlp_all = [
        [[units_whole[L + 2 * layer_at + kind, at] for at in range(shards)] for kind in range(2)]
        for layer_at in range(L - 1)
    ]
    last_whole = last_whole.reshape(2, shards, D, -1)
    mlp_all.append([[last_whole[kind, at] for at in range(shards)] for kind in range(2)])

    bias_flat = biases.reshape(-1)
    bias_tail = bias_flat[L * layer_span :]
    freq_low = frequencies(stamps).astype(LOW_TYPE)

    def own_columns(vector):
        return lax.dynamic_slice_in_dim(vector, dp_at * row_width, row_width, 0)

    hidden_cols = product(freq_low, first_map) + own_columns(bias_tail[D : 2 * D])
    gathered_cols = lax.all_gather(
        jnp.concatenate(
            [
                hidden_cols,
                w_embed[conditioners - PATCH_IN : conditioners],
                w_embed[-PATCH_IN:],
            ]
        ),
        "dp",
        axis=1,
        tiled=True,
    )
    hidden_time = gathered_cols[:latents]
    patch_map = gathered_cols[latents : latents + PATCH_IN].astype(LOW_TYPE)
    head_map = gathered_cols[latents + PATCH_IN :].astype(LOW_TYPE)
    smooth_time = jax.nn.silu(hidden_time).astype(LOW_TYPE)
    class_picks = (marks[:, None] == jnp.arange(NCLS, dtype=jnp.int32)[None, :]).astype(LOW_TYPE)
    condition_rows = (
        product(smooth_time, second_map)
        + own_columns(bias_tail[2 * D : 3 * D])
        + product(class_picks, embed_low[:NCLS])
    )
    cond_rows = jax.nn.silu(condition_rows).astype(LOW_TYPE)
    mod_low = w_mod.astype(LOW_TYPE)
    final_low = embed_low[conditioners:-PATCH_IN]
    final_width = final_low.shape[0] // shards
    mod_cols = jnp.concatenate(
        [product(cond_rows, mod_low[layer_at]) for layer_at in range(L)]
        + [
            product_t(
                cond_rows, lax.dynamic_slice_in_dim(final_low, shard_at * final_width, final_width, 0)
            )
        ],
        axis=1,
    )
    mod_cols = lax.psum_scatter(mod_cols, "dp", scatter_dimension=0, tiled=True)
    mod_all = own_latents(
        jnp.swapaxes(lax.all_gather(mod_cols.astype(LOW_TYPE), "tensor"), 0, 1)
    ).astype(jnp.float32)
    mod_parts = []
    for layer_at in range(L):
        modulation = (
            mod_all[:, :, layer_at * mod_width : (layer_at + 1) * mod_width].reshape(-1, 6 * D)
            + bias_flat[layer_at * layer_span + 4 * D + FF : (layer_at + 1) * layer_span]
        )
        mod_parts.append(
            [modulation[:, None, part_at * D : (part_at + 1) * D] for part_at in range(6)]
        )
    final_mod = mod_all[:, :, L * mod_width :].reshape(-1, 2 * D) + bias_tail[3 * D : 5 * D]

    patches_own, noise_own = (own_latents(patches), own_latents(noise_draw))
    signal = own_latents(signal_levels(timesteps)[:, None])[:, :, None]
    noised = (jnp.sqrt(signal) * patches_own + jnp.sqrt(1.0 - signal) * noise_own).astype(LOW_TYPE)
    stream = product(noised, patch_map) + bias_tail[:D] + positions()
    saved_states = []
    for layer_at in range(L):
        stream, kept_state = layer_forward(
            stream,
            mod_parts[layer_at],
            attn_all[layer_at],
            mlp_all[layer_at],
            bias_flat[layer_at * layer_span : (layer_at + 1) * layer_span],
        )
        saved_states.append(kept_state)
    normed_last, inverse_last = normalize(stream)
    hidden_last = (normed_last * (1.0 + final_mod[:, None, D:]) + final_mod[:, None, :D]).astype(
        LOW_TYPE
    )
    predicted = product_t(hidden_last, head_map)
    errors = predicted - noise_own
    elements = dp_count // GROUPS * patches.shape[0] * S * PATCH_IN
    loss_here = jnp.sum(errors * errors) / elements
    grad_pred = (2.0 * errors / elements).astype(LOW_TYPE)
    grad_head = weight_grad(grad_pred, hidden_last)
    grad_hidden = product(grad_pred, head_map)
    grad_final = jnp.concatenate(
        [jnp.sum(grad_hidden, 1), jnp.sum(grad_hidden * normed_last, 1)], axis=1
    ).astype(LOW_TYPE)
    grad_stream = normalize_back(
        grad_hidden * (1.0 + final_mod[:, None, D:]), normed_last, inverse_last
    )
    mod_list, bias_list, sums_list, flows = ([None] * L, [None] * L, [None] * L, None)
    moved_squares = 0.0
    late, grad_stream = tied(jnp.concatenate([second_map, cond_rows]), grad_stream)
    late = lax.all_gather(late, "dp", axis=1, tiled=True)
    second_time, cond_act = (late[:D], late[D:])
    for layer_at in range(L - 1, -1, -1):
        grad_stream, fresh, flows, mod_list[layer_at], bias_list[layer_at] = layer_backward(
            grad_stream,
            mod_parts[layer_at],
            attn_all[layer_at],
            mlp_all[layer_at],
            saved_states[layer_at],
            flows,
        )
        if flows:
            sums_list[layer_at + 1] = [flows[0], homeward(flows[1])]
            moved_squares = moved_squares + flows[2] + squared(flows[1])
        flows = fresh
    last_mlp = mlp_third(mlp_second(flows[0]))
    last_attn = attn_third(attn_second(flows[1]))
    moved_squares = moved_squares + squared(last_mlp) + squared(last_attn)
    last_mlp = homeward(last_mlp)
    grad_patch = weight_grad(noised, grad_stream.astype(LOW_TYPE))
    mine = patches_own.shape[0]
    early = jnp.concatenate(
        [grad_now.reshape(-1) for grad_now in mod_list[1:]]
        + [grad_final.reshape(-1)]
        + [grad_now.astype(LOW_TYPE) for grad_now in bias_list[1:]]
        + [grad_head.astype(LOW_TYPE).reshape(-1)]
    )
    late_part = jnp.concatenate(
        [
            mod_list[0].reshape(-1),
            bias_list[0].astype(LOW_TYPE),
            jnp.sum(grad_stream, (0, 1)).astype(LOW_TYPE),
            grad_patch.astype(LOW_TYPE).reshape(-1),
        ]
    )
    devices = dp_count * shards

    def cutter(vectors):
        gathered = lax.all_gather(vectors, ("dp", "tensor"))
        offset = 0

        def taken(width):
            nonlocal offset
            offset += width
            return gathered[:, offset - width : offset]

        return taken

    take_early, take_late = (cutter(early), cutter(late_part))
    takers = [take_late] + [take_early] * (L - 1)
    grad_mods = [
        natural_order(taker(mine * 6 * D).reshape(devices, mine, 6 * D), stretches)
        for taker in takers
    ]
    grad_finals = natural_order(take_early(mine * 2 * D).reshape(devices, mine, 2 * D), stretches)

    def group_sums(part):
        shaped = part.astype(jnp.float32).reshape(stretches, 2, 2, 2, shards // 2, -1)
        return jnp.sum(shaped, (0, 2, 4)).reshape(GROUPS, -1)

    layer_bias = 7 * D + FF - 3 * D
    bias_sums = [group_sums(taker(layer_bias)) for taker in takers]
    patch_bias = group_sums(take_late(D))
    patch_sums = group_sums(take_late(PATCH_IN * D)).reshape(GROUPS, PATCH_IN, D)
    head_sums = group_sums(take_early(PATCH_IN * D)).reshape(GROUPS, PATCH_IN, D)

    own_mods = [
        lax.dynamic_slice_in_dim(grad_now, shard_at * mod_width, mod_width, 1)
        for grad_now in grad_mods
    ]
    grad_cond_parts = sum(
        product_t(own_mods[layer_at], mod_low[layer_at]) for layer_at in range(L)
    )
    grad_cond_act = jnp.sum(
        lax.all_gather(grad_cond_parts.astype(LOW_TYPE), "tensor").astype(jnp.float32), 0
    ) + product(grad_finals, final_low)
    grad_condition = lax.all_gather(
        jax.vjp(jax.nn.silu, condition_rows)[1](grad_cond_act)[0].astype(LOW_TYPE),
        "dp",
        axis=1,
        tiled=True,
    )
    grad_smooth = product_t(grad_condition, second_time)
    grad_hidden_time = jax.vjp(jax.nn.silu, hidden_time)[1](grad_smooth)[0].astype(LOW_TYPE)

    def of_group(value):
        shaped = value.reshape((stretches, GROUPS, latents // dp_count) + value.shape[1:])
        return picked_at(shaped, group_at, 1).reshape((-1,) + value.shape[1:])

    def of_stretch(value):
        width = value.shape[-1] // stretches
        return lax.dynamic_slice_in_dim(value, stretch * width, width, value.ndim - 1)

    def latent_sums(value):
        shaped = value.astype(jnp.float32).reshape(stretches, GROUPS, latents // dp_count, -1)
        return jnp.sum(shaped, (0, 2))

    grad_condition_own = of_stretch(of_group(grad_condition))
    cond_own = of_stretch(of_group(cond_act))
    grad_embed = jnp.concatenate(
        [
            weight_grad(of_group(class_picks), grad_condition_own),
            weight_grad(of_group(freq_low), of_stretch(of_group(grad_hidden_time))),
            weight_grad(of_group(smooth_time), grad_condition_own),
            of_stretch(picked_at(patch_sums, group_at, 0)),
            weight_grad(of_group(grad_finals), cond_own),
            of_stretch(picked_at(head_sums, group_at, 0)),
        ],
        0,
    )
    grad_mod_map = jnp.stack([weight_grad(cond_own, of_group(grad_now)) for grad_now in own_mods])
    bias_groups = jnp.concatenate(
        [
            part
            for layer_at in range(L)
            for part in (bias_sums[layer_at], latent_sums(grad_mods[layer_at]))
        ]
        + [
            patch_bias,
            latent_sums(grad_hidden_time),
            latent_sums(grad_condition),
            latent_sums(grad_finals),
        ],
        axis=1,
    )
    side_squares = jnp.sum(grad_mod_map * grad_mod_map) + jnp.sum(grad_embed * grad_embed) / shards
    bias_squares = jnp.sum(bias_groups * bias_groups, 1)
    last_attn, (side_squares, bias_squares) = tied(last_attn, (side_squares, bias_squares))
    sums_list[0] = [last_mlp, homeward(last_attn)]
    attn_now = jnp.stack(
        [
            jnp.stack(
                [part[:, at * col_width : (at + 1) * col_width] for part in sums[1] for at in (0, 1)]
            )
            for sums in sums_list
        ]
    ).astype(jnp.float32)
    mlp_now = jnp.stack([jnp.stack(sums[0]) for sums in sums_list]).astype(jnp.float32)
    reduced = [attn_now, mlp_now, grad_mod_map, grad_embed]
    groups_here = jnp.arange(GROUPS, dtype=jnp.int32)
    picked = (groups_here == group_at).astype(jnp.float32)
    moved_group = (dp_at - (dp_at & 1) + (shard_at >> 1)) % GROUPS
    moved_picked = (groups_here == moved_group).astype(jnp.float32)
    totals = jnp.concatenate(
        [
            picked * side_squares + moved_picked * moved_squares,
            jnp.full((GROUPS,), loss_here),
            jnp.zeros((128 - 2 * GROUPS,)),
        ]
    )
    for axis in ("tensor", "dp"):
        rows_now = lax.all_gather(jnp.broadcast_to(totals, (8, 128)), axis, axis=0, tiled=True)
        totals = jnp.sum(rows_now.reshape(-1, 8, 128)[:, 0], 0)
    group_norms = jnp.sqrt(totals[:GROUPS] + bias_squares)
    clip_scale = CLIP_NORM / (group_norms + 1e-06)
    own_scale = jnp.sum(picked * clip_scale)
    shift_group = GROUPS.bit_length() - 1
    weights_in = (w_attn, w_mlp, w_mod, w_embed)
    momenta_in = (momentum_attn, momentum_mlp, momentum_mod, momentum_embed)
    firsts_in = (first_attn, first_mlp, first_mod, first_embed)
    seconds_in = (second_attn, second_mlp, second_mod, second_embed)
    axes_at = (2, 2, 1, 1)
    steps, summed, new_firsts, new_seconds = ([None] * 4, [None] * 4, [None] * 4, [None] * 4)

    def crossed(index_at):
        block = steps[index_at]
        for bit_at in range(1, shift_group):
            block = group_step(block, axes_at[index_at], shift_group, bit_at)
        return block.reshape(weights_in[index_at].shape)

    for index_at in (3, 1, 0, 2):
        grad_now = reduced[index_at]
        if index_at == 0:
            grad_now, steps[3] = tied(grad_now, steps[3])
        if index_at == 2:
            summed[3] = crossed(3)
            grad_now, (summed[3], steps[1]) = tied(grad_now, (summed[3], steps[1]))
        update, new_firsts[index_at], new_seconds[index_at] = adam_update(
            grad_now * own_scale, firsts_in[index_at], seconds_in[index_at]
        )
        axis_at = axes_at[index_at]
        steps[index_at] = group_step(
            split_bits(update, axis_at, shift_group), axis_at, shift_group, 0
        )
    for index_at in (1, 0, 2):
        summed[index_at] = crossed(index_at)
    new_weights, new_momenta = ([], [])
    for index_at in range(4):
        outer_grad = LEARN_RATE * (summed[index_at] / GROUPS + WEIGHT_DECAY * weights_in[index_at])
        momentum_new = OUTER_MOMENTUM * momenta_in[index_at] + outer_grad
        new_weights.append(
            weights_in[index_at] - OUTER_RATE * (outer_grad + OUTER_MOMENTUM * momentum_new)
        )
        new_momenta.append(momentum_new)
    clipped_bias = bias_groups * clip_scale[:, None]
    bias_updates, bias_first, bias_second = adam_update(
        clipped_bias, first_bias.reshape(GROUPS, -1), second_bias.reshape(GROUPS, -1)
    )
    outer_bias = LEARN_RATE * (jnp.mean(bias_updates, 0) + WEIGHT_DECAY * bias_flat)
    bias_momentum = OUTER_MOMENTUM * momentum_bias.reshape(-1) + outer_bias
    bias_new = bias_flat - OUTER_RATE * (outer_bias + OUTER_MOMENTUM * bias_momentum)
    return (
        totals[GROUPS] / GROUPS,
        group_norms,
        clipped_bias.reshape(first_bias.shape),
        new_weights[0],
        new_weights[1],
        new_weights[2],
        new_weights[3],
        bias_new.reshape(biases.shape),
        new_momenta[0],
        new_momenta[1],
        new_momenta[2],
        new_momenta[3],
        bias_momentum.reshape(biases.shape),
        new_firsts[0],
        new_seconds[0],
        new_firsts[1],
        new_seconds[1],
        new_firsts[2],
        new_seconds[2],
        new_firsts[3],
        new_seconds[3],
        bias_first.reshape(first_bias.shape),
        bias_second.reshape(second_bias.shape),
    )


def solution(mesh):
    placed = (
        P("dp", None, None),
        P("dp", None, None),
        P("dp"),
        P("dp"),
        P(None, None, "dp", "tensor"),
        P(None, None, "dp", "tensor"),
        P(None, "dp", "tensor"),
        P(None, "dp"),
        P(),
        P(None, None, "dp", "tensor"),
        P(None, None, "dp", "tensor"),
        P(None, "dp", "tensor"),
        P(None, "dp"),
        P(),
        P(None, None, "dp", "tensor"),
        P(None, None, "dp", "tensor"),
        P(None, None, "dp", "tensor"),
        P(None, None, "dp", "tensor"),
        P(None, "dp", "tensor"),
        P(None, "dp", "tensor"),
        P(None, "dp"),
        P(None, "dp"),
        P(),
        P(),
    )
    return jax.shard_map(
        per_device,
        mesh=mesh,
        in_specs=placed,
        out_specs=(
            P(),
            P(),
            P(),
            P(None, None, "dp", "tensor"),
            P(None, None, "dp", "tensor"),
            P(None, "dp", "tensor"),
            P(None, "dp"),
            P(),
            P(None, None, "dp", "tensor"),
            P(None, None, "dp", "tensor"),
            P(None, "dp", "tensor"),
            P(None, "dp"),
            P(),
            P(None, None, "dp", "tensor"),
            P(None, None, "dp", "tensor"),
            P(None, None, "dp", "tensor"),
            P(None, None, "dp", "tensor"),
            P(None, "dp", "tensor"),
            P(None, "dp", "tensor"),
            P(None, "dp"),
            P(None, "dp"),
            P(),
            P(),
        ),
        check_vma=False,
    )
```
